32 devices in a mesh: ens: 2 (over y), grid: 16 (over z, x, core).
Axes of the slice: x: 2, y: 2, z: 4, core: 2. Of those that a mesh axis runs over, the one named last changes fastest.
Arguments:
- fields: bfloat16 [2, 384, 768, 256], P('ens', 'grid'), may hold values from -6 to 6
- mode_counts: int32 [384], P('grid'), may hold values from 96 to 384, as said below
- gain_attn: float32 [256], replicated, may hold values from 0.5 to 1.5
- w_query: bfloat16 [256, 256], replicated, may hold values from -1 to 1
- w_key: bfloat16 [256, 256], replicated, may hold values from -8 to 8
- w_value: bfloat16 [256, 256], replicated, may hold values from -0.375 to 0.375
- w_out: bfloat16 [256, 256], replicated, may hold values from -0.375 to 0.375
- gain_spec: float32 [256], replicated, may hold values from 0.5 to 1.5
- w_first: bfloat16 [2, 8, 32, 32], replicated, may hold values from -1 to 1
- w_second: bfloat16 [2, 8, 32, 32], replicated, may hold values from -1 to 1
Outputs:
- layer_out: bfloat16 [2, 384, 768, 256], P('ens', 'grid')
The draws below stay inside these ranges and needn't reach their ends.
Inputs may be any that keep to these rules, and one draw needn't show every extreme that they name: `mode_counts`: longitude wavenumbers kept in each latitude row; some row keeps all 384.
All inputs are finite; a program needn't handle non-finite values.
Results may differ from the reference program's by a relative error of at most 0.012.
Values may be sent and summed in bfloat16 or wider, within the bound.
A program may use at most 256 MiB of HBM per device.

```python
import math
import jax
import jax.numpy as jnp
from jax import lax

D = 256
HEAD = 32
HEADS = 8
BLOCK = 32
NBLK = 8
NLAT = 384
NLON = 768
KLON = 384
KLAT = 128
MEMBERS = 2


def draw_pair(key):
    shared_part = jax.random.normal(jax.random.fold_in(key, 11), (D, D), jnp.float32) / math.sqrt(D)
    own_part = jax.random.normal(jax.random.fold_in(key, 12), (D, D), jnp.float32) / math.sqrt(D)
    return (shared_part, own_part)


def draw_w_query(key, part):
    shared_part, own_part = draw_pair(key)
    return jnp.clip(shared_part, -1.0, 1.0).astype(jnp.bfloat16)


def draw_w_key(key, part):
    shared_part, own_part = draw_pair(key)
    return jnp.clip(own_part, -8.0, 8.0).astype(jnp.bfloat16)


def draw_mode_counts(key, part):
    counts = jax.random.randint(jax.random.fold_in(key, 21), (NLAT,), KLON // 4, KLON + 1)
    chosen = jax.random.randint(jax.random.fold_in(key, 22), (), 0, NLAT)
    return jnp.where(jnp.arange(NLAT, dtype=jnp.int32) == chosen, KLON, counts).astype(jnp.int32)


def block_scale(rng, shape, cuts, smallest, largest):
    gain, own = 1.0, jax.random.fold_in(rng, 6)
    for axis_at, parts in cuts:
        draws = jnp.exp(jax.random.uniform(jax.random.fold_in(own, axis_at), (parts,), jnp.float32, smallest / len(cuts), largest / len(cuts)))
        gain = gain * jnp.repeat(draws, shape[axis_at] // parts).reshape([-1 if axis == axis_at else 1 for axis in range(len(shape))])
    return gain


def noise(stream_key, extent, width, most, cuts=(), held_as=jnp.bfloat16):
    gain = block_scale(stream_key, extent, cuts, -0.22, 0.18) if cuts else 1.0
    result = jax.random.normal(stream_key, extent, jnp.float32) * width * gain
    return jnp.minimum(jnp.maximum(result, -most), most).astype(held_as)


def setup_inputs(seed: int = 0) -> dict:
    arg_keys = jax.random.split(jax.random.key(seed), 11)
    return {
        "fields": noise(arg_keys[0], (MEMBERS, NLAT, NLON, D), 1.0, 6.0, ((0, 2), (1, 16))),
        "mode_counts": draw_mode_counts(jax.random.fold_in(arg_keys[10], 71), 0),
        "gain_attn": jnp.clip(1.0 + 0.1 * jax.random.normal(arg_keys[2], (D,), jnp.float32), 0.5, 1.5),
        "w_query": draw_w_query(jax.random.fold_in(arg_keys[10], 71), 0),
        "w_key": draw_w_key(jax.random.fold_in(arg_keys[10], 71), 0),
        "w_value": noise(arg_keys[5], (D, D), D ** -0.5, 0.375),
        "w_out": noise(arg_keys[6], (D, D), D ** -0.5, 0.375),
        "gain_spec": jnp.clip(1.0 + 0.1 * jax.random.normal(arg_keys[7], (D,), jnp.float32), 0.5, 1.5),
        "w_first": noise(arg_keys[8], (2, NBLK, BLOCK, BLOCK), BLOCK ** -0.5, 1.0),
        "w_second": noise(arg_keys[9], (2, NBLK, BLOCK, BLOCK), BLOCK ** -0.5, 1.0),
    }


norm_eps = 1e-05

def layer_norm(inputs, gain_vec):
    widened = inputs.astype(jnp.float32)
    center = widened - lax.optimization_barrier(jnp.mean(widened, axis=-1, keepdims=True))
    spread = lax.optimization_barrier(jnp.mean(center * center, axis=-1, keepdims=True))
    return center * lax.rsqrt(spread + norm_eps) * gain_vec

def lon_table(points, mode_count):
    positions = jnp.arange(points, dtype=jnp.int32)
    frequency = jnp.arange(mode_count, dtype=jnp.int32)
    turn_count = positions[:, None] * frequency[None, :] % points
    angles = 2.0 * math.pi / points * turn_count.astype(jnp.float32)
    factor = 1.0 / math.sqrt(points)
    return jnp.concatenate([jnp.cos(angles) * factor, -jnp.sin(angles) * factor], axis=1).astype(jnp.bfloat16)

def lon_inverse(points, mode_count):
    positions = jnp.arange(points, dtype=jnp.int32)
    frequency = jnp.arange(mode_count, dtype=jnp.int32)
    turn_count = frequency[:, None] * positions[None, :] % points
    angles = 2.0 * math.pi / points * turn_count.astype(jnp.float32)
    weight = jnp.where(frequency == 0, 1.0, 2.0).astype(jnp.float32)[:, None] / math.sqrt(points)
    return jnp.stack([jnp.cos(angles) * weight, -jnp.sin(angles) * weight]).astype(jnp.bfloat16)

def lat_angles(row_count, mode_count):
    frequency = jnp.arange(mode_count, dtype=jnp.int32)
    frequency = jnp.where(frequency < mode_count // 2, frequency, frequency - mode_count)
    positions = jnp.arange(row_count, dtype=jnp.int32)
    turn_count = frequency[:, None] * positions[None, :] % row_count
    return 2.0 * math.pi / row_count * turn_count.astype(jnp.float32)

def lat_forward(row_count, mode_count):
    angles = lat_angles(row_count, mode_count)
    factor = 1.0 / math.sqrt(row_count)
    cosine = jnp.cos(angles) * factor
    sine_part = jnp.sin(angles) * factor
    return jnp.stack([jnp.stack([cosine, sine_part], axis=1), jnp.stack([-sine_part, cosine], axis=1)]).astype(jnp.bfloat16)

def lat_inverse(row_count, mode_count):
    angles = jnp.transpose(lat_angles(row_count, mode_count))
    factor = 1.0 / math.sqrt(row_count)
    cosine = jnp.cos(angles) * factor
    sine_part = jnp.sin(angles) * factor
    return jnp.stack([jnp.stack([cosine, -sine_part]), jnp.stack([sine_part, cosine])]).astype(jnp.bfloat16)

def complex_blocks(weight):
    real_part = weight[0]
    imag_part = weight[1]
    return jnp.stack([jnp.stack([real_part, imag_part]), jnp.stack([-imag_part, real_part])])

def mix_blocks(spec, big):
    blocks = spec.reshape(spec.shape[:3] + (big.shape[2], big.shape[3]))
    out_blocks = jnp.einsum('pqkbi,psbio->sqkbo', blocks.astype(jnp.float32), big.astype(jnp.float32))
    return out_blocks.reshape(spec.shape)

def reference(fields, mode_counts, gain_attn, w_query, w_key, w_value, w_out, gain_spec, w_first, w_second):
    score_scale = 1.0 / math.sqrt(HEAD)

    def attend(lat_row):
        normed = layer_norm(lat_row, gain_attn).astype(jnp.bfloat16)
        queries = jnp.dot(normed, w_query, preferred_element_type=jnp.float32).astype(jnp.bfloat16)
        key_rows = jnp.dot(normed, w_key, preferred_element_type=jnp.float32).astype(jnp.bfloat16)
        value_rows = jnp.dot(normed, w_value, preferred_element_type=jnp.float32).astype(jnp.bfloat16)
        queries = queries.reshape(MEMBERS, NLON, HEADS, HEAD).astype(jnp.float32)
        key_rows = key_rows.reshape(MEMBERS, NLON, HEADS, HEAD).astype(jnp.float32)
        value_rows = value_rows.reshape(MEMBERS, NLON, HEADS, HEAD).astype(jnp.float32)
        scores = jnp.einsum('mwhe,nwhe->nmhw', queries, key_rows) * score_scale
        row_max = lax.optimization_barrier(jnp.max(scores, axis=0, keepdims=True))
        exps = jnp.exp(scores - row_max)
        totals = lax.optimization_barrier(jnp.sum(exps, axis=0))
        weights = exps.astype(jnp.bfloat16).astype(jnp.float32)
        mixed_out = jnp.einsum('nmhw,nwhe->mwhe', weights, value_rows)
        mixed_out = mixed_out / jnp.transpose(totals, (0, 2, 1))[..., None]
        mixed_out = mixed_out.astype(jnp.bfloat16).reshape(MEMBERS, NLON, D)
        return (lat_row.astype(jnp.float32) + jnp.dot(mixed_out, w_out, preferred_element_type=jnp.float32)).astype(jnp.bfloat16)
    attended = jnp.moveaxis(lax.map(attend, jnp.moveaxis(fields, 1, 0)), 0, 1)
    retained = (jnp.arange(KLON, dtype=jnp.int32)[None, :] < mode_counts[:, None]).astype(jnp.float32)
    lon_fwd = lon_table(NLON, KLON).astype(jnp.float32)
    lon_back = lon_inverse(NLON, KLON).astype(jnp.float32)
    forward = lat_forward(NLAT, KLAT).astype(jnp.float32)
    inverse = lat_inverse(NLAT, KLAT).astype(jnp.float32)
    big_one = complex_blocks(w_first)
    big_two = complex_blocks(w_second)

    def spectral(member):
        normed_two = layer_norm(member, gain_spec).astype(jnp.bfloat16)
        spectrum = jnp.einsum('jxd,xk->jkd', normed_two.astype(jnp.float32), lon_fwd)
        spectrum = (spectrum.reshape(NLAT, 2, KLON, D) * retained[:, None, :, None]).astype(jnp.bfloat16)
        rows_spec = jnp.einsum('pqrj,jrkd->pqkd', forward, spectrum.astype(jnp.float32)).astype(jnp.bfloat16)
        hidden = jnp.maximum(mix_blocks(rows_spec, big_one), 0.0).astype(jnp.bfloat16)
        second = mix_blocks(hidden, big_two).astype(jnp.bfloat16)
        back_rows = jnp.einsum('rpjq,pqkd->jrkd', inverse, second.astype(jnp.float32))
        back_rows = (back_rows * retained[:, None, :, None]).astype(jnp.bfloat16)
        field_out = jnp.einsum('jrkd,rkx->jxd', back_rows.astype(jnp.float32), lon_back)
        return (member.astype(jnp.float32) + field_out).astype(jnp.bfloat16)
    return lax.map(spectral, attended)
```

```python
import functools
import math

import jax
import jax.numpy as jnp
import numpy as np
from jax import lax
from jax.experimental import pallas as pl
from jax.experimental.pallas import tpu as pltpu
from jax.sharding import PartitionSpec as P

HEAD = 32
NLAT = 384
KLON = 384
KLAT = 128
CHUNKS = 6
BACK_CHUNKS = 2

MESH = pl.DeviceIdType.MESH
SWAP_AHEAD = 6
ARRIVE_LAG = 3
PACK = 16

norm_eps = 1e-05


def layer_norm(widened, gain_vec):
    center = widened - jnp.mean(widened, axis=-1, keepdims=True)
    spread = jnp.mean(center * center, axis=-1, keepdims=True)
    return (center * lax.rsqrt(spread + norm_eps) * gain_vec).astype(jnp.bfloat16)


def wave_order(groups):
    held = KLON // groups
    place = jnp.arange(2 * KLON, dtype=jnp.int32)
    part = place // held % 2
    wave = place // (2 * held) * held + place % held
    return part, wave


def lon_forward(points, groups):
    part, wave = wave_order(groups)
    positions = jnp.arange(points, dtype=jnp.int32)
    turn_count = wave[:, None] * positions[None, :] % points
    angles = 2.0 * math.pi / points * turn_count.astype(jnp.float32)
    factor = 1.0 / math.sqrt(points)
    return jnp.where(
        part[:, None] == 0, jnp.cos(angles) * factor, -jnp.sin(angles) * factor
    ).astype(jnp.bfloat16)


def lon_inverse(points, groups):
    part, wave = wave_order(groups)
    positions = jnp.arange(points, dtype=jnp.int32)
    turn_count = positions[:, None] * wave[None, :] % points
    angles = 2.0 * math.pi / points * turn_count.astype(jnp.float32)
    weight = jnp.where(wave == 0, 1.0, 2.0).astype(jnp.float32)[None, :] / math.sqrt(points)
    return jnp.where(
        part[None, :] == 0, jnp.cos(angles) * weight, -jnp.sin(angles) * weight
    ).astype(jnp.bfloat16)


def lat_angles(row_count, mode_count):
    frequency = jnp.arange(mode_count, dtype=jnp.int32)
    frequency = jnp.where(frequency < mode_count // 2, frequency, frequency - mode_count)
    positions = jnp.arange(row_count, dtype=jnp.int32)
    turn_count = frequency[:, None] * positions[None, :] % row_count
    return 2.0 * math.pi / row_count * turn_count.astype(jnp.float32)


def lat_forward(row_count, mode_count):
    angles = lat_angles(row_count, mode_count)
    factor = 1.0 / math.sqrt(row_count)
    cosine = jnp.cos(angles) * factor
    sine_part = jnp.sin(angles) * factor
    return jnp.stack(
        [jnp.stack([cosine, sine_part], axis=1), jnp.stack([-sine_part, cosine], axis=1)]
    ).astype(jnp.bfloat16)


def lat_inverse(row_count, mode_count):
    angles = jnp.transpose(lat_angles(row_count, mode_count))
    factor = 1.0 / math.sqrt(row_count)
    cosine = jnp.cos(angles) * factor
    sine_part = jnp.sin(angles) * factor
    return jnp.stack([jnp.stack([cosine, -sine_part]), jnp.stack([sine_part, cosine])]).astype(
        jnp.bfloat16
    )


def complex_blocks(weight):
    real_part = weight[0]
    imag_part = weight[1]
    return jnp.stack([jnp.stack([real_part, imag_part]), jnp.stack([-imag_part, real_part])])


def mix_blocks(spec, big):
    blocks = spec.reshape(spec.shape[:3] + (big.shape[2], big.shape[3]))
    out_blocks = jnp.einsum("pqkbi,psbio->sqkbo", blocks, big, preferred_element_type=jnp.float32)
    return out_blocks.reshape(spec.shape)


def dot(left, right):
    return jnp.dot(left, right, preferred_element_type=jnp.float32)


def attend_kernel(others, first_row, sub, counts, own, *refs):
    other_refs = refs[:others]
    (gain_one, w_qkv, w_out, gain_two, table, sums, waves, attended, spectrum, normed) = refs[others:]
    points, feat = own.shape[1:]
    scale = 1.0 / math.sqrt(HEAD)
    for start in range(0, points, sub):
        rows = pl.ds(start, sub)
        fields = own[0, rows, :].astype(jnp.float32)
        joined = dot(layer_norm(fields, gain_one[...]), w_qkv[...]).astype(jnp.bfloat16)
        queries = joined[:, :feat].astype(jnp.float32)
        own_keys = joined[:, feat : 2 * feat].astype(jnp.float32)
        values = [joined[:, 2 * feat :].astype(jnp.float32)]
        shifted = [jnp.zeros((sub, feat), jnp.float32)]
        for ref in other_refs:
            side = layer_norm(ref[0, rows, :].astype(jnp.float32), gain_one[...])
            pair = dot(side, w_qkv[:, feat:]).astype(jnp.bfloat16)
            terms = queries * (pair[:, :feat].astype(jnp.float32) - own_keys)
            upper = terms.astype(jnp.bfloat16)
            lower = (terms - upper.astype(jnp.float32)).astype(jnp.bfloat16)
            total = dot(upper, sums[...]) + dot(lower, sums[...])
            shifted.append(total * scale)
            values.append(pair[:, feat:].astype(jnp.float32))
        largest = functools.reduce(jnp.maximum, shifted)
        exps = [jnp.exp(item - largest) for item in shifted]
        totals = functools.reduce(jnp.add, exps)
        mixed = functools.reduce(
            jnp.add,
            [e.astype(jnp.bfloat16).astype(jnp.float32) * v for e, v in zip(exps, values)],
        )
        mixed = (mixed / totals).astype(jnp.bfloat16)
        result = (fields + dot(mixed, w_out[...])).astype(jnp.bfloat16)
        attended[0, rows, :] = result
        normed[rows, :] = layer_norm(result.astype(jnp.float32), gain_two[...])
    kept = waves[...] < counts[first_row + pl.program_id(0)]
    spec = dot(table[...], normed[...])
    spec = jnp.where(kept, spec, 0.0).astype(jnp.bfloat16)
    if len(spectrum.shape) == 4:
        spectrum[:, 0] = spec.reshape(spectrum.shape[0], spectrum.shape[2], feat)
    else:
        spectrum[0] = spec


def attend(chunk, rows, aligned, groups, fields, others, counts, gains, weights, tables):
    points, feat = fields.shape[1:]
    first_row = chunk * rows
    sub = points // 3 if points % 48 == 0 else points
    whole = lambda a: pl.BlockSpec(a.shape, lambda i, c: (0,) * a.ndim)
    w_qkv, w_out = weights
    table, sums, waves = tables
    held = 2 * KLON // groups
    if aligned:
        spec_shape = (groups, rows, held, feat)
        spec_block = pl.BlockSpec((groups, 1, held, feat), lambda i, c: (0, i, 0, 0))
    else:
        spec_shape = (rows, 2 * KLON, feat)
        spec_block = pl.BlockSpec((1, 2 * KLON, feat), lambda i, c: (i, 0, 0))
    row_block = pl.BlockSpec((1, points, feat), lambda i, c: (i, 0, 0))
    own_block = pl.BlockSpec((1, points, feat), lambda i, c: (first_row + i, 0, 0))
    params = (gains[0], w_qkv, w_out, gains[1], table, sums, waves)
    flops = 2 * rows * points * feat * (feat * 8 + 2 * KLON)
    attended, spectrum = pl.pallas_call(
        functools.partial(attend_kernel, len(others), first_row, sub),
        grid_spec=pltpu.PrefetchScalarGridSpec(
            num_scalar_prefetch=1,
            grid=(rows,),
            in_specs=[own_block] + [row_block] * len(others) + [whole(p) for p in params],
            out_specs=[row_block, spec_block],
            scratch_shapes=[pltpu.VMEM((points, feat), jnp.bfloat16)],
        ),
        out_shape=[
            jax.ShapeDtypeStruct((rows, points, feat), jnp.bfloat16),
            jax.ShapeDtypeStruct(spec_shape, jnp.bfloat16),
        ],
        cost_estimate=pl.CostEstimate(
            flops=flops, bytes_accessed=rows * points * feat * 8, transcendentals=rows * points * feat * 2
        ),
        compiler_params=pltpu.CompilerParams(vmem_limit_bytes=40 * 1024 * 1024),
    )(counts, fields, *others, *params)
    if not aligned:
        spectrum = jnp.transpose(spectrum.reshape(rows, groups, held, feat), (1, 0, 2, 3))
    return attended, spectrum


def finish_kernel(first_row, counts, spectrum, attended, table, waves, *refs):
    out = refs[-1]
    feat = out.shape[-1]
    kept = waves[...] < counts[first_row + pl.program_id(0)]
    if len(spectrum.shape) == 4:
        spec = spectrum[:, 0].reshape(2 * KLON, feat)
    else:
        spec = spectrum[0]
    spec = jnp.where(kept, spec.astype(jnp.float32), 0.0).astype(jnp.bfloat16)
    out[0] = (attended[0].astype(jnp.float32) + dot(table[...], spec)).astype(jnp.bfloat16)


def finish(first_row, offset, lat_dev, aligned, groups, spectrum, attended, counts, table, waves, so_far):
    rows, points, feat = attended.shape
    held = 2 * KLON // groups
    whole = lambda a: pl.BlockSpec(a.shape, lambda i, c: (0,) * a.ndim)
    if aligned:
        spec_block = pl.BlockSpec((groups, 1, held, feat), lambda i, c: (0, offset + i, 0, 0))
    else:
        spectrum = jnp.transpose(spectrum, (1, 0, 2, 3)).reshape(-1, 2 * KLON, feat)
        spec_block = pl.BlockSpec((1, 2 * KLON, feat), lambda i, c: (offset + i, 0, 0))
    row_block = pl.BlockSpec((1, points, feat), lambda i, c: (i, 0, 0))
    out_block = pl.BlockSpec((1, points, feat), lambda i, c: (first_row + i, 0, 0))
    operands = [counts, spectrum, attended, table, waves]
    specs = [spec_block, row_block, whole(table), whole(waves)]
    aliases = {}
    if so_far is not None:
        aliases = {len(operands): 0}
        operands.append(so_far)
        specs.append(pl.BlockSpec(memory_space=pl.ANY))
    return pl.pallas_call(
        functools.partial(finish_kernel, first_row),
        grid_spec=pltpu.PrefetchScalarGridSpec(
            num_scalar_prefetch=1, grid=(rows,), in_specs=specs, out_specs=out_block
        ),
        out_shape=jax.ShapeDtypeStruct((lat_dev, points, feat), jnp.bfloat16),
        input_output_aliases=aliases,
        cost_estimate=pl.CostEstimate(
            flops=4 * rows * points * feat * KLON,
            bytes_accessed=rows * points * feat * 6,
            transcendentals=0,
        ),
        compiler_params=pltpu.CompilerParams(vmem_limit_bytes=40 * 1024 * 1024),
    )(*operands)


def shards(
    mesh_sizes, fields, mode_counts, gain_attn, w_query, w_key, w_value, w_out, gain_spec, w_first, w_second
):
    members, groups = mesh_sizes
    fields = fields[0]
    lat_dev, points, feat = fields.shape
    held = KLON // groups
    aligned = (2 * held) % 16 == 0
    chunks = max(c for c in range(1, CHUNKS + 1) if lat_dev % c == 0)
    rows = lat_dev // chunks
    shifts = [
        [(i, (i + s) % members) for i in range(members)] for s in range(1, members)
    ]
    others = []
    for c in range(chunks):
        others.append([lax.ppermute(fields[c * rows : (c + 1) * rows], "ens", s) for s in shifts])
    w_qkv = jnp.concatenate([w_query, w_key, w_value], axis=1)
    lanes = jnp.arange(feat, dtype=jnp.int32) // HEAD
    sums = (lanes[:, None] == lanes[None, :]).astype(jnp.bfloat16)
    waves = wave_order(groups)[1][:, None]
    gains = (gain_attn[None, :], gain_spec[None, :])
    tables = (lon_forward(points, groups), sums, waves)
    back_table = lon_inverse(points, groups)
    forward = lat_forward(NLAT, KLAT).reshape(2, KLAT, 2, groups, chunks, rows)
    backs = max(c for c in range(1, BACK_CHUNKS + 1) if chunks % c == 0)
    per_back = chunks // backs
    inverse = lat_inverse(NLAT, KLAT).reshape(2, 2, groups, backs, per_back * rows, KLAT)
    big_one = complex_blocks(w_first)
    big_two = complex_blocks(w_second)
    kept_fields = []
    rows_spec = None
    for c in range(chunks):
        attended, spectrum = attend(
            c, rows, aligned, groups, fields, others[c], mode_counts, gains, (w_qkv, w_out), tables
        )
        kept_fields.append(attended)
        arrived = lax.all_to_all(spectrum, "grid", split_axis=0, concat_axis=0)
        arrived = arrived.reshape(groups, rows, 2, held, feat)
        term = jnp.einsum(
            "pqrgj,gjrkd->pqkd",
            forward[:, :, :, :, c],
            arrived,
            preferred_element_type=jnp.float32,
        )
        rows_spec = term if rows_spec is None else rows_spec + term
        if c < chunks - 1:
            rows_spec = lax.optimization_barrier(rows_spec)
    rows_spec = rows_spec.astype(jnp.bfloat16)
    hidden = jnp.maximum(mix_blocks(rows_spec, big_one), 0.0).astype(jnp.bfloat16)
    second = mix_blocks(hidden, big_two).astype(jnp.bfloat16)
    out = None
    for b in range(backs):
        back_rows = jnp.einsum(
            "rpgjq,pqkd->gjrkd", inverse[:, :, :, b], second, preferred_element_type=jnp.float32
        ).astype(jnp.bfloat16)
        returned = lax.all_to_all(
            back_rows.reshape(groups, per_back * rows, 2 * held, feat), "grid", split_axis=0, concat_axis=0
        )
        for i in range(per_back):
            c = b * per_back + i
            out = finish(
                c * rows, i * rows, lat_dev, aligned, groups, returned, kept_fields[c], mode_counts,
                back_table, tables[2], out,
            )
    return out[None]


def np_wave_order(groups):
    held = KLON // groups
    place = np.arange(2 * KLON)
    return place // held % 2, place // (2 * held) * held + place % held


def np_lon_forward(points, groups):
    part, wave = np_wave_order(groups)
    turns = wave[:, None] * np.arange(points)[None, :] % points
    angles = 2.0 * math.pi / points * turns
    rows = np.where(part[:, None] == 0, np.cos(angles), -np.sin(angles)) / math.sqrt(points)
    return jnp.asarray(rows.astype(np.float32), dtype=jnp.bfloat16)


def np_lat_tables(groups, batches, nb):
    frequency = np.arange(KLAT)
    frequency = np.where(frequency < KLAT // 2, frequency, frequency - KLAT)
    angles = 2.0 * math.pi / NLAT * (frequency[:, None] * np.arange(NLAT)[None, :] % NLAT)
    cosine = np.cos(angles) / math.sqrt(NLAT)
    sine = np.sin(angles) / math.sqrt(NLAT)
    both = np.stack([np.stack([cosine, sine], axis=1), np.stack([-sine, cosine], axis=1)])
    forward = both.reshape(2, KLAT, 2, groups, batches, nb).transpose(4, 0, 1, 2, 5, 3)
    forward = forward.reshape(batches, 2 * KLAT, 2 * nb * groups).astype(np.float32)
    inverse = forward.transpose(0, 2, 1)
    return jnp.asarray(forward, dtype=jnp.bfloat16), jnp.asarray(inverse, dtype=jnp.bfloat16)


def np_turn(groups):
    count = groups * PACK
    source = np.arange(count).reshape(groups, PACK).T.reshape(-1)
    turn = np.zeros((count, count), np.float32)
    turn[np.arange(count), source] = 1.0
    return jnp.asarray(turn, dtype=jnp.bfloat16)


def layer_kernel(
    points_sub,
    nb,
    counts,
    fields,
    gain_one,
    w_query,
    w_key,
    w_value,
    w_out,
    gain_two,
    table,
    sums,
    waves,
    forward,
    inverse,
    turn,
    turn_back,
    spread,
    w_first,
    w_second,
    out,
    own,
    other,
    attended,
    sent,
    arrived,
    turned,
    rows_spec,
    second,
    normed,
    back_table,
    blocks,
    result,
    own_sem,
    swap_send,
    swap_recv,
    fwd_send,
    fwd_recv,
    back_send,
    back_recv,
    out_sem,
):
    rows, groups, width, feat = sent.shape
    points = other.shape[1]
    held = width // 2
    packs = width // PACK
    sub = points_sub
    member = lax.axis_index("ens")
    me = lax.axis_index("grid")
    scale = 1.0 / math.sqrt(HEAD)
    partners = [me ^ o for o in range(groups - 1, 0, -1)]

    barrier = pltpu.get_barrier_semaphore()
    for t in partners:
        pl.semaphore_signal(barrier, inc=1, device_id={"grid": t}, device_id_type=MESH)
    pl.semaphore_signal(barrier, inc=1, device_id={"ens": 1 - member}, device_id_type=MESH)
    pl.semaphore_wait(barrier, groups)

    def swap(r):
        return pltpu.make_async_remote_copy(
            src_ref=fields.at[r],
            dst_ref=other.at[r],
            send_sem=swap_send.at[r],
            recv_sem=swap_recv.at[r],
            device_id={"ens": 1 - member},
            device_id_type=MESH,
        )

    def fetch(r, slot):
        return pltpu.make_async_copy(fields.at[r], own.at[slot], own_sem.at[slot])

    ahead = min(SWAP_AHEAD, rows)
    for r in range(ahead):
        swap(r).start()
    fetch(0, 0).start()

    eye = lax.broadcasted_iota(jnp.int32, (feat, feat), 0) // HEAD
    same = eye == lax.broadcasted_iota(jnp.int32, (feat, feat), 1) // HEAD
    for layer, weight in enumerate((w_first, w_second)):
        for part in range(2):
            wide = dot(weight[part], spread[...])
            blocks[2 * layer + part] = jnp.where(same, wide, 0.0).astype(jnp.bfloat16)
    back_table[...] = jnp.transpose(table[...])
    rows_spec[...] = jnp.zeros_like(rows_spec)
    spot = pl.ds(pl.multiple_of(me * width, PACK), width)

    def attend(r):
        slot = lax.rem(r, 2)
        fetch(r, slot).wait()

        @pl.when(r + 1 < rows)
        def _():
            fetch(r + 1, 1 - slot).start()

        swap(r).wait_recv()

        @pl.when(r + ahead < rows)
        def _():
            swap(r + ahead).start()

        for start in range(0, points, sub):
            span = pl.ds(start, sub)
            field = own[slot, span, :].astype(jnp.float32)
            norm = layer_norm(field, gain_one[...])
            queries = dot(norm, w_query[...]).astype(jnp.bfloat16).astype(jnp.float32)
            own_keys = dot(norm, w_key[...]).astype(jnp.bfloat16).astype(jnp.float32)
            own_values = dot(norm, w_value[...]).astype(jnp.bfloat16).astype(jnp.float32)
            side = layer_norm(other[r, span, :].astype(jnp.float32), gain_one[...])
            keys = dot(side, w_key[...]).astype(jnp.bfloat16).astype(jnp.float32)
            values = dot(side, w_value[...]).astype(jnp.bfloat16).astype(jnp.float32)
            terms = queries * (keys - own_keys)
            upper = terms.astype(jnp.bfloat16)
            lower = (terms - upper.astype(jnp.float32)).astype(jnp.bfloat16)
            shifted = (dot(upper, sums[...]) + dot(lower, sums[...])) * scale
            largest = jnp.maximum(shifted, 0.0)
            own_exp = jnp.exp(-largest)
            side_exp = jnp.exp(shifted - largest)
            mixed = own_exp.astype(jnp.bfloat16).astype(jnp.float32) * own_values
            mixed += side_exp.astype(jnp.bfloat16).astype(jnp.float32) * values
            mixed = (mixed / (own_exp + side_exp)).astype(jnp.bfloat16)
            done = (field + dot(mixed, w_out[...])).astype(jnp.bfloat16)
            attended[r, span, :] = done
            normed[span, :] = layer_norm(done.astype(jnp.float32), gain_two[...])
        spec = dot(table[...], normed[...])
        spec = jnp.where(waves[...] < counts[r], spec, 0.0).astype(jnp.bfloat16)
        sent[r] = spec.reshape(groups, width, feat)
        arrived[r, me] = sent[r, me]
        for t in partners:
            pltpu.make_async_remote_copy(
                src_ref=sent.at[r, t],
                dst_ref=arrived.at[r, me],
                send_sem=fwd_send.at[r],
                recv_sem=fwd_recv.at[r],
                device_id={"grid": t},
                device_id_type=MESH,
            ).start()

    def turn_in(r):
        whole = arrived.at[r, pl.ds(0, groups - 1)]
        pltpu.make_async_copy(whole, whole, fwd_recv.at[r]).wait()
        place = pl.ds(pl.multiple_of(lax.rem(r, nb) * groups, PACK), groups)
        for b in range(packs):
            block = arrived[r, :, b * PACK : (b + 1) * PACK, :].reshape(groups * PACK, feat)
            moved = dot(turn[...], block).astype(jnp.bfloat16)
            turned[b * PACK : (b + 1) * PACK, place, :] = moved.reshape(PACK, groups, feat)

    def lat_in(b):
        def step(k, _):
            pair = jnp.concatenate([turned[k], turned[held + k]], axis=0)
            rows_spec[k] += dot(forward[b], pair)
            return 0

        lax.fori_loop(0, held, step, 0, unroll=4)

    def phase_in(i, _):
        @pl.when(i < rows)
        def _():
            attend(i)

        @pl.when(i >= ARRIVE_LAG)
        def _():
            turn_in(i - ARRIVE_LAG)

        @pl.when((i >= ARRIVE_LAG) & (lax.rem(i - ARRIVE_LAG, nb) == nb - 1))
        def _():
            lat_in((i - ARRIVE_LAG) // nb)

        return 0

    lax.fori_loop(0, rows + ARRIVE_LAG, phase_in, 0)

    half = second.shape[1] // 2
    per = max(p for p in range(1, 5) if held % p == 0)

    def complex_mix(real, imag, layer):
        w_real, w_imag = blocks[2 * layer], blocks[2 * layer + 1]
        return dot(real, w_real) - dot(imag, w_imag), dot(real, w_imag) + dot(imag, w_real)

    def mix(i, _):
        span = pl.ds(i * per, per)
        real = rows_spec[span, :half].reshape(per * half, feat).astype(jnp.bfloat16)
        imag = rows_spec[span, half:].reshape(per * half, feat).astype(jnp.bfloat16)
        real, imag = complex_mix(real, imag, 0)
        real = jnp.maximum(real, 0.0).astype(jnp.bfloat16)
        imag = jnp.maximum(imag, 0.0).astype(jnp.bfloat16)
        real, imag = complex_mix(real, imag, 1)
        second[span, :half] = real.astype(jnp.bfloat16).reshape(per, half, feat)
        second[span, half:] = imag.astype(jnp.bfloat16).reshape(per, half, feat)
        return 0

    lax.fori_loop(0, held // per, mix, 0)

    def wait_sent(r):
        whole = sent.at[r, pl.ds(0, groups - 1)]
        pltpu.make_async_copy(whole, whole, fwd_send.at[r]).wait()

    def lat_out(b):
        def step(k, _):
            both = dot(inverse[b], second[k]).astype(jnp.bfloat16)
            turned[k] = both[: nb * groups]
            turned[held + k] = both[nb * groups :]
            return 0

        lax.fori_loop(0, held, step, 0, unroll=4)

        def send_row(r, _):
            j = b * nb + r
            wait_sent(j)
            place = pl.ds(pl.multiple_of(r * groups, PACK), groups)
            for p in range(packs):
                block = turned[p * PACK : (p + 1) * PACK, place, :].reshape(groups * PACK, feat)
                moved = dot(turn_back[...], block).astype(jnp.bfloat16)
                sent[j, :, p * PACK : (p + 1) * PACK, :] = moved.reshape(groups, PACK, feat)
            other[j, spot, :] = sent[j, me]
            for t in partners:
                pltpu.make_async_remote_copy(
                    src_ref=sent.at[j, t],
                    dst_ref=other.at[j, spot],
                    send_sem=back_send.at[j],
                    recv_sem=back_recv.at[j],
                    device_id={"grid": t},
                    device_id_type=MESH,
                ).start()
            return 0

        lax.fori_loop(0, nb, send_row, 0)

    def put(j, slot):
        return pltpu.make_async_copy(result.at[slot], out.at[j], out_sem.at[slot])

    def finish(j):
        whole = other.at[j, pl.ds(0, (groups - 1) * width)]
        pltpu.make_async_copy(whole, whole, back_recv.at[j]).wait()
        weight = jnp.where(waves[...] == 0, 1.0, 2.0)
        weight = jnp.where(waves[...] < counts[j], weight, 0.0)
        spec = (other[j].astype(jnp.float32) * weight).astype(jnp.bfloat16)
        total = attended[j].astype(jnp.float32) + dot(back_table[...], spec)
        slot = lax.rem(j, 2)

        @pl.when(j >= 2)
        def _():
            put(j - 2, slot).wait()

        result[slot] = total.astype(jnp.bfloat16)
        put(j, slot).start()

    def phase_out(i, _):
        @pl.when((i < rows) & (lax.rem(i, nb) == 0))
        def _():
            lat_out(i // nb)

        @pl.when(i >= nb)
        def _():
            finish(i - nb)

        return 0

    lax.fori_loop(0, rows + nb, phase_out, 0)

    def drain(r, _):
        swap(r).wait_send()
        whole = sent.at[r, pl.ds(0, groups - 1)]
        pltpu.make_async_copy(whole, whole, back_send.at[r]).wait()
        return 0

    lax.fori_loop(0, rows, drain, 0)
    for j in range(rows - 2, rows):
        put(j, j % 2).wait()


def fused(mesh_sizes, fields, mode_counts, gain_attn, w_query, w_key, w_value, w_out, gain_spec, w_first, w_second):
    _, groups = mesh_sizes
    fields = fields[0]
    rows, points, feat = fields.shape
    width = 2 * KLON // groups
    held = width // 2
    nb = max(n for n in range(1, rows + 1) if rows % n == 0 and 2 * n * groups <= max(feat, 2 * groups))
    forward, inverse = np_lat_tables(groups, rows // nb, nb)
    turn = np_turn(groups)
    block = w_first.shape[-1]
    lanes = np.arange(feat)
    heads = jnp.asarray((lanes[:, None] // HEAD == lanes[None, :] // HEAD).astype(np.float32), dtype=jnp.bfloat16)
    spread = jnp.asarray((np.arange(block)[:, None] == lanes[None, :] % block).astype(np.float32), dtype=jnp.bfloat16)
    waves = jnp.asarray(np_wave_order(groups)[1][:, None], dtype=jnp.int32)
    operands = [
        mode_counts, fields, gain_attn[None, :], w_query, w_key, w_value, w_out, gain_spec[None, :],
        np_lon_forward(points, groups), heads, waves, forward, inverse, turn, turn.T, spread,
        w_first.reshape(2, feat, block), w_second.reshape(2, feat, block),
    ]
    vmem = pl.BlockSpec(memory_space=pltpu.VMEM)
    hbm = pl.BlockSpec(memory_space=pl.ANY)
    specs = [pl.BlockSpec(memory_space=pltpu.SMEM), hbm] + [vmem] * (len(operands) - 2)
    half = jnp.bfloat16
    dma = pltpu.SemaphoreType.DMA
    out = pl.pallas_call(
        functools.partial(layer_kernel, points // 3 if points % 48 == 0 else points, nb),
        in_specs=specs,
        out_specs=hbm,
        out_shape=jax.ShapeDtypeStruct((rows, points, feat), half),
        scratch_shapes=[
            pltpu.VMEM((2, points, feat), half),
            pltpu.VMEM((rows, points, feat), half),
            pltpu.VMEM((rows, points, feat), half),
            pltpu.VMEM((rows, groups, width, feat), half),
            pltpu.VMEM((rows, groups, width, feat), half),
            pltpu.VMEM((width, nb * groups, feat), half),
            pltpu.VMEM((held, 2 * KLAT, feat), jnp.float32),
            pltpu.VMEM((held, 2 * KLAT, feat), half),
            pltpu.VMEM((points, feat), half),
            pltpu.VMEM((points, 2 * KLON), half),
            pltpu.VMEM((4, feat, feat), half),
            pltpu.VMEM((2, points, feat), half),
            dma((2,)),
            dma((rows,)),
            dma((rows,)),
            dma((rows,)),
            dma((rows,)),
            dma((rows,)),
            dma((rows,)),
            dma((2,)),
        ],
        compiler_params=pltpu.CompilerParams(
            collective_id=0, has_side_effects=True, vmem_limit_bytes=67043328
        ),
        name="layer",
    )(*operands)
    return out[None]


def streams(members, groups, lat_dev, points, feat):
    width = 2 * KLON // groups
    return (
        members == 2
        and groups == PACK
        and (2 * KLON) % (groups * PACK) == 0
        and points == 2 * KLON
        and feat % 128 == 0
        and lat_dev % 2 == 0
        and width % PACK == 0
    )


def layer(mesh_sizes, *args):
    if streams(*mesh_sizes, *args[0].shape[1:]):
        return fused(mesh_sizes, *args)
    return shards(mesh_sizes, *args)


def solution(mesh):
    in_specs = (P("ens", "grid", None, None), P("grid"), P(), P(), P(), P(), P(), P(), P(), P())
    out_specs = P("ens", "grid", None, None)
    sizes = (mesh.shape["ens"], mesh.shape["grid"])
    return jax.shard_map(
        functools.partial(layer, sizes),
        mesh=mesh,
        in_specs=in_specs,
        out_specs=out_specs,
        check_vma=False,
    )
```

```python
import functools
import math

import jax
import jax.numpy as jnp
import numpy as np
from jax import lax
from jax.experimental import pallas as pl
from jax.experimental.pallas import tpu as pltpu
from jax.sharding import PartitionSpec as P

HEAD = 32
NLAT = 384
KLON = 384
KLAT = 128
CHUNKS = 6
BACK_CHUNKS = 2

MESH = pl.DeviceIdType.MESH
SWAP_AHEAD = 6
ARRIVE_LAG = 3
PACK = 16

norm_eps = 1e-05


def layer_norm(widened, gain_vec):
    center = widened - jnp.mean(widened, axis=-1, keepdims=True)
    spread = jnp.mean(center * center, axis=-1, keepdims=True)
    return (center * lax.rsqrt(spread + norm_eps) * gain_vec).astype(jnp.bfloat16)


def wave_order(groups):
    held = KLON // groups
    place = jnp.arange(2 * KLON, dtype=jnp.int32)
    part = place // held % 2
    wave = place // (2 * held) * held + place % held
    return part, wave


def lon_forward(points, groups):
    part, wave = wave_order(groups)
    positions = jnp.arange(points, dtype=jnp.int32)
    turn_count = wave[:, None] * positions[None, :] % points
    angles = 2.0 * math.pi / points * turn_count.astype(jnp.float32)
    factor = 1.0 / math.sqrt(points)
    return jnp.where(
        part[:, None] == 0, jnp.cos(angles) * factor, -jnp.sin(angles) * factor
    ).astype(jnp.bfloat16)


def lon_inverse(points, groups):
    part, wave = wave_order(groups)
    positions = jnp.arange(points, dtype=jnp.int32)
    turn_count = positions[:, None] * wave[None, :] % points
    angles = 2.0 * math.pi / points * turn_count.astype(jnp.float32)
    weight = jnp.where(wave == 0, 1.0, 2.0).astype(jnp.float32)[None, :] / math.sqrt(points)
    return jnp.where(
        part[None, :] == 0, jnp.cos(angles) * weight, -jnp.sin(angles) * weight
    ).astype(jnp.bfloat16)


def lat_angles(row_count, mode_count):
    frequency = jnp.arange(mode_count, dtype=jnp.int32)
    frequency = jnp.where(frequency < mode_count // 2, frequency, frequency - mode_count)
    positions = jnp.arange(row_count, dtype=jnp.int32)
    turn_count = frequency[:, None] * positions[None, :] % row_count
    return 2.0 * math.pi / row_count * turn_count.astype(jnp.float32)


def lat_forward(row_count, mode_count):
    angles = lat_angles(row_count, mode_count)
    factor = 1.0 / math.sqrt(row_count)
    cosine = jnp.cos(angles) * factor
    sine_part = jnp.sin(angles) * factor
    return jnp.stack(
        [jnp.stack([cosine, sine_part], axis=1), jnp.stack([-sine_part, cosine], axis=1)]
    ).astype(jnp.bfloat16)


def lat_inverse(row_count, mode_count):
    angles = jnp.transpose(lat_angles(row_count, mode_count))
    factor = 1.0 / math.sqrt(row_count)
    cosine = jnp.cos(angles) * factor
    sine_part = jnp.sin(angles) * factor
    return jnp.stack([jnp.stack([cosine, -sine_part]), jnp.stack([sine_part, cosine])]).astype(
        jnp.bfloat16
    )


def complex_blocks(weight):
    real_part = weight[0]
    imag_part = weight[1]
    return jnp.stack([jnp.stack([real_part, imag_part]), jnp.stack([-imag_part, real_part])])


def mix_blocks(spec, big):
    blocks = spec.reshape(spec.shape[:3] + (big.shape[2], big.shape[3]))
    out_blocks = jnp.einsum("pqkbi,psbio->sqkbo", blocks, big, preferred_element_type=jnp.float32)
    return out_blocks.reshape(spec.shape)


def dot(left, right):
    return jnp.dot(left, right, preferred_element_type=jnp.float32)


def attend_kernel(others, first_row, sub, counts, own, *refs):
    other_refs = refs[:others]
    (gain_one, w_qkv, w_out, gain_two, table, sums, waves, attended, spectrum, normed) = refs[others:]
    points, feat = own.shape[1:]
    scale = 1.0 / math.sqrt(HEAD)
    for start in range(0, points, sub):
        rows = pl.ds(start, sub)
        fields = own[0, rows, :].astype(jnp.float32)
        joined = dot(layer_norm(fields, gain_one[...]), w_qkv[...]).astype(jnp.bfloat16)
        queries = joined[:, :feat].astype(jnp.float32)
        own_keys = joined[:, feat : 2 * feat].astype(jnp.float32)
        values = [joined[:, 2 * feat :].astype(jnp.float32)]
        shifted = [jnp.zeros((sub, feat), jnp.float32)]
        for ref in other_refs:
            side = layer_norm(ref[0, rows, :].astype(jnp.float32), gain_one[...])
            pair = dot(side, w_qkv[:, feat:]).astype(jnp.bfloat16)
            terms = queries * (pair[:, :feat].astype(jnp.float32) - own_keys)
            upper = terms.astype(jnp.bfloat16)
            lower = (terms - upper.astype(jnp.float32)).astype(jnp.bfloat16)
            total = dot(upper, sums[...]) + dot(lower, sums[...])
            shifted.append(total * scale)
            values.append(pair[:, feat:].astype(jnp.float32))
        largest = functools.reduce(jnp.maximum, shifted)
        exps = [jnp.exp(item - largest) for item in shifted]
        totals = functools.reduce(jnp.add, exps)
        mixed = functools.reduce(
            jnp.add,
            [e.astype(jnp.bfloat16).astype(jnp.float32) * v for e, v in zip(exps, values)],
        )
        mixed = (mixed / totals).astype(jnp.bfloat16)
        result = (fields + dot(mixed, w_out[...])).astype(jnp.bfloat16)
        attended[0, rows, :] = result
        normed[rows, :] = layer_norm(result.astype(jnp.float32), gain_two[...])
    kept = waves[...] < counts[first_row + pl.program_id(0)]
    spec = dot(table[...], normed[...])
    spec = jnp.where(kept, spec, 0.0).astype(jnp.bfloat16)
    if len(spectrum.shape) == 4:
        spectrum[:, 0] = spec.reshape(spectrum.shape[0], spectrum.shape[2], feat)
    else:
        spectrum[0] = spec


def attend(chunk, rows, aligned, groups, fields, others, counts, gains, weights, tables):
    points, feat = fields.shape[1:]
    first_row = chunk * rows
    sub = points // 3 if points % 48 == 0 else points
    whole = lambda a: pl.BlockSpec(a.shape, lambda i, c: (0,) * a.ndim)
    w_qkv, w_out = weights
    table, sums, waves = tables
    held = 2 * KLON // groups
    if aligned:
        spec_shape = (groups, rows, held, feat)
        spec_block = pl.BlockSpec((groups, 1, held, feat), lambda i, c: (0, i, 0, 0))
    else:
        spec_shape = (rows, 2 * KLON, feat)
        spec_block = pl.BlockSpec((1, 2 * KLON, feat), lambda i, c: (i, 0, 0))
    row_block = pl.BlockSpec((1, points, feat), lambda i, c: (i, 0, 0))
    own_block = pl.BlockSpec((1, points, feat), lambda i, c: (first_row + i, 0, 0))
    params = (gains[0], w_qkv, w_out, gains[1], table, sums, waves)
    flops = 2 * rows * points * feat * (feat * 8 + 2 * KLON)
    attended, spectrum = pl.pallas_call(
        functools.partial(attend_kernel, len(others), first_row, sub),
        grid_spec=pltpu.PrefetchScalarGridSpec(
            num_scalar_prefetch=1,
            grid=(rows,),
            in_specs=[own_block] + [row_block] * len(others) + [whole(p) for p in params],
            out_specs=[row_block, spec_block],
            scratch_shapes=[pltpu.VMEM((points, feat), jnp.bfloat16)],
        ),
        out_shape=[
            jax.ShapeDtypeStruct((rows, points, feat), jnp.bfloat16),
            jax.ShapeDtypeStruct(spec_shape, jnp.bfloat16),
        ],
        cost_estimate=pl.CostEstimate(
            flops=flops, bytes_accessed=rows * points * feat * 8, transcendentals=rows * points * feat * 2
        ),
        compiler_params=pltpu.CompilerParams(vmem_limit_bytes=40 * 1024 * 1024),
    )(counts, fields, *others, *params)
    if not aligned:
        spectrum = jnp.transpose(spectrum.reshape(rows, groups, held, feat), (1, 0, 2, 3))
    return attended, spectrum


def finish_kernel(first_row, counts, spectrum, attended, table, waves, *refs):
    out = refs[-1]
    feat = out.shape[-1]
    kept = waves[...] < counts[first_row + pl.program_id(0)]
    if len(spectrum.shape) == 4:
        spec = spectrum[:, 0].reshape(2 * KLON, feat)
    else:
        spec = spectrum[0]
    spec = jnp.where(kept, spec.astype(jnp.float32), 0.0).astype(jnp.bfloat16)
    out[0] = (attended[0].astype(jnp.float32) + dot(table[...], spec)).astype(jnp.bfloat16)


def finish(first_row, offset, lat_dev, aligned, groups, spectrum, attended, counts, table, waves, so_far):
    rows, points, feat = attended.shape
    held = 2 * KLON // groups
    whole = lambda a: pl.BlockSpec(a.shape, lambda i, c: (0,) * a.ndim)
    if aligned:
        spec_block = pl.BlockSpec((groups, 1, held, feat), lambda i, c: (0, offset + i, 0, 0))
    else:
        spectrum = jnp.transpose(spectrum, (1, 0, 2, 3)).reshape(-1, 2 * KLON, feat)
        spec_block = pl.BlockSpec((1, 2 * KLON, feat), lambda i, c: (offset + i, 0, 0))
    row_block = pl.BlockSpec((1, points, feat), lambda i, c: (i, 0, 0))
    out_block = pl.BlockSpec((1, points, feat), lambda i, c: (first_row + i, 0, 0))
    operands = [counts, spectrum, attended, table, waves]
    specs = [spec_block, row_block, whole(table), whole(waves)]
    aliases = {}
    if so_far is not None:
        aliases = {len(operands): 0}
        operands.append(so_far)
        specs.append(pl.BlockSpec(memory_space=pl.ANY))
    return pl.pallas_call(
        functools.partial(finish_kernel, first_row),
        grid_spec=pltpu.PrefetchScalarGridSpec(
            num_scalar_prefetch=1, grid=(rows,), in_specs=specs, out_specs=out_block
        ),
        out_shape=jax.ShapeDtypeStruct((lat_dev, points, feat), jnp.bfloat16),
        input_output_aliases=aliases,
        cost_estimate=pl.CostEstimate(
            flops=4 * rows * points * feat * KLON,
            bytes_accessed=rows * points * feat * 6,
            transcendentals=0,
        ),
        compiler_params=pltpu.CompilerParams(vmem_limit_bytes=40 * 1024 * 1024),
    )(*operands)


def shards(
    mesh_sizes, fields, mode_counts, gain_attn, w_query, w_key, w_value, w_out, gain_spec, w_first, w_second
):
    members, groups = mesh_sizes
    fields = fields[0]
    lat_dev, points, feat = fields.shape
    held = KLON // groups
    aligned = (2 * held) % 16 == 0
    chunks = max(c for c in range(1, CHUNKS + 1) if lat_dev % c == 0)
    rows = lat_dev // chunks
    shifts = [
        [(i, (i + s) % members) for i in range(members)] for s in range(1, members)
    ]
    others = []
    for c in range(chunks):
        others.append([lax.ppermute(fields[c * rows : (c + 1) * rows], "ens", s) for s in shifts])
    w_qkv = jnp.concatenate([w_query, w_key, w_value], axis=1)
    lanes = jnp.arange(feat, dtype=jnp.int32) // HEAD
    sums = (lanes[:, None] == lanes[None, :]).astype(jnp.bfloat16)
    waves = wave_order(groups)[1][:, None]
    gains = (gain_attn[None, :], gain_spec[None, :])
    tables = (lon_forward(points, groups), sums, waves)
    back_table = lon_inverse(points, groups)
    forward = lat_forward(NLAT, KLAT).reshape(2, KLAT, 2, groups, chunks, rows)
    backs = max(c for c in range(1, BACK_CHUNKS + 1) if chunks % c == 0)
    per_back = chunks // backs
    inverse = lat_inverse(NLAT, KLAT).reshape(2, 2, groups, backs, per_back * rows, KLAT)
    big_one = complex_blocks(w_first)
    big_two = complex_blocks(w_second)
    kept_fields = []
    rows_spec = None
    for c in range(chunks):
        attended, spectrum = attend(
            c, rows, aligned, groups, fields, others[c], mode_counts, gains, (w_qkv, w_out), tables
        )
        kept_fields.append(attended)
        arrived = lax.all_to_all(spectrum, "grid", split_axis=0, concat_axis=0)
        arrived = arrived.reshape(groups, rows, 2, held, feat)
        term = jnp.einsum(
            "pqrgj,gjrkd->pqkd",
            forward[:, :, :, :, c],
            arrived,
            preferred_element_type=jnp.float32,
        )
        rows_spec = term if rows_spec is None else rows_spec + term
        if c < chunks - 1:
            rows_spec = lax.optimization_barrier(rows_spec)
    rows_spec = rows_spec.astype(jnp.bfloat16)
    hidden = jnp.maximum(mix_blocks(rows_spec, big_one), 0.0).astype(jnp.bfloat16)
    second = mix_blocks(hidden, big_two).astype(jnp.bfloat16)
    out = None
    for b in range(backs):
        back_rows = jnp.einsum(
            "rpgjq,pqkd->gjrkd", inverse[:, :, :, b], second, preferred_element_type=jnp.float32
        ).astype(jnp.bfloat16)
        returned = lax.all_to_all(
            back_rows.reshape(groups, per_back * rows, 2 * held, feat), "grid", split_axis=0, concat_axis=0
        )
        for i in range(per_back):
            c = b * per_back + i
            out = finish(
                c * rows, i * rows, lat_dev, aligned, groups, returned, kept_fields[c], mode_counts,
                back_table, tables[2], out,
            )
    return out[None]


def np_wave_order(groups):
    held = KLON // groups
    each = PACK // 2
    place = np.arange(2 * KLON)
    group, pack, within = place // (2 * held), place % (2 * held) // PACK, place % each
    return place // each % 2, group * held + pack * each + within


def np_lon_forward(points, groups):
    part, wave = np_wave_order(groups)
    turns = wave[:, None] * np.arange(points)[None, :] % points
    angles = 2.0 * math.pi / points * turns
    rows = np.where(part[:, None] == 0, np.cos(angles), -np.sin(angles)) / math.sqrt(points)
    return jnp.asarray(rows.astype(np.float32), dtype=jnp.bfloat16)


def np_lat_tables(groups, batches, nb):
    frequency = np.arange(KLAT)
    frequency = np.where(frequency < KLAT // 2, frequency, frequency - KLAT)
    angles = 2.0 * math.pi / NLAT * (frequency[:, None] * np.arange(NLAT)[None, :] % NLAT)
    cosine = np.cos(angles) / math.sqrt(NLAT)
    sine = np.sin(angles) / math.sqrt(NLAT)
    both = np.stack([np.stack([cosine, sine], axis=1), np.stack([-sine, cosine], axis=1)])
    forward = both.reshape(2, KLAT, 2, groups, batches, nb).transpose(4, 0, 1, 2, 5, 3)
    forward = forward.reshape(batches, 2 * KLAT, 2 * nb * groups).astype(np.float32)
    inverse = both.reshape(2, KLAT, 2, 2, groups // 2, batches * nb).transpose(3, 2, 5, 4, 0, 1)
    inverse = inverse.reshape(2, batches * nb * groups, 2 * KLAT).astype(np.float32)
    return jnp.asarray(forward, dtype=jnp.bfloat16), jnp.asarray(inverse, dtype=jnp.bfloat16)


def np_turn(groups):
    count = groups * PACK
    source = np.arange(count).reshape(groups, PACK).T.reshape(-1)
    turn = np.zeros((count, count), np.float32)
    turn[np.arange(count), source] = 1.0
    return jnp.asarray(turn, dtype=jnp.bfloat16)


def layer_kernel(
    points_sub,
    nb,
    counts,
    fields,
    gain_one,
    w_query,
    w_key,
    w_value,
    w_out,
    gain_two,
    table,
    sums,
    waves,
    forward,
    inverse,
    turn,
    spread,
    w_first,
    w_second,
    out,
    own,
    other,
    attended,
    sent,
    arrived,
    turned,
    rows_spec,
    second,
    far,
    normed,
    back_table,
    blocks,
    result,
    own_sem,
    swap_send,
    swap_recv,
    fwd_send,
    fwd_recv,
    far_send,
    far_recv,
    back_send,
    back_recv,
    out_sem,
):
    rows, groups, width, feat = sent.shape
    points = other.shape[1]
    held = width // 2
    packs = width // PACK
    batches = rows // nb
    sub = points_sub
    member = lax.axis_index("ens")
    me = lax.axis_index("grid")
    scale = 1.0 / math.sqrt(HEAD)
    partners = [me ^ o for o in range(groups - 1, 0, -1)]
    each = PACK // 2
    half = groups // 2
    quarter = groups // 4
    side_at = me // half
    far_side = 1 - side_at
    place_at = lax.rem(me, half)
    lane_at = lax.rem(me, quarter)
    inner = me // quarter == 1 + side_at
    relay = (1 + far_side) * quarter + lane_at
    slot_at = jnp.where(inner, 0, 1)
    relayed = packs - 1

    barrier = pltpu.get_barrier_semaphore()
    for t in partners:
        pl.semaphore_signal(barrier, inc=1, device_id={"grid": t}, device_id_type=MESH)
    pl.semaphore_signal(barrier, inc=1, device_id={"ens": 1 - member}, device_id_type=MESH)
    pl.semaphore_wait(barrier, groups)

    def swap(r):
        return pltpu.make_async_remote_copy(
            src_ref=fields.at[r],
            dst_ref=other.at[r],
            send_sem=swap_send.at[r],
            recv_sem=swap_recv.at[r],
            device_id={"ens": 1 - member},
            device_id_type=MESH,
        )

    def fetch(r, slot):
        return pltpu.make_async_copy(fields.at[r], own.at[slot], own_sem.at[slot])

    ahead = min(SWAP_AHEAD, rows)
    for r in range(ahead):
        swap(r).start()
    fetch(0, 0).start()

    eye = lax.broadcasted_iota(jnp.int32, (feat, feat), 0) // HEAD
    same = eye == lax.broadcasted_iota(jnp.int32, (feat, feat), 1) // HEAD
    for layer, weight in enumerate((w_first, w_second)):
        for part in range(2):
            wide = dot(weight[part], spread[...])
            blocks[2 * layer + part] = jnp.where(same, wide, 0.0).astype(jnp.bfloat16)
    back_table[...] = jnp.transpose(table[...])
    rows_spec[...] = jnp.zeros_like(rows_spec)

    def attend(r):
        slot = lax.rem(r, 2)
        fetch(r, slot).wait()

        @pl.when(r + 1 < rows)
        def _():
            fetch(r + 1, 1 - slot).start()

        swap(r).wait_recv()

        @pl.when(r + ahead < rows)
        def _():
            swap(r + ahead).start()

        for start in range(0, points, sub):
            span = pl.ds(start, sub)
            field = own[slot, span, :].astype(jnp.float32)
            norm = layer_norm(field, gain_one[...])
            queries = dot(norm, w_query[...]).astype(jnp.bfloat16).astype(jnp.float32)
            own_keys = dot(norm, w_key[...]).astype(jnp.bfloat16).astype(jnp.float32)
            own_values = dot(norm, w_value[...]).astype(jnp.bfloat16).astype(jnp.float32)
            side = layer_norm(other[r, span, :].astype(jnp.float32), gain_one[...])
            keys = dot(side, w_key[...]).astype(jnp.bfloat16).astype(jnp.float32)
            values = dot(side, w_value[...]).astype(jnp.bfloat16).astype(jnp.float32)
            terms = queries * (keys - own_keys)
            upper = terms.astype(jnp.bfloat16)
            lower = (terms - upper.astype(jnp.float32)).astype(jnp.bfloat16)
            shifted = (dot(upper, sums[...]) + dot(lower, sums[...])) * scale
            largest = jnp.maximum(shifted, 0.0)
            own_exp = jnp.exp(-largest)
            side_exp = jnp.exp(shifted - largest)
            mixed = own_exp.astype(jnp.bfloat16).astype(jnp.float32) * own_values
            mixed += side_exp.astype(jnp.bfloat16).astype(jnp.float32) * values
            mixed = (mixed / (own_exp + side_exp)).astype(jnp.bfloat16)
            done = (field + dot(mixed, w_out[...])).astype(jnp.bfloat16)
            attended[r, span, :] = done
            normed[span, :] = layer_norm(done.astype(jnp.float32), gain_two[...])
        spec = dot(table[...], normed[...])
        spec = jnp.where(waves[...] < counts[r], spec, 0.0).astype(jnp.bfloat16)
        sent[r] = spec.reshape(groups, width, feat)
        arrived[r, me] = sent[r, me]
        for t in partners:
            pltpu.make_async_remote_copy(
                src_ref=sent.at[r, t],
                dst_ref=arrived.at[r, me],
                send_sem=fwd_send.at[r],
                recv_sem=fwd_recv.at[r],
                device_id={"grid": t},
                device_id_type=MESH,
            ).start()

    def turn_in(r):
        whole = arrived.at[r, pl.ds(0, groups - 1)]
        pltpu.make_async_copy(whole, whole, fwd_recv.at[r]).wait()
        place = pl.ds(pl.multiple_of(lax.rem(r, nb) * groups, PACK), groups)
        for b in range(packs):
            block = arrived[r, :, b * PACK : (b + 1) * PACK, :].reshape(groups * PACK, feat)
            moved = dot(turn[...], block).astype(jnp.bfloat16)
            turned[b * PACK : (b + 1) * PACK, place, :] = moved.reshape(PACK, groups, feat)

    def lat_in(b, first, count):
        def step(i, _):
            k = first + i
            at = k // each * PACK + lax.rem(k, each)
            pair = jnp.concatenate([turned[at], turned[at + each]], axis=0)
            rows_spec[k] += dot(forward[b], pair)
            return 0

        lax.fori_loop(0, count, step, 0, unroll=4)

    def phase_in(i, _):
        @pl.when(i < rows)
        def _():
            attend(i)

        @pl.when(i >= ARRIVE_LAG)
        def _():
            turn_in(i - ARRIVE_LAG)

        b = (i - ARRIVE_LAG) // nb

        @pl.when((i >= ARRIVE_LAG) & (lax.rem(i - ARRIVE_LAG, nb) == nb - 1) & (b < batches - 1))
        def _():
            lat_in(b, 0, held)

        return 0

    lax.fori_loop(0, rows + ARRIVE_LAG, phase_in, 0)

    mode = second.shape[1] // 2

    def complex_mix(real, imag, layer):
        w_real, w_imag = blocks[2 * layer], blocks[2 * layer + 1]
        return dot(real, w_real) - dot(imag, w_imag), dot(real, w_imag) + dot(imag, w_real)

    def ship(p):
        span = pl.ds(p * each, each)
        return pltpu.make_async_remote_copy(
            src_ref=second.at[span],
            dst_ref=far.at[slot_at, span],
            send_sem=far_send.at[p],
            recv_sem=far_recv.at[slot_at * relayed + p],
            device_id={"grid": relay},
            device_id_type=MESH,
        )

    def mix(p, _):
        lat_in(batches - 1, p * each, each)
        span = pl.ds(p * each, each)
        real = rows_spec[span, :mode].reshape(each * mode, feat).astype(jnp.bfloat16)
        imag = rows_spec[span, mode:].reshape(each * mode, feat).astype(jnp.bfloat16)
        real, imag = complex_mix(real, imag, 0)
        real = jnp.maximum(real, 0.0).astype(jnp.bfloat16)
        imag = jnp.maximum(imag, 0.0).astype(jnp.bfloat16)
        real, imag = complex_mix(real, imag, 1)
        second[span, :mode] = real.astype(jnp.bfloat16).reshape(each, mode, feat)
        second[span, mode:] = imag.astype(jnp.bfloat16).reshape(each, mode, feat)

        @pl.when(p < relayed)
        def _():
            ship(p).start()

        return 0

    lax.fori_loop(0, packs, mix, 0)

    def wait_sent(r, _):
        whole = sent.at[r, pl.ds(0, groups - 1)]
        pltpu.make_async_copy(whole, whole, fwd_send.at[r]).wait()
        return 0

    lax.fori_loop(0, rows, wait_sent, 0)

    pair = PACK // half
    span_in = nb * groups
    span_out = rows * half

    def spread_rows(read, group, p, to_own, buffer, a, b, sem):
        to = side_at if to_own else far_side

        def lat(k, _):
            both = dot(inverse[to], read(k)).astype(jnp.bfloat16)
            for r in range(2):
                for c, start in enumerate(range(0, span_out, span_in)):
                    size = min(span_in, span_out - start)
                    at = r * span_out + start
                    turned[c * PACK + r * each + k, :size] = both[at : at + size]
            return 0

        lax.fori_loop(0, each, lat, 0, unroll=4)
        spot = pl.ds(pl.multiple_of(group * width + p * PACK, PACK), PACK)
        cut = pl.ds(pl.multiple_of(b * PACK, PACK), PACK)

        def send(i, _):
            per = span_in // PACK
            lead = pl.ds(i // per * PACK, PACK)
            block = turned[lead, pl.ds(pl.multiple_of(lax.rem(i, per) * PACK, PACK), PACK), :]
            moved = dot(turn[...], block.reshape(PACK * PACK, feat)).astype(jnp.bfloat16)
            span = pl.ds(i * pair, pair)
            buffer[span, pl.ds(a * half, half), cut, :] = moved.reshape(pair, half, PACK, feat)
            if to_own:
                other[span, spot, :] = buffer[span, a * half + place_at, cut, :]
            for o in range(half - 1, 0 if to_own else -1, -1):
                t = place_at ^ o
                pltpu.make_async_remote_copy(
                    src_ref=buffer.at[span, a * half + t, cut],
                    dst_ref=other.at[span, spot],
                    send_sem=sem,
                    recv_sem=back_recv.at[i],
                    device_id={"grid": to * half + t},
                    device_id_type=MESH,
                ).start()
            return 0

        lax.fori_loop(0, rows // pair, send, 0)

    def own_rows(p, _):
        spread_rows(lambda k: second[p * each + k], me, p, True, sent, 0, p, back_send.at[p])
        return 0

    lax.fori_loop(0, packs, own_rows, 0)
    last = packs - 1
    spread_rows(lambda k: second[last * each + k], me, last, False, sent, 1, last, back_send.at[packs])

    @pl.when(inner)
    def _():
        def relay_rows(q, _):
            p, u = q // 2, lax.rem(q, 2)
            group = (1 + far_side + u * (2 * far_side - 1)) * quarter + lane_at
            got = far.at[u, pl.ds(p * each, each)]
            pltpu.make_async_copy(got, got, far_recv.at[u * relayed + p]).wait()
            sem = back_send.at[packs + 1 + q]
            spread_rows(lambda k: far[u, p * each + k], group, p, True, arrived, u, p, sem)
            return 0

        lax.fori_loop(0, 2 * relayed, relay_rows, 0)

    def put(j, slot):
        return pltpu.make_async_copy(result.at[slot], out.at[j], out_sem.at[slot])

    def finish(j, slot, more):
        weight = jnp.where(waves[...] == 0, 1.0, 2.0)
        weight = jnp.where(waves[...] < counts[j], weight, 0.0)
        spec = (other[j].astype(jnp.float32) * weight).astype(jnp.bfloat16)
        total = attended[j].astype(jnp.float32) + dot(back_table[...], spec)

        @pl.when(more)
        def _():
            put(j, slot).wait()

        result[slot] = total.astype(jnp.bfloat16)
        put(j, slot).start()

    def phase_out(i, _):
        span = pl.ds(i * pair, pair)

        @pl.when(inner)
        def _():
            whole = other.at[span, pl.ds(0, (groups - 1) * width - 2 * relayed * PACK)]
            pltpu.make_async_copy(whole, whole, back_recv.at[i]).wait()

        @pl.when(jnp.logical_not(inner))
        def _():
            whole = other.at[span, pl.ds(0, (groups - 1) * width)]
            pltpu.make_async_copy(whole, whole, back_recv.at[i]).wait()

        for r in range(pair):
            finish(i * pair + r, r, i > 0)
        return 0

    lax.fori_loop(0, rows // pair, phase_out, 0)

    def drain(r, _):
        swap(r).wait_send()
        return 0

    lax.fori_loop(0, rows, drain, 0)
    for p in range(relayed):
        ship(p).wait_send()
    most = sent.at[:, pl.ds(0, half), pl.ds(0, PACK)]
    fewer = sent.at[:, pl.ds(0, half - 1), pl.ds(0, PACK)]
    for p in range(packs):
        pltpu.make_async_copy(fewer, fewer, back_send.at[p]).wait()
    pltpu.make_async_copy(most, most, back_send.at[packs]).wait()

    @pl.when(inner)
    def _():
        for q in range(2 * relayed):
            pltpu.make_async_copy(fewer, fewer, back_send.at[packs + 1 + q]).wait()

    for r in range(pair):
        put(rows - pair + r, r).wait()


def fused(mesh_sizes, fields, mode_counts, gain_attn, w_query, w_key, w_value, w_out, gain_spec, w_first, w_second):
    _, groups = mesh_sizes
    fields = fields[0]
    rows, points, feat = fields.shape
    width = 2 * KLON // groups
    held = width // 2
    nb = max(n for n in range(1, rows + 1) if rows % n == 0 and 2 * n * groups <= max(feat, 2 * groups))
    forward, inverse = np_lat_tables(groups, rows // nb, nb)
    turn = np_turn(groups)
    block = w_first.shape[-1]
    lanes = np.arange(feat)
    heads = jnp.asarray((lanes[:, None] // HEAD == lanes[None, :] // HEAD).astype(np.float32), dtype=jnp.bfloat16)
    spread = jnp.asarray((np.arange(block)[:, None] == lanes[None, :] % block).astype(np.float32), dtype=jnp.bfloat16)
    waves = jnp.asarray(np_wave_order(groups)[1][:, None], dtype=jnp.int32)
    operands = [
        mode_counts, fields, gain_attn[None, :], w_query, w_key, w_value, w_out, gain_spec[None, :],
        np_lon_forward(points, groups), heads, waves, forward, inverse, turn, spread,
        w_first.reshape(2, feat, block), w_second.reshape(2, feat, block),
    ]
    vmem = pl.BlockSpec(memory_space=pltpu.VMEM)
    hbm = pl.BlockSpec(memory_space=pl.ANY)
    specs = [pl.BlockSpec(memory_space=pltpu.SMEM), hbm] + [vmem] * (len(operands) - 2)
    half = jnp.bfloat16
    dma = pltpu.SemaphoreType.DMA
    out = pl.pallas_call(
        functools.partial(layer_kernel, points // 3 if points % 48 == 0 else points, nb),
        in_specs=specs,
        out_specs=hbm,
        out_shape=jax.ShapeDtypeStruct((rows, points, feat), half),
        scratch_shapes=[
            pltpu.VMEM((2, points, feat), half),
            pltpu.VMEM((rows, points, feat), half),
            pltpu.VMEM((rows, points, feat), half),
            pltpu.VMEM((rows, groups, width, feat), half),
            pltpu.VMEM((rows, groups, width, feat), half),
            pltpu.VMEM((width, nb * groups, feat), half),
            pltpu.VMEM((held, 2 * KLAT, feat), jnp.float32),
            pltpu.VMEM((held, 2 * KLAT, feat), half),
            pltpu.VMEM((2, held - PACK // 2, 2 * KLAT, feat), half),
            pltpu.VMEM((points, feat), half),
            pltpu.VMEM((points, 2 * KLON), half),
            pltpu.VMEM((4, feat, feat), half),
            pltpu.VMEM((2, points, feat), half),
            dma((2,)),
            dma((rows,)),
            dma((rows,)),
            dma((rows,)),
            dma((rows,)),
            dma((width // PACK - 1,)),
            dma((2 * (width // PACK - 1),)),
            dma((3 * (width // PACK),)),
            dma((rows // 2,)),
            dma((2,)),
        ],
        compiler_params=pltpu.CompilerParams(
            collective_id=0, has_side_effects=True, vmem_limit_bytes=67043328
        ),
        name="layer",
    )(*operands)
    return out[None]


def streams(members, groups, lat_dev, points, feat):
    width = 2 * KLON // groups
    return (
        members == 2
        and groups == PACK
        and (2 * KLON) % (groups * PACK) == 0
        and points == 2 * KLON
        and feat % 128 == 0
        and lat_dev % 2 == 0
        and width % PACK == 0
        and width > PACK
    )


def layer(mesh_sizes, *args):
    if streams(*mesh_sizes, *args[0].shape[1:]):
        return fused(mesh_sizes, *args)
    return shards(mesh_sizes, *args)


def solution(mesh):
    in_specs = (P("ens", "grid", None, None), P("grid"), P(), P(), P(), P(), P(), P(), P(), P())
    out_specs = P("ens", "grid", None, None)
    sizes = (mesh.shape["ens"], mesh.shape["grid"])
    return jax.shard_map(
        functools.partial(layer, sizes),
        mesh=mesh,
        in_specs=in_specs,
        out_specs=out_specs,
        check_vma=False,
    )
```

```python
import functools
import math

import jax
import jax.numpy as jnp
import numpy as np
from jax import lax
from jax.experimental import pallas as pl
from jax.experimental.pallas import tpu as pltpu
from jax.sharding import PartitionSpec as P

HEAD = 32
NLAT = 384
KLON = 384
KLAT = 128
CHUNKS = 6
BACK_CHUNKS = 2

MESH = pl.DeviceIdType.MESH
SWAP_AHEAD = 6
ARRIVE_LAG = 3
PACK = 16

norm_eps = 1e-05


def layer_norm(widened, gain_vec):
    center = widened - jnp.mean(widened, axis=-1, keepdims=True)
    spread = jnp.mean(center * center, axis=-1, keepdims=True)
    return (center * lax.rsqrt(spread + norm_eps) * gain_vec).astype(jnp.bfloat16)


def wave_order(groups):
    held = KLON // groups
    place = jnp.arange(2 * KLON, dtype=jnp.int32)
    part = place // held % 2
    wave = place // (2 * held) * held + place % held
    return part, wave


def lon_forward(points, groups):
    part, wave = wave_order(groups)
    positions = jnp.arange(points, dtype=jnp.int32)
    turn_count = wave[:, None] * positions[None, :] % points
    angles = 2.0 * math.pi / points * turn_count.astype(jnp.float32)
    factor = 1.0 / math.sqrt(points)
    return jnp.where(
        part[:, None] == 0, jnp.cos(angles) * factor, -jnp.sin(angles) * factor
    ).astype(jnp.bfloat16)


def lon_inverse(points, groups):
    part, wave = wave_order(groups)
    positions = jnp.arange(points, dtype=jnp.int32)
    turn_count = positions[:, None] * wave[None, :] % points
    angles = 2.0 * math.pi / points * turn_count.astype(jnp.float32)
    weight = jnp.where(wave == 0, 1.0, 2.0).astype(jnp.float32)[None, :] / math.sqrt(points)
    return jnp.where(
        part[None, :] == 0, jnp.cos(angles) * weight, -jnp.sin(angles) * weight
    ).astype(jnp.bfloat16)


def lat_angles(row_count, mode_count):
    frequency = jnp.arange(mode_count, dtype=jnp.int32)
    frequency = jnp.where(frequency < mode_count // 2, frequency, frequency - mode_count)
    positions = jnp.arange(row_count, dtype=jnp.int32)
    turn_count = frequency[:, None] * positions[None, :] % row_count
    return 2.0 * math.pi / row_count * turn_count.astype(jnp.float32)


def lat_forward(row_count, mode_count):
    angles = lat_angles(row_count, mode_count)
    factor = 1.0 / math.sqrt(row_count)
    cosine = jnp.cos(angles) * factor
    sine_part = jnp.sin(angles) * factor
    return jnp.stack(
        [jnp.stack([cosine, sine_part], axis=1), jnp.stack([-sine_part, cosine], axis=1)]
    ).astype(jnp.bfloat16)


def lat_inverse(row_count, mode_count):
    angles = jnp.transpose(lat_angles(row_count, mode_count))
    factor = 1.0 / math.sqrt(row_count)
    cosine = jnp.cos(angles) * factor
    sine_part = jnp.sin(angles) * factor
    return jnp.stack([jnp.stack([cosine, -sine_part]), jnp.stack([sine_part, cosine])]).astype(
        jnp.bfloat16
    )


def complex_blocks(weight):
    real_part = weight[0]
    imag_part = weight[1]
    return jnp.stack([jnp.stack([real_part, imag_part]), jnp.stack([-imag_part, real_part])])


def mix_blocks(spec, big):
    blocks = spec.reshape(spec.shape[:3] + (big.shape[2], big.shape[3]))
    out_blocks = jnp.einsum("pqkbi,psbio->sqkbo", blocks, big, preferred_element_type=jnp.float32)
    return out_blocks.reshape(spec.shape)


def dot(left, right):
    return jnp.dot(left, right, preferred_element_type=jnp.float32)


def attend_kernel(others, first_row, sub, counts, own, *refs):
    other_refs = refs[:others]
    (gain_one, w_qkv, w_out, gain_two, table, sums, waves, attended, spectrum, normed) = refs[others:]
    points, feat = own.shape[1:]
    scale = 1.0 / math.sqrt(HEAD)
    for start in range(0, points, sub):
        rows = pl.ds(start, sub)
        fields = own[0, rows, :].astype(jnp.float32)
        joined = dot(layer_norm(fields, gain_one[...]), w_qkv[...]).astype(jnp.bfloat16)
        queries = joined[:, :feat].astype(jnp.float32)
        own_keys = joined[:, feat : 2 * feat].astype(jnp.float32)
        values = [joined[:, 2 * feat :].astype(jnp.float32)]
        shifted = [jnp.zeros((sub, feat), jnp.float32)]
        for ref in other_refs:
            side = layer_norm(ref[0, rows, :].astype(jnp.float32), gain_one[...])
            pair = dot(side, w_qkv[:, feat:]).astype(jnp.bfloat16)
            terms = queries * (pair[:, :feat].astype(jnp.float32) - own_keys)
            upper = terms.astype(jnp.bfloat16)
            lower = (terms - upper.astype(jnp.float32)).astype(jnp.bfloat16)
            total = dot(upper, sums[...]) + dot(lower, sums[...])
            shifted.append(total * scale)
            values.append(pair[:, feat:].astype(jnp.float32))
        largest = functools.reduce(jnp.maximum, shifted)
        exps = [jnp.exp(item - largest) for item in shifted]
        totals = functools.reduce(jnp.add, exps)
        mixed = functools.reduce(
            jnp.add,
            [e.astype(jnp.bfloat16).astype(jnp.float32) * v for e, v in zip(exps, values)],
        )
        mixed = (mixed / totals).astype(jnp.bfloat16)
        result = (fields + dot(mixed, w_out[...])).astype(jnp.bfloat16)
        attended[0, rows, :] = result
        normed[rows, :] = layer_norm(result.astype(jnp.float32), gain_two[...])
    kept = waves[...] < counts[first_row + pl.program_id(0)]
    spec = dot(table[...], normed[...])
    spec = jnp.where(kept, spec, 0.0).astype(jnp.bfloat16)
    if len(spectrum.shape) == 4:
        spectrum[:, 0] = spec.reshape(spectrum.shape[0], spectrum.shape[2], feat)
    else:
        spectrum[0] = spec


def attend(chunk, rows, aligned, groups, fields, others, counts, gains, weights, tables):
    points, feat = fields.shape[1:]
    first_row = chunk * rows
    sub = points // 3 if points % 48 == 0 else points
    whole = lambda a: pl.BlockSpec(a.shape, lambda i, c: (0,) * a.ndim)
    w_qkv, w_out = weights
    table, sums, waves = tables
    held = 2 * KLON // groups
    if aligned:
        spec_shape = (groups, rows, held, feat)
        spec_block = pl.BlockSpec((groups, 1, held, feat), lambda i, c: (0, i, 0, 0))
    else:
        spec_shape = (rows, 2 * KLON, feat)
        spec_block = pl.BlockSpec((1, 2 * KLON, feat), lambda i, c: (i, 0, 0))
    row_block = pl.BlockSpec((1, points, feat), lambda i, c: (i, 0, 0))
    own_block = pl.BlockSpec((1, points, feat), lambda i, c: (first_row + i, 0, 0))
    params = (gains[0], w_qkv, w_out, gains[1], table, sums, waves)
    flops = 2 * rows * points * feat * (feat * 8 + 2 * KLON)
    attended, spectrum = pl.pallas_call(
        functools.partial(attend_kernel, len(others), first_row, sub),
        grid_spec=pltpu.PrefetchScalarGridSpec(
            num_scalar_prefetch=1,
            grid=(rows,),
            in_specs=[own_block] + [row_block] * len(others) + [whole(p) for p in params],
            out_specs=[row_block, spec_block],
            scratch_shapes=[pltpu.VMEM((points, feat), jnp.bfloat16)],
        ),
        out_shape=[
            jax.ShapeDtypeStruct((rows, points, feat), jnp.bfloat16),
            jax.ShapeDtypeStruct(spec_shape, jnp.bfloat16),
        ],
        cost_estimate=pl.CostEstimate(
            flops=flops, bytes_accessed=rows * points * feat * 8, transcendentals=rows * points * feat * 2
        ),
        compiler_params=pltpu.CompilerParams(vmem_limit_bytes=40 * 1024 * 1024),
    )(counts, fields, *others, *params)
    if not aligned:
        spectrum = jnp.transpose(spectrum.reshape(rows, groups, held, feat), (1, 0, 2, 3))
    return attended, spectrum


def finish_kernel(first_row, counts, spectrum, attended, table, waves, *refs):
    out = refs[-1]
    feat = out.shape[-1]
    kept = waves[...] < counts[first_row + pl.program_id(0)]
    if len(spectrum.shape) == 4:
        spec = spectrum[:, 0].reshape(2 * KLON, feat)
    else:
        spec = spectrum[0]
    spec = jnp.where(kept, spec.astype(jnp.float32), 0.0).astype(jnp.bfloat16)
    out[0] = (attended[0].astype(jnp.float32) + dot(table[...], spec)).astype(jnp.bfloat16)


def finish(first_row, offset, lat_dev, aligned, groups, spectrum, attended, counts, table, waves, so_far):
    rows, points, feat = attended.shape
    held = 2 * KLON // groups
    whole = lambda a: pl.BlockSpec(a.shape, lambda i, c: (0,) * a.ndim)
    if aligned:
        spec_block = pl.BlockSpec((groups, 1, held, feat), lambda i, c: (0, offset + i, 0, 0))
    else:
        spectrum = jnp.transpose(spectrum, (1, 0, 2, 3)).reshape(-1, 2 * KLON, feat)
        spec_block = pl.BlockSpec((1, 2 * KLON, feat), lambda i, c: (offset + i, 0, 0))
    row_block = pl.BlockSpec((1, points, feat), lambda i, c: (i, 0, 0))
    out_block = pl.BlockSpec((1, points, feat), lambda i, c: (first_row + i, 0, 0))
    operands = [counts, spectrum, attended, table, waves]
    specs = [spec_block, row_block, whole(table), whole(waves)]
    aliases = {}
    if so_far is not None:
        aliases = {len(operands): 0}
        operands.append(so_far)
        specs.append(pl.BlockSpec(memory_space=pl.ANY))
    return pl.pallas_call(
        functools.partial(finish_kernel, first_row),
        grid_spec=pltpu.PrefetchScalarGridSpec(
            num_scalar_prefetch=1, grid=(rows,), in_specs=specs, out_specs=out_block
        ),
        out_shape=jax.ShapeDtypeStruct((lat_dev, points, feat), jnp.bfloat16),
        input_output_aliases=aliases,
        cost_estimate=pl.CostEstimate(
            flops=4 * rows * points * feat * KLON,
            bytes_accessed=rows * points * feat * 6,
            transcendentals=0,
        ),
        compiler_params=pltpu.CompilerParams(vmem_limit_bytes=40 * 1024 * 1024),
    )(*operands)


def shards(
    mesh_sizes, fields, mode_counts, gain_attn, w_query, w_key, w_value, w_out, gain_spec, w_first, w_second
):
    members, groups = mesh_sizes
    fields = fields[0]
    lat_dev, points, feat = fields.shape
    held = KLON // groups
    aligned = (2 * held) % 16 == 0
    chunks = max(c for c in range(1, CHUNKS + 1) if lat_dev % c == 0)
    rows = lat_dev // chunks
    shifts = [
        [(i, (i + s) % members) for i in range(members)] for s in range(1, members)
    ]
    others = []
    for c in range(chunks):
        others.append([lax.ppermute(fields[c * rows : (c + 1) * rows], "ens", s) for s in shifts])
    w_qkv = jnp.concatenate([w_query, w_key, w_value], axis=1)
    lanes = jnp.arange(feat, dtype=jnp.int32) // HEAD
    sums = (lanes[:, None] == lanes[None, :]).astype(jnp.bfloat16)
    waves = wave_order(groups)[1][:, None]
    gains = (gain_attn[None, :], gain_spec[None, :])
    tables = (lon_forward(points, groups), sums, waves)
    back_table = lon_inverse(points, groups)
    forward = lat_forward(NLAT, KLAT).reshape(2, KLAT, 2, groups, chunks, rows)
    backs = max(c for c in range(1, BACK_CHUNKS + 1) if chunks % c == 0)
    per_back = chunks // backs
    inverse = lat_inverse(NLAT, KLAT).reshape(2, 2, groups, backs, per_back * rows, KLAT)
    big_one = complex_blocks(w_first)
    big_two = complex_blocks(w_second)
    kept_fields = []
    rows_spec = None
    for c in range(chunks):
        attended, spectrum = attend(
            c, rows, aligned, groups, fields, others[c], mode_counts, gains, (w_qkv, w_out), tables
        )
        kept_fields.append(attended)
        arrived = lax.all_to_all(spectrum, "grid", split_axis=0, concat_axis=0)
        arrived = arrived.reshape(groups, rows, 2, held, feat)
        term = jnp.einsum(
            "pqrgj,gjrkd->pqkd",
            forward[:, :, :, :, c],
            arrived,
            preferred_element_type=jnp.float32,
        )
        rows_spec = term if rows_spec is None else rows_spec + term
        if c < chunks - 1:
            rows_spec = lax.optimization_barrier(rows_spec)
    rows_spec = rows_spec.astype(jnp.bfloat16)
    hidden = jnp.maximum(mix_blocks(rows_spec, big_one), 0.0).astype(jnp.bfloat16)
    second = mix_blocks(hidden, big_two).astype(jnp.bfloat16)
    out = None
    for b in range(backs):
        back_rows = jnp.einsum(
            "rpgjq,pqkd->gjrkd", inverse[:, :, :, b], second, preferred_element_type=jnp.float32
        ).astype(jnp.bfloat16)
        returned = lax.all_to_all(
            back_rows.reshape(groups, per_back * rows, 2 * held, feat), "grid", split_axis=0, concat_axis=0
        )
        for i in range(per_back):
            c = b * per_back + i
            out = finish(
                c * rows, i * rows, lat_dev, aligned, groups, returned, kept_fields[c], mode_counts,
                back_table, tables[2], out,
            )
    return out[None]


def np_wave_order(groups):
    held = KLON // groups
    each = PACK // 2
    place = np.arange(2 * KLON)
    group, pack, within = place // (2 * held), place % (2 * held) // PACK, place % each
    return place // each % 2, group * held + pack * each + within


def np_lon_forward(points, groups):
    part, wave = np_wave_order(groups)
    turns = wave[:, None] * np.arange(points)[None, :] % points
    angles = 2.0 * math.pi / points * turns
    rows = np.where(part[:, None] == 0, np.cos(angles), -np.sin(angles)) / math.sqrt(points)
    return jnp.asarray(rows.astype(np.float32), dtype=jnp.bfloat16)


def np_lat_tables(groups, batches, nb):
    frequency = np.arange(KLAT)
    frequency = np.where(frequency < KLAT // 2, frequency, frequency - KLAT)
    angles = 2.0 * math.pi / NLAT * (frequency[:, None] * np.arange(NLAT)[None, :] % NLAT)
    cosine = np.cos(angles) / math.sqrt(NLAT)
    sine = np.sin(angles) / math.sqrt(NLAT)
    both = np.stack([np.stack([cosine, sine], axis=1), np.stack([-sine, cosine], axis=1)])
    forward = both.reshape(2, KLAT, 2, groups, batches, nb).transpose(4, 0, 1, 2, 5, 3)
    forward = forward.reshape(batches, 2 * KLAT, 2 * nb * groups).astype(np.float32)
    inverse = both.reshape(2, KLAT, 2, 2, groups // 2, batches * nb).transpose(3, 2, 5, 4, 0, 1)
    inverse = inverse.reshape(2, batches * nb * groups, 2 * KLAT).astype(np.float32)
    return jnp.asarray(forward, dtype=jnp.bfloat16), jnp.asarray(inverse, dtype=jnp.bfloat16)


def np_turn(groups):
    count = groups * PACK
    source = np.arange(count).reshape(groups, PACK).T.reshape(-1)
    turn = np.zeros((count, count), np.float32)
    turn[np.arange(count), source] = 1.0
    return jnp.asarray(turn, dtype=jnp.bfloat16)


def enter_kernel(points_sub, nb, held_count, counts, fields, *refs):
    sources, out, held_refs = refs[:held_count], refs[held_count], refs[held_count + 1 : 2 * held_count + 1]
    rest, sems = refs[2 * held_count + 1 : -1], refs[-1]
    copies = [
        pltpu.make_async_copy(source, target, sems.at[i])
        for i, (source, target) in enumerate(zip(sources, held_refs))
    ]
    for copy in copies:
        copy.start()
    layer_kernel(points_sub, nb, copies, counts, fields, *held_refs, out, *rest)


def layer_kernel(
    points_sub,
    nb,
    copies,
    counts,
    fields,
    gain_one,
    w_query,
    w_key,
    w_value,
    w_out,
    gain_two,
    table,
    sums,
    waves,
    forward,
    inverse,
    turn,
    spread,
    w_first,
    w_second,
    out,
    own,
    other,
    attended,
    sent,
    arrived,
    turned,
    rows_spec,
    second,
    far,
    normed,
    back_table,
    blocks,
    result,
    own_sem,
    swap_send,
    swap_recv,
    fwd_send,
    fwd_recv,
    far_send,
    far_recv,
    back_send,
    back_recv,
    out_sem,
):
    rows, groups, width, feat = sent.shape
    points = other.shape[1]
    held = width // 2
    packs = width // PACK
    batches = rows // nb
    sub = points_sub
    member = lax.axis_index("ens")
    me = lax.axis_index("grid")
    scale = 1.0 / math.sqrt(HEAD)
    partners = [me ^ o for o in range(groups - 1, 0, -1)]
    each = PACK // 2
    half = groups // 2
    quarter = groups // 4
    side_at = me // half
    far_side = 1 - side_at
    place_at = lax.rem(me, half)
    lane_at = lax.rem(me, quarter)
    inner = me // quarter == 1 + side_at
    relay = (1 + far_side) * quarter + lane_at
    slot_at = jnp.where(inner, 0, 1)
    relayed = packs - 1

    barrier = pltpu.get_barrier_semaphore()
    for t in partners:
        pl.semaphore_signal(barrier, inc=1, device_id={"grid": t}, device_id_type=MESH)
    pl.semaphore_signal(barrier, inc=1, device_id={"ens": 1 - member}, device_id_type=MESH)
    pl.semaphore_wait(barrier, groups)

    thirds = points // sub

    def swap(r, s):
        span = pl.ds(s * sub, sub)
        return pltpu.make_async_remote_copy(
            src_ref=fields.at[r, span],
            dst_ref=other.at[r, span],
            send_sem=swap_send.at[r],
            recv_sem=swap_recv.at[r * thirds + s],
            device_id={"ens": 1 - member},
            device_id_type=MESH,
        )

    def fetch(r, slot):
        return pltpu.make_async_copy(fields.at[r], own.at[slot], own_sem.at[slot])

    ahead = min(SWAP_AHEAD, rows)
    for r in range(ahead):
        for s in range(thirds):
            swap(r, s).start()
    fetch(0, 0).start()
    for copy in copies:
        copy.wait()

    eye = lax.broadcasted_iota(jnp.int32, (feat, feat), 0) // HEAD
    same = eye == lax.broadcasted_iota(jnp.int32, (feat, feat), 1) // HEAD
    for layer, weight in enumerate((w_first, w_second)):
        for part in range(2):
            wide = dot(weight[part], spread[...])
            blocks[2 * layer + part] = jnp.where(same, wide, 0.0).astype(jnp.bfloat16)
    back_table[...] = jnp.transpose(table[...])
    rows_spec[...] = jnp.zeros_like(rows_spec)

    def attend(r):
        slot = lax.rem(r, 2)
        fetch(r, slot).wait()

        @pl.when(r + 1 < rows)
        def _():
            fetch(r + 1, 1 - slot).start()

        @pl.when(r + ahead < rows)
        def _():
            for s in range(thirds):
                swap(r + ahead, s).start()

        for s in range(thirds):
            swap(r, s).wait_recv()
            span = pl.ds(s * sub, sub)
            field = own[slot, span, :].astype(jnp.float32)
            norm = layer_norm(field, gain_one[...])
            queries = dot(norm, w_query[...]).astype(jnp.bfloat16).astype(jnp.float32)
            own_keys = dot(norm, w_key[...]).astype(jnp.bfloat16).astype(jnp.float32)
            own_values = dot(norm, w_value[...]).astype(jnp.bfloat16).astype(jnp.float32)
            side = layer_norm(other[r, span, :].astype(jnp.float32), gain_one[...])
            keys = dot(side, w_key[...]).astype(jnp.bfloat16).astype(jnp.float32)
            values = dot(side, w_value[...]).astype(jnp.bfloat16).astype(jnp.float32)
            terms = queries * (keys - own_keys)
            upper = terms.astype(jnp.bfloat16)
            lower = (terms - upper.astype(jnp.float32)).astype(jnp.bfloat16)
            shifted = (dot(upper, sums[...]) + dot(lower, sums[...])) * scale
            largest = jnp.maximum(shifted, 0.0)
            own_exp = jnp.exp(-largest)
            side_exp = jnp.exp(shifted - largest)
            mixed = own_exp.astype(jnp.bfloat16).astype(jnp.float32) * own_values
            mixed += side_exp.astype(jnp.bfloat16).astype(jnp.float32) * values
            mixed = (mixed / (own_exp + side_exp)).astype(jnp.bfloat16)
            done = (field + dot(mixed, w_out[...])).astype(jnp.bfloat16)
            attended[r, span, :] = done
            normed[span, :] = layer_norm(done.astype(jnp.float32), gain_two[...])
        spec = dot(table[...], normed[...])
        spec = jnp.where(waves[...] < counts[r], spec, 0.0).astype(jnp.bfloat16)
        sent[r] = spec.reshape(groups, width, feat)
        arrived[r, me] = sent[r, me]
        for t in partners:
            pltpu.make_async_remote_copy(
                src_ref=sent.at[r, t],
                dst_ref=arrived.at[r, me],
                send_sem=fwd_send.at[r],
                recv_sem=fwd_recv.at[r],
                device_id={"grid": t},
                device_id_type=MESH,
            ).start()

    def turn_in(r):
        whole = arrived.at[r, pl.ds(0, groups - 1)]
        pltpu.make_async_copy(whole, whole, fwd_recv.at[r]).wait()
        place = pl.ds(pl.multiple_of(lax.rem(r, nb) * groups, PACK), groups)
        for b in range(packs):
            block = arrived[r, :, b * PACK : (b + 1) * PACK, :].reshape(groups * PACK, feat)
            moved = dot(turn[...], block).astype(jnp.bfloat16)
            turned[b * PACK : (b + 1) * PACK, place, :] = moved.reshape(PACK, groups, feat)

    def lat_in(b, first, count):
        def step(i, _):
            k = first + i
            at = k // each * PACK + lax.rem(k, each)
            pair = jnp.concatenate([turned[at], turned[at + each]], axis=0)
            rows_spec[k] += dot(forward[b], pair)
            return 0

        lax.fori_loop(0, count, step, 0, unroll=4)

    def phase_in(i, _):
        @pl.when(i < rows)
        def _():
            attend(i)

        @pl.when(i >= ARRIVE_LAG)
        def _():
            turn_in(i - ARRIVE_LAG)

        b = (i - ARRIVE_LAG) // nb

        @pl.when((i >= ARRIVE_LAG) & (lax.rem(i - ARRIVE_LAG, nb) == nb - 1) & (b < batches - 1))
        def _():
            lat_in(b, 0, held)

        return 0

    lax.fori_loop(0, rows + ARRIVE_LAG, phase_in, 0)

    mode = second.shape[1] // 2

    def complex_mix(real, imag, layer):
        w_real, w_imag = blocks[2 * layer], blocks[2 * layer + 1]
        return dot(real, w_real) - dot(imag, w_imag), dot(real, w_imag) + dot(imag, w_real)

    def ship(p):
        span = pl.ds(p * each, each)
        return pltpu.make_async_remote_copy(
            src_ref=second.at[span],
            dst_ref=far.at[slot_at, span],
            send_sem=far_send.at[p],
            recv_sem=far_recv.at[slot_at * relayed + p],
            device_id={"grid": relay},
            device_id_type=MESH,
        )

    def mix(p, _):
        lat_in(batches - 1, p * each, each)
        span = pl.ds(p * each, each)
        real = rows_spec[span, :mode].reshape(each * mode, feat).astype(jnp.bfloat16)
        imag = rows_spec[span, mode:].reshape(each * mode, feat).astype(jnp.bfloat16)
        real, imag = complex_mix(real, imag, 0)
        real = jnp.maximum(real, 0.0).astype(jnp.bfloat16)
        imag = jnp.maximum(imag, 0.0).astype(jnp.bfloat16)
        real, imag = complex_mix(real, imag, 1)
        second[span, :mode] = real.astype(jnp.bfloat16).reshape(each, mode, feat)
        second[span, mode:] = imag.astype(jnp.bfloat16).reshape(each, mode, feat)

        @pl.when(inner & (p < relayed))
        def _():
            ship(p).start()

        return 0

    lax.fori_loop(0, packs, mix, 0)

    def wait_sent(r, _):
        whole = sent.at[r, pl.ds(0, groups - 1)]
        pltpu.make_async_copy(whole, whole, fwd_send.at[r]).wait()
        return 0

    lax.fori_loop(0, rows, wait_sent, 0)

    pair = PACK // half
    span_in = nb * groups
    span_out = rows * half

    def spread_rows(read, group, p, to_own, buffer, a, b, sem):
        to = side_at if to_own else far_side

        def lat(k, _):
            both = dot(inverse[to], read(k)).astype(jnp.bfloat16)
            for r in range(2):
                for c, start in enumerate(range(0, span_out, span_in)):
                    size = min(span_in, span_out - start)
                    at = r * span_out + start
                    turned[c * PACK + r * each + k, :size] = both[at : at + size]
            return 0

        lax.fori_loop(0, each, lat, 0, unroll=4)
        spot = pl.ds(pl.multiple_of(group * width + p * PACK, PACK), PACK)
        cut = pl.ds(pl.multiple_of(b * PACK, PACK), PACK)

        def send(i, _):
            per = span_in // PACK
            lead = pl.ds(i // per * PACK, PACK)
            block = turned[lead, pl.ds(pl.multiple_of(lax.rem(i, per) * PACK, PACK), PACK), :]
            moved = dot(turn[...], block.reshape(PACK * PACK, feat)).astype(jnp.bfloat16)
            span = pl.ds(i * pair, pair)
            buffer[span, pl.ds(a * half, half), cut, :] = moved.reshape(pair, half, PACK, feat)
            if to_own:
                other[span, spot, :] = buffer[span, a * half + place_at, cut, :]
            for o in range(half - 1, 0 if to_own else -1, -1):
                t = place_at ^ o
                pltpu.make_async_remote_copy(
                    src_ref=buffer.at[span, a * half + t, cut],
                    dst_ref=other.at[span, spot],
                    send_sem=sem,
                    recv_sem=back_recv.at[i],
                    device_id={"grid": to * half + t},
                    device_id_type=MESH,
                ).start()
            return 0

        lax.fori_loop(0, rows // pair, send, 0)

    def own_rows(p, _):
        spread_rows(lambda k: second[p * each + k], me, p, True, sent, 0, p, back_send.at[p])
        return 0

    lax.fori_loop(0, packs, own_rows, 0)

    @pl.when(jnp.logical_not(inner))
    def _():
        for p in range(relayed):
            ship(p).start()

    last = packs - 1
    spread_rows(lambda k: second[last * each + k], me, last, False, sent, 1, last, back_send.at[packs])

    @pl.when(inner)
    def _():
        def relay_rows(q, _):
            p, u = q // 2, lax.rem(q, 2)
            group = (1 + far_side + u * (2 * far_side - 1)) * quarter + lane_at
            got = far.at[u, pl.ds(p * each, each)]
            pltpu.make_async_copy(got, got, far_recv.at[u * relayed + p]).wait()
            sem = back_send.at[packs + 1 + q]
            spread_rows(lambda k: far[u, p * each + k], group, p, True, arrived, u, p, sem)
            return 0

        lax.fori_loop(0, 2 * relayed, relay_rows, 0)

    def put(j, slot):
        return pltpu.make_async_copy(result.at[slot], out.at[j], out_sem.at[slot])

    def finish(j, slot, more):
        weight = jnp.where(waves[...] == 0, 1.0, 2.0)
        weight = jnp.where(waves[...] < counts[j], weight, 0.0)
        spec = (other[j].astype(jnp.float32) * weight).astype(jnp.bfloat16)
        total = attended[j].astype(jnp.float32) + dot(back_table[...], spec)

        @pl.when(more)
        def _():
            put(j, slot).wait()

        result[slot] = total.astype(jnp.bfloat16)
        put(j, slot).start()

    def phase_out(i, _):
        span = pl.ds(i * pair, pair)

        @pl.when(inner)
        def _():
            whole = other.at[span, pl.ds(0, (groups - 1) * width - 2 * relayed * PACK)]
            pltpu.make_async_copy(whole, whole, back_recv.at[i]).wait()

        @pl.when(jnp.logical_not(inner))
        def _():
            whole = other.at[span, pl.ds(0, (groups - 1) * width)]
            pltpu.make_async_copy(whole, whole, back_recv.at[i]).wait()

        for r in range(pair):
            finish(i * pair + r, r, i > 0)
        return 0

    lax.fori_loop(0, rows // pair, phase_out, 0)

    def drain(r, _):
        pltpu.make_async_copy(fields.at[r], fields.at[r], swap_send.at[r]).wait()
        return 0

    lax.fori_loop(0, rows, drain, 0)
    for p in range(relayed):
        ship(p).wait_send()
    most = sent.at[:, pl.ds(0, half), pl.ds(0, PACK)]
    fewer = sent.at[:, pl.ds(0, half - 1), pl.ds(0, PACK)]
    for p in range(packs):
        pltpu.make_async_copy(fewer, fewer, back_send.at[p]).wait()
    pltpu.make_async_copy(most, most, back_send.at[packs]).wait()

    @pl.when(inner)
    def _():
        for q in range(2 * relayed):
            pltpu.make_async_copy(fewer, fewer, back_send.at[packs + 1 + q]).wait()

    for r in range(pair):
        put(rows - pair + r, r).wait()


def fused(mesh_sizes, fields, mode_counts, gain_attn, w_query, w_key, w_value, w_out, gain_spec, w_first, w_second):
    _, groups = mesh_sizes
    fields = fields[0]
    rows, points, feat = fields.shape
    width = 2 * KLON // groups
    held = width // 2
    nb = max(n for n in range(1, rows + 1) if rows % n == 0 and 2 * n * groups <= max(feat, 2 * groups))
    forward, inverse = np_lat_tables(groups, rows // nb, nb)
    turn = np_turn(groups)
    block = w_first.shape[-1]
    lanes = np.arange(feat)
    heads = jnp.asarray((lanes[:, None] // HEAD == lanes[None, :] // HEAD).astype(np.float32), dtype=jnp.bfloat16)
    spread = jnp.asarray((np.arange(block)[:, None] == lanes[None, :] % block).astype(np.float32), dtype=jnp.bfloat16)
    waves = jnp.asarray(np_wave_order(groups)[1][:, None], dtype=jnp.int32)
    operands = [
        mode_counts, fields, gain_attn[None, :], w_query, w_key, w_value, w_out, gain_spec[None, :],
        np_lon_forward(points, groups), heads, waves, forward, inverse, turn, spread,
        w_first.reshape(2, feat, block), w_second.reshape(2, feat, block),
    ]
    hbm = pl.BlockSpec(memory_space=pl.ANY)
    specs = [pl.BlockSpec(memory_space=pltpu.SMEM)] + [hbm] * (len(operands) - 1)
    held_operands = operands[2:]
    sub = points // 3 if points % 48 == 0 else points
    half = jnp.bfloat16
    dma = pltpu.SemaphoreType.DMA
    out = pl.pallas_call(
        functools.partial(enter_kernel, sub, nb, len(held_operands)),
        in_specs=specs,
        out_specs=hbm,
        out_shape=jax.ShapeDtypeStruct((rows, points, feat), half),
        scratch_shapes=[pltpu.VMEM(o.shape, o.dtype) for o in held_operands]
        + [
            pltpu.VMEM((2, points, feat), half),
            pltpu.VMEM((rows, points, feat), half),
            pltpu.VMEM((rows, points, feat), half),
            pltpu.VMEM((rows, groups, width, feat), half),
            pltpu.VMEM((rows, groups, width, feat), half),
            pltpu.VMEM((width, nb * groups, feat), half),
            pltpu.VMEM((held, 2 * KLAT, feat), jnp.float32),
            pltpu.VMEM((held, 2 * KLAT, feat), half),
            pltpu.VMEM((2, held - PACK // 2, 2 * KLAT, feat), half),
            pltpu.VMEM((points, feat), half),
            pltpu.VMEM((points, 2 * KLON), half),
            pltpu.VMEM((4, feat, feat), half),
            pltpu.VMEM((2, points, feat), half),
            dma((2,)),
            dma((rows,)),
            dma((rows * (points // sub),)),
            dma((rows,)),
            dma((rows,)),
            dma((width // PACK - 1,)),
            dma((2 * (width // PACK - 1),)),
            dma((3 * (width // PACK),)),
            dma((rows // 2,)),
            dma((2,)),
            dma((len(held_operands),)),
        ],
        compiler_params=pltpu.CompilerParams(
            collective_id=0, has_side_effects=True, vmem_limit_bytes=67043328
        ),
        name="layer",
    )(*operands)
    return out[None]


def streams(members, groups, lat_dev, points, feat):
    width = 2 * KLON // groups
    return (
        members == 2
        and groups == PACK
        and (2 * KLON) % (groups * PACK) == 0
        and points == 2 * KLON
        and feat % 128 == 0
        and lat_dev % 2 == 0
        and width % PACK == 0
        and width > PACK
    )


def layer(mesh_sizes, *args):
    if streams(*mesh_sizes, *args[0].shape[1:]):
        return fused(mesh_sizes, *args)
    return shards(mesh_sizes, *args)


def solution(mesh):
    in_specs = (P("ens", "grid", None, None), P("grid"), P(), P(), P(), P(), P(), P(), P(), P())
    out_specs = P("ens", "grid", None, None)
    sizes = (mesh.shape["ens"], mesh.shape["grid"])
    return jax.shard_map(
        functools.partial(layer, sizes),
        mesh=mesh,
        in_specs=in_specs,
        out_specs=out_specs,
        check_vma=False,
    )
```

```python
import functools
import math

import jax
import jax.numpy as jnp
import numpy as np
from jax import lax
from jax.experimental import pallas as pl
from jax.experimental.pallas import tpu as pltpu
from jax.sharding import PartitionSpec as P

HEAD = 32
NLAT = 384
KLON = 384
KLAT = 128
CHUNKS = 6
BACK_CHUNKS = 2

MESH = pl.DeviceIdType.MESH
SWAP_AHEAD = 6
ARRIVE_LAG = 3
PACK = 16

norm_eps = 1e-05


def layer_norm(widened, gain_vec):
    center = widened - jnp.mean(widened, axis=-1, keepdims=True)
    spread = jnp.mean(center * center, axis=-1, keepdims=True)
    return (center * lax.rsqrt(spread + norm_eps) * gain_vec).astype(jnp.bfloat16)


def wave_order(groups):
    held = KLON // groups
    place = jnp.arange(2 * KLON, dtype=jnp.int32)
    part = place // held % 2
    wave = place // (2 * held) * held + place % held
    return part, wave


def lon_forward(points, groups):
    part, wave = wave_order(groups)
    positions = jnp.arange(points, dtype=jnp.int32)
    turn_count = wave[:, None] * positions[None, :] % points
    angles = 2.0 * math.pi / points * turn_count.astype(jnp.float32)
    factor = 1.0 / math.sqrt(points)
    return jnp.where(
        part[:, None] == 0, jnp.cos(angles) * factor, -jnp.sin(angles) * factor
    ).astype(jnp.bfloat16)


def lon_inverse(points, groups):
    part, wave = wave_order(groups)
    positions = jnp.arange(points, dtype=jnp.int32)
    turn_count = positions[:, None] * wave[None, :] % points
    angles = 2.0 * math.pi / points * turn_count.astype(jnp.float32)
    weight = jnp.where(wave == 0, 1.0, 2.0).astype(jnp.float32)[None, :] / math.sqrt(points)
    return jnp.where(
        part[None, :] == 0, jnp.cos(angles) * weight, -jnp.sin(angles) * weight
    ).astype(jnp.bfloat16)


def lat_angles(row_count, mode_count):
    frequency = jnp.arange(mode_count, dtype=jnp.int32)
    frequency = jnp.where(frequency < mode_count // 2, frequency, frequency - mode_count)
    positions = jnp.arange(row_count, dtype=jnp.int32)
    turn_count = frequency[:, None] * positions[None, :] % row_count
    return 2.0 * math.pi / row_count * turn_count.astype(jnp.float32)


def lat_forward(row_count, mode_count):
    angles = lat_angles(row_count, mode_count)
    factor = 1.0 / math.sqrt(row_count)
    cosine = jnp.cos(angles) * factor
    sine_part = jnp.sin(angles) * factor
    return jnp.stack(
        [jnp.stack([cosine, sine_part], axis=1), jnp.stack([-sine_part, cosine], axis=1)]
    ).astype(jnp.bfloat16)


def lat_inverse(row_count, mode_count):
    angles = jnp.transpose(lat_angles(row_count, mode_count))
    factor = 1.0 / math.sqrt(row_count)
    cosine = jnp.cos(angles) * factor
    sine_part = jnp.sin(angles) * factor
    return jnp.stack([jnp.stack([cosine, -sine_part]), jnp.stack([sine_part, cosine])]).astype(
        jnp.bfloat16
    )


def complex_blocks(weight):
    real_part = weight[0]
    imag_part = weight[1]
    return jnp.stack([jnp.stack([real_part, imag_part]), jnp.stack([-imag_part, real_part])])


def mix_blocks(spec, big):
    blocks = spec.reshape(spec.shape[:3] + (big.shape[2], big.shape[3]))
    out_blocks = jnp.einsum("pqkbi,psbio->sqkbo", blocks, big, preferred_element_type=jnp.float32)
    return out_blocks.reshape(spec.shape)


def dot(left, right):
    return jnp.dot(left, right, preferred_element_type=jnp.float32)


def attend_kernel(others, first_row, sub, counts, own, *refs):
    other_refs = refs[:others]
    (gain_one, w_qkv, w_out, gain_two, table, sums, waves, attended, spectrum, normed) = refs[others:]
    points, feat = own.shape[1:]
    scale = 1.0 / math.sqrt(HEAD)
    for start in range(0, points, sub):
        rows = pl.ds(start, sub)
        fields = own[0, rows, :].astype(jnp.float32)
        joined = dot(layer_norm(fields, gain_one[...]), w_qkv[...]).astype(jnp.bfloat16)
        queries = joined[:, :feat].astype(jnp.float32)
        own_keys = joined[:, feat : 2 * feat].astype(jnp.float32)
        values = [joined[:, 2 * feat :].astype(jnp.float32)]
        shifted = [jnp.zeros((sub, feat), jnp.float32)]
        for ref in other_refs:
            side = layer_norm(ref[0, rows, :].astype(jnp.float32), gain_one[...])
            pair = dot(side, w_qkv[:, feat:]).astype(jnp.bfloat16)
            terms = queries * (pair[:, :feat].astype(jnp.float32) - own_keys)
            upper = terms.astype(jnp.bfloat16)
            lower = (terms - upper.astype(jnp.float32)).astype(jnp.bfloat16)
            total = dot(upper, sums[...]) + dot(lower, sums[...])
            shifted.append(total * scale)
            values.append(pair[:, feat:].astype(jnp.float32))
        largest = functools.reduce(jnp.maximum, shifted)
        exps = [jnp.exp(item - largest) for item in shifted]
        totals = functools.reduce(jnp.add, exps)
        mixed = functools.reduce(
            jnp.add,
            [e.astype(jnp.bfloat16).astype(jnp.float32) * v for e, v in zip(exps, values)],
        )
        mixed = (mixed / totals).astype(jnp.bfloat16)
        result = (fields + dot(mixed, w_out[...])).astype(jnp.bfloat16)
        attended[0, rows, :] = result
        normed[rows, :] = layer_norm(result.astype(jnp.float32), gain_two[...])
    kept = waves[...] < counts[first_row + pl.program_id(0)]
    spec = dot(table[...], normed[...])
    spec = jnp.where(kept, spec, 0.0).astype(jnp.bfloat16)
    if len(spectrum.shape) == 4:
        spectrum[:, 0] = spec.reshape(spectrum.shape[0], spectrum.shape[2], feat)
    else:
        spectrum[0] = spec


def attend(chunk, rows, aligned, groups, fields, others, counts, gains, weights, tables):
    points, feat = fields.shape[1:]
    first_row = chunk * rows
    sub = points // 3 if points % 48 == 0 else points
    whole = lambda a: pl.BlockSpec(a.shape, lambda i, c: (0,) * a.ndim)
    w_qkv, w_out = weights
    table, sums, waves = tables
    held = 2 * KLON // groups
    if aligned:
        spec_shape = (groups, rows, held, feat)
        spec_block = pl.BlockSpec((groups, 1, held, feat), lambda i, c: (0, i, 0, 0))
    else:
        spec_shape = (rows, 2 * KLON, feat)
        spec_block = pl.BlockSpec((1, 2 * KLON, feat), lambda i, c: (i, 0, 0))
    row_block = pl.BlockSpec((1, points, feat), lambda i, c: (i, 0, 0))
    own_block = pl.BlockSpec((1, points, feat), lambda i, c: (first_row + i, 0, 0))
    params = (gains[0], w_qkv, w_out, gains[1], table, sums, waves)
    flops = 2 * rows * points * feat * (feat * 8 + 2 * KLON)
    attended, spectrum = pl.pallas_call(
        functools.partial(attend_kernel, len(others), first_row, sub),
        grid_spec=pltpu.PrefetchScalarGridSpec(
            num_scalar_prefetch=1,
            grid=(rows,),
            in_specs=[own_block] + [row_block] * len(others) + [whole(p) for p in params],
            out_specs=[row_block, spec_block],
            scratch_shapes=[pltpu.VMEM((points, feat), jnp.bfloat16)],
        ),
        out_shape=[
            jax.ShapeDtypeStruct((rows, points, feat), jnp.bfloat16),
            jax.ShapeDtypeStruct(spec_shape, jnp.bfloat16),
        ],
        cost_estimate=pl.CostEstimate(
            flops=flops, bytes_accessed=rows * points * feat * 8, transcendentals=rows * points * feat * 2
        ),
        compiler_params=pltpu.CompilerParams(vmem_limit_bytes=40 * 1024 * 1024),
    )(counts, fields, *others, *params)
    if not aligned:
        spectrum = jnp.transpose(spectrum.reshape(rows, groups, held, feat), (1, 0, 2, 3))
    return attended, spectrum


def finish_kernel(first_row, counts, spectrum, attended, table, waves, *refs):
    out = refs[-1]
    feat = out.shape[-1]
    kept = waves[...] < counts[first_row + pl.program_id(0)]
    if len(spectrum.shape) == 4:
        spec = spectrum[:, 0].reshape(2 * KLON, feat)
    else:
        spec = spectrum[0]
    spec = jnp.where(kept, spec.astype(jnp.float32), 0.0).astype(jnp.bfloat16)
    out[0] = (attended[0].astype(jnp.float32) + dot(table[...], spec)).astype(jnp.bfloat16)


def finish(first_row, offset, lat_dev, aligned, groups, spectrum, attended, counts, table, waves, so_far):
    rows, points, feat = attended.shape
    held = 2 * KLON // groups
    whole = lambda a: pl.BlockSpec(a.shape, lambda i, c: (0,) * a.ndim)
    if aligned:
        spec_block = pl.BlockSpec((groups, 1, held, feat), lambda i, c: (0, offset + i, 0, 0))
    else:
        spectrum = jnp.transpose(spectrum, (1, 0, 2, 3)).reshape(-1, 2 * KLON, feat)
        spec_block = pl.BlockSpec((1, 2 * KLON, feat), lambda i, c: (offset + i, 0, 0))
    row_block = pl.BlockSpec((1, points, feat), lambda i, c: (i, 0, 0))
    out_block = pl.BlockSpec((1, points, feat), lambda i, c: (first_row + i, 0, 0))
    operands = [counts, spectrum, attended, table, waves]
    specs = [spec_block, row_block, whole(table), whole(waves)]
    aliases = {}
    if so_far is not None:
        aliases = {len(operands): 0}
        operands.append(so_far)
        specs.append(pl.BlockSpec(memory_space=pl.ANY))
    return pl.pallas_call(
        functools.partial(finish_kernel, first_row),
        grid_spec=pltpu.PrefetchScalarGridSpec(
            num_scalar_prefetch=1, grid=(rows,), in_specs=specs, out_specs=out_block
        ),
        out_shape=jax.ShapeDtypeStruct((lat_dev, points, feat), jnp.bfloat16),
        input_output_aliases=aliases,
        cost_estimate=pl.CostEstimate(
            flops=4 * rows * points * feat * KLON,
            bytes_accessed=rows * points * feat * 6,
            transcendentals=0,
        ),
        compiler_params=pltpu.CompilerParams(vmem_limit_bytes=40 * 1024 * 1024),
    )(*operands)


def shards(
    mesh_sizes, fields, mode_counts, gain_attn, w_query, w_key, w_value, w_out, gain_spec, w_first, w_second
):
    members, groups = mesh_sizes
    fields = fields[0]
    lat_dev, points, feat = fields.shape
    held = KLON // groups
    aligned = (2 * held) % 16 == 0
    chunks = max(c for c in range(1, CHUNKS + 1) if lat_dev % c == 0)
    rows = lat_dev // chunks
    shifts = [
        [(i, (i + s) % members) for i in range(members)] for s in range(1, members)
    ]
    others = []
    for c in range(chunks):
        others.append([lax.ppermute(fields[c * rows : (c + 1) * rows], "ens", s) for s in shifts])
    w_qkv = jnp.concatenate([w_query, w_key, w_value], axis=1)
    lanes = jnp.arange(feat, dtype=jnp.int32) // HEAD
    sums = (lanes[:, None] == lanes[None, :]).astype(jnp.bfloat16)
    waves = wave_order(groups)[1][:, None]
    gains = (gain_attn[None, :], gain_spec[None, :])
    tables = (lon_forward(points, groups), sums, waves)
    back_table = lon_inverse(points, groups)
    forward = lat_forward(NLAT, KLAT).reshape(2, KLAT, 2, groups, chunks, rows)
    backs = max(c for c in range(1, BACK_CHUNKS + 1) if chunks % c == 0)
    per_back = chunks // backs
    inverse = lat_inverse(NLAT, KLAT).reshape(2, 2, groups, backs, per_back * rows, KLAT)
    big_one = complex_blocks(w_first)
    big_two = complex_blocks(w_second)
    kept_fields = []
    rows_spec = None
    for c in range(chunks):
        attended, spectrum = attend(
            c, rows, aligned, groups, fields, others[c], mode_counts, gains, (w_qkv, w_out), tables
        )
        kept_fields.append(attended)
        arrived = lax.all_to_all(spectrum, "grid", split_axis=0, concat_axis=0)
        arrived = arrived.reshape(groups, rows, 2, held, feat)
        term = jnp.einsum(
            "pqrgj,gjrkd->pqkd",
            forward[:, :, :, :, c],
            arrived,
            preferred_element_type=jnp.float32,
        )
        rows_spec = term if rows_spec is None else rows_spec + term
        if c < chunks - 1:
            rows_spec = lax.optimization_barrier(rows_spec)
    rows_spec = rows_spec.astype(jnp.bfloat16)
    hidden = jnp.maximum(mix_blocks(rows_spec, big_one), 0.0).astype(jnp.bfloat16)
    second = mix_blocks(hidden, big_two).astype(jnp.bfloat16)
    out = None
    for b in range(backs):
        back_rows = jnp.einsum(
            "rpgjq,pqkd->gjrkd", inverse[:, :, :, b], second, preferred_element_type=jnp.float32
        ).astype(jnp.bfloat16)
        returned = lax.all_to_all(
            back_rows.reshape(groups, per_back * rows, 2 * held, feat), "grid", split_axis=0, concat_axis=0
        )
        for i in range(per_back):
            c = b * per_back + i
            out = finish(
                c * rows, i * rows, lat_dev, aligned, groups, returned, kept_fields[c], mode_counts,
                back_table, tables[2], out,
            )
    return out[None]


def np_wave_order(groups):
    held = KLON // groups
    each = PACK // 2
    place = np.arange(2 * KLON)
    group, pack, within = place // (2 * held), place % (2 * held) // PACK, place % each
    return place // each % 2, group * held + pack * each + within


def np_lon_forward(points, groups):
    part, wave = np_wave_order(groups)
    turns = wave[:, None] * np.arange(points)[None, :] % points
    angles = 2.0 * math.pi / points * turns
    rows = np.where(part[:, None] == 0, np.cos(angles), -np.sin(angles)) / math.sqrt(points)
    return jnp.asarray(rows.astype(np.float32), dtype=jnp.bfloat16)


def np_lat_tables(groups, batches, nb):
    frequency = np.arange(KLAT)
    frequency = np.where(frequency < KLAT // 2, frequency, frequency - KLAT)
    angles = 2.0 * math.pi / NLAT * (frequency[:, None] * np.arange(NLAT)[None, :] % NLAT)
    cosine = np.cos(angles) / math.sqrt(NLAT)
    sine = np.sin(angles) / math.sqrt(NLAT)
    both = np.stack([np.stack([cosine, sine], axis=1), np.stack([-sine, cosine], axis=1)])
    forward = both.reshape(2, KLAT, 2, groups, batches, nb).transpose(4, 0, 1, 2, 5, 3)
    forward = forward.reshape(batches, 2 * KLAT, 2 * nb * groups).astype(np.float32)
    inverse = both.reshape(2, KLAT, 2, 2, groups // 2, batches * nb).transpose(3, 2, 5, 4, 0, 1)
    inverse = inverse.reshape(2, batches * nb * groups, 2 * KLAT).astype(np.float32)
    return jnp.asarray(forward, dtype=jnp.bfloat16), jnp.asarray(inverse, dtype=jnp.bfloat16)


def np_turn(groups):
    count = groups * PACK
    source = np.arange(count).reshape(groups, PACK).T.reshape(-1)
    turn = np.zeros((count, count), np.float32)
    turn[np.arange(count), source] = 1.0
    return jnp.asarray(turn, dtype=jnp.bfloat16)


def enter_kernel(points_sub, nb, held_count, counts, fields, *refs):
    sources, out, held_refs = refs[:held_count], refs[held_count], refs[held_count + 1 : 2 * held_count + 1]
    rest, sems = refs[2 * held_count + 1 : -1], refs[-1]
    copies = [
        pltpu.make_async_copy(source, target, sems.at[i])
        for i, (source, target) in enumerate(zip(sources, held_refs))
    ]
    for copy in copies:
        copy.start()
    layer_kernel(points_sub, nb, copies, counts, fields, *held_refs, out, *rest)


def layer_kernel(
    points_sub,
    nb,
    copies,
    counts,
    fields,
    gain_one,
    w_query,
    w_key,
    w_value,
    w_out,
    gain_two,
    table,
    sums,
    waves,
    forward,
    inverse,
    turn,
    spread,
    w_first,
    w_second,
    attended,
    own,
    other,
    sent,
    arrived,
    turned,
    rows_spec,
    second,
    far,
    normed,
    back_table,
    blocks,
    own_sem,
    swap_send,
    swap_recv,
    fwd_send,
    fwd_recv,
    far_send,
    far_recv,
    back_send,
    back_recv,
):
    rows, groups, width, feat = sent.shape
    points = other.shape[1]
    held = width // 2
    packs = width // PACK
    batches = rows // nb
    sub = points_sub
    member = lax.axis_index("ens")
    me = lax.axis_index("grid")
    scale = 1.0 / math.sqrt(HEAD)
    partners = [me ^ o for o in range(groups - 1, 0, -1)]
    each = PACK // 2
    half = groups // 2
    quarter = groups // 4
    side_at = me // half
    far_side = 1 - side_at
    place_at = lax.rem(me, half)
    lane_at = lax.rem(me, quarter)
    inner = me // quarter == 1 + side_at
    relay = (1 + far_side) * quarter + lane_at
    slot_at = jnp.where(inner, 0, 1)
    relayed = packs - 1

    barrier = pltpu.get_barrier_semaphore()
    for t in partners:
        pl.semaphore_signal(barrier, inc=1, device_id={"grid": t}, device_id_type=MESH)
    pl.semaphore_signal(barrier, inc=1, device_id={"ens": 1 - member}, device_id_type=MESH)
    pl.semaphore_wait(barrier, groups)

    thirds = points // sub

    def swap(r, s):
        span = pl.ds(s * sub, sub)
        return pltpu.make_async_remote_copy(
            src_ref=fields.at[r, span],
            dst_ref=other.at[r, span],
            send_sem=swap_send.at[r],
            recv_sem=swap_recv.at[r * thirds + s],
            device_id={"ens": 1 - member},
            device_id_type=MESH,
        )

    def fetch(r, slot):
        return pltpu.make_async_copy(fields.at[r], own.at[slot], own_sem.at[slot])

    ahead = min(SWAP_AHEAD, rows)
    for r in range(ahead):
        for s in range(thirds):
            swap(r, s).start()
    fetch(0, 0).start()
    for copy in copies:
        copy.wait()

    eye = lax.broadcasted_iota(jnp.int32, (feat, feat), 0) // HEAD
    same = eye == lax.broadcasted_iota(jnp.int32, (feat, feat), 1) // HEAD
    for layer, weight in enumerate((w_first, w_second)):
        for part in range(2):
            wide = dot(weight[part], spread[...])
            blocks[2 * layer + part] = jnp.where(same, wide, 0.0).astype(jnp.bfloat16)
    back_table[...] = jnp.transpose(table[...])
    rows_spec[...] = jnp.zeros_like(rows_spec)

    def attend(r):
        slot = lax.rem(r, 2)
        fetch(r, slot).wait()

        @pl.when(r + 1 < rows)
        def _():
            fetch(r + 1, 1 - slot).start()

        @pl.when(r + ahead < rows)
        def _():
            for s in range(thirds):
                swap(r + ahead, s).start()

        for s in range(thirds):
            swap(r, s).wait_recv()
            span = pl.ds(s * sub, sub)
            field = own[slot, span, :].astype(jnp.float32)
            norm = layer_norm(field, gain_one[...])
            queries = dot(norm, w_query[...]).astype(jnp.bfloat16).astype(jnp.float32)
            own_keys = dot(norm, w_key[...]).astype(jnp.bfloat16).astype(jnp.float32)
            own_values = dot(norm, w_value[...]).astype(jnp.bfloat16).astype(jnp.float32)
            side = layer_norm(other[r, span, :].astype(jnp.float32), gain_one[...])
            keys = dot(side, w_key[...]).astype(jnp.bfloat16).astype(jnp.float32)
            values = dot(side, w_value[...]).astype(jnp.bfloat16).astype(jnp.float32)
            terms = queries * (keys - own_keys)
            upper = terms.astype(jnp.bfloat16)
            lower = (terms - upper.astype(jnp.float32)).astype(jnp.bfloat16)
            shifted = (dot(upper, sums[...]) + dot(lower, sums[...])) * scale
            largest = jnp.maximum(shifted, 0.0)
            own_exp = jnp.exp(-largest)
            side_exp = jnp.exp(shifted - largest)
            mixed = own_exp.astype(jnp.bfloat16).astype(jnp.float32) * own_values
            mixed += side_exp.astype(jnp.bfloat16).astype(jnp.float32) * values
            mixed = (mixed / (own_exp + side_exp)).astype(jnp.bfloat16)
            done = (field + dot(mixed, w_out[...])).astype(jnp.bfloat16)
            attended[r, span, :] = done
            normed[span, :] = layer_norm(done.astype(jnp.float32), gain_two[...])
        spec = dot(table[...], normed[...])
        spec = jnp.where(waves[...] < counts[r], spec, 0.0).astype(jnp.bfloat16)
        sent[r] = spec.reshape(groups, width, feat)
        arrived[r, me] = sent[r, me]
        for t in partners:
            pltpu.make_async_remote_copy(
                src_ref=sent.at[r, t],
                dst_ref=arrived.at[r, me],
                send_sem=fwd_send.at[r],
                recv_sem=fwd_recv.at[r],
                device_id={"grid": t},
                device_id_type=MESH,
            ).start()

    def turn_in(r):
        whole = arrived.at[r, pl.ds(0, groups - 1)]
        pltpu.make_async_copy(whole, whole, fwd_recv.at[r]).wait()
        place = pl.ds(pl.multiple_of(lax.rem(r, nb) * groups, PACK), groups)
        for b in range(packs):
            block = arrived[r, :, b * PACK : (b + 1) * PACK, :].reshape(groups * PACK, feat)
            moved = dot(turn[...], block).astype(jnp.bfloat16)
            turned[b * PACK : (b + 1) * PACK, place, :] = moved.reshape(PACK, groups, feat)

    def lat_in(b, first, count):
        def step(i, _):
            k = first + i
            at = k // each * PACK + lax.rem(k, each)
            pair = jnp.concatenate([turned[at], turned[at + each]], axis=0)
            rows_spec[k] += dot(forward[b], pair)
            return 0

        lax.fori_loop(0, count, step, 0, unroll=4)

    def phase_in(i, _):
        @pl.when(i < rows)
        def _():
            attend(i)

        @pl.when(i >= ARRIVE_LAG)
        def _():
            turn_in(i - ARRIVE_LAG)

        b = (i - ARRIVE_LAG) // nb

        @pl.when((i >= ARRIVE_LAG) & (lax.rem(i - ARRIVE_LAG, nb) == nb - 1) & (b < batches - 1))
        def _():
            lat_in(b, 0, held)

        return 0

    lax.fori_loop(0, rows + ARRIVE_LAG, phase_in, 0)

    mode = second.shape[1] // 2

    def complex_mix(real, imag, layer):
        w_real, w_imag = blocks[2 * layer], blocks[2 * layer + 1]
        return dot(real, w_real) - dot(imag, w_imag), dot(real, w_imag) + dot(imag, w_real)

    def ship(p):
        span = pl.ds(p * each, each)
        return pltpu.make_async_remote_copy(
            src_ref=second.at[span],
            dst_ref=far.at[slot_at, span],
            send_sem=far_send.at[p],
            recv_sem=far_recv.at[slot_at * relayed + p],
            device_id={"grid": relay},
            device_id_type=MESH,
        )

    def mix(p, _):
        lat_in(batches - 1, p * each, each)
        span = pl.ds(p * each, each)
        real = rows_spec[span, :mode].reshape(each * mode, feat).astype(jnp.bfloat16)
        imag = rows_spec[span, mode:].reshape(each * mode, feat).astype(jnp.bfloat16)
        real, imag = complex_mix(real, imag, 0)
        real = jnp.maximum(real, 0.0).astype(jnp.bfloat16)
        imag = jnp.maximum(imag, 0.0).astype(jnp.bfloat16)
        real, imag = complex_mix(real, imag, 1)
        second[span, :mode] = real.astype(jnp.bfloat16).reshape(each, mode, feat)
        second[span, mode:] = imag.astype(jnp.bfloat16).reshape(each, mode, feat)

        @pl.when(inner & (p < relayed))
        def _():
            ship(p).start()

        return 0

    lax.fori_loop(0, packs, mix, 0)

    def wait_sent(r, _):
        whole = sent.at[r, pl.ds(0, groups - 1)]
        pltpu.make_async_copy(whole, whole, fwd_send.at[r]).wait()
        return 0

    lax.fori_loop(0, rows, wait_sent, 0)

    pair = PACK // half
    span_in = nb * groups
    span_out = rows * half

    def spread_rows(read, group, p, to_own, buffer, a, b, sem):
        to = side_at if to_own else far_side

        def lat(k, _):
            both = dot(inverse[to], read(k)).astype(jnp.bfloat16)
            for r in range(2):
                for c, start in enumerate(range(0, span_out, span_in)):
                    size = min(span_in, span_out - start)
                    at = r * span_out + start
                    turned[c * PACK + r * each + k, :size] = both[at : at + size]
            return 0

        lax.fori_loop(0, each, lat, 0, unroll=4)
        spot = pl.ds(pl.multiple_of(group * width + p * PACK, PACK), PACK)
        cut = pl.ds(pl.multiple_of(b * PACK, PACK), PACK)

        def send(i, _):
            per = span_in // PACK
            lead = pl.ds(i // per * PACK, PACK)
            block = turned[lead, pl.ds(pl.multiple_of(lax.rem(i, per) * PACK, PACK), PACK), :]
            moved = dot(turn[...], block.reshape(PACK * PACK, feat)).astype(jnp.bfloat16)
            span = pl.ds(i * pair, pair)
            buffer[span, pl.ds(a * half, half), cut, :] = moved.reshape(pair, half, PACK, feat)
            if to_own:
                other[span, spot, :] = buffer[span, a * half + place_at, cut, :]
            for o in range(half - 1, 0 if to_own else -1, -1):
                t = place_at ^ o
                pltpu.make_async_remote_copy(
                    src_ref=buffer.at[span, a * half + t, cut],
                    dst_ref=other.at[span, spot],
                    send_sem=sem,
                    recv_sem=back_recv.at[i],
                    device_id={"grid": to * half + t},
                    device_id_type=MESH,
                ).start()
            return 0

        lax.fori_loop(0, rows // pair, send, 0)

    def own_rows(p, _):
        spread_rows(lambda k: second[p * each + k], me, p, True, sent, 0, p, back_send.at[p])
        return 0

    lax.fori_loop(0, packs, own_rows, 0)

    @pl.when(jnp.logical_not(inner))
    def _():
        for p in range(relayed):
            ship(p).start()

    last = packs - 1
    spread_rows(lambda k: second[last * each + k], me, last, False, sent, 1, last, back_send.at[packs])

    @pl.when(inner)
    def _():
        def relay_rows(q, _):
            u, p = q // relayed, lax.rem(q, relayed)
            group = (1 + far_side + u * (2 * far_side - 1)) * quarter + lane_at
            got = far.at[u, pl.ds(p * each, each)]
            pltpu.make_async_copy(got, got, far_recv.at[u * relayed + p]).wait()
            sem = back_send.at[packs + 1 + q]
            spread_rows(lambda k: far[u, p * each + k], group, p, True, arrived, u, p, sem)
            return 0

        lax.fori_loop(0, 2 * relayed, relay_rows, 0)

    def finish(j):
        weight = jnp.where(waves[...] == 0, 1.0, 2.0)
        weight = jnp.where(waves[...] < counts[j], weight, 0.0)
        spec = (other[j].astype(jnp.float32) * weight).astype(jnp.bfloat16)
        total = attended[j].astype(jnp.float32) + dot(back_table[...], spec)
        attended[j] = total.astype(jnp.bfloat16)

    def phase_out(i, _):
        span = pl.ds(i * pair, pair)

        @pl.when(inner)
        def _():
            whole = other.at[span, pl.ds(0, (groups - 1) * width - 2 * relayed * PACK)]
            pltpu.make_async_copy(whole, whole, back_recv.at[i]).wait()

        @pl.when(jnp.logical_not(inner))
        def _():
            whole = other.at[span, pl.ds(0, (groups - 1) * width)]
            pltpu.make_async_copy(whole, whole, back_recv.at[i]).wait()

        for r in range(pair):
            finish(i * pair + r)
        return 0

    lax.fori_loop(0, rows // pair, phase_out, 0)

    def drain(r, _):
        pltpu.make_async_copy(fields.at[r], fields.at[r], swap_send.at[r]).wait()
        return 0

    lax.fori_loop(0, rows, drain, 0)
    for p in range(relayed):
        ship(p).wait_send()
    most = sent.at[:, pl.ds(0, half), pl.ds(0, PACK)]
    fewer = sent.at[:, pl.ds(0, half - 1), pl.ds(0, PACK)]
    for p in range(packs):
        pltpu.make_async_copy(fewer, fewer, back_send.at[p]).wait()
    pltpu.make_async_copy(most, most, back_send.at[packs]).wait()

    @pl.when(inner)
    def _():
        for q in range(2 * relayed):
            pltpu.make_async_copy(fewer, fewer, back_send.at[packs + 1 + q]).wait()


def fused(mesh_sizes, fields, mode_counts, gain_attn, w_query, w_key, w_value, w_out, gain_spec, w_first, w_second):
    _, groups = mesh_sizes
    fields = fields[0]
    rows, points, feat = fields.shape
    width = 2 * KLON // groups
    held = width // 2
    nb = max(n for n in range(1, rows + 1) if rows % n == 0 and 2 * n * groups <= max(feat, 2 * groups))
    forward, inverse = np_lat_tables(groups, rows // nb, nb)
    turn = np_turn(groups)
    block = w_first.shape[-1]
    lanes = np.arange(feat)
    heads = jnp.asarray((lanes[:, None] // HEAD == lanes[None, :] // HEAD).astype(np.float32), dtype=jnp.bfloat16)
    spread = jnp.asarray((np.arange(block)[:, None] == lanes[None, :] % block).astype(np.float32), dtype=jnp.bfloat16)
    waves = jnp.asarray(np_wave_order(groups)[1][:, None], dtype=jnp.int32)
    operands = [
        mode_counts, fields, gain_attn[None, :], w_query, w_key, w_value, w_out, gain_spec[None, :],
        np_lon_forward(points, groups), heads, waves, forward, inverse, turn, spread,
        w_first.reshape(2, feat, block), w_second.reshape(2, feat, block),
    ]
    hbm = pl.BlockSpec(memory_space=pl.ANY)
    specs = [pl.BlockSpec(memory_space=pltpu.SMEM)] + [hbm] * (len(operands) - 1)
    held_operands = operands[2:]
    sub = points // 3 if points % 48 == 0 else points
    half = jnp.bfloat16
    dma = pltpu.SemaphoreType.DMA
    out = pl.pallas_call(
        functools.partial(enter_kernel, sub, nb, len(held_operands)),
        in_specs=specs,
        out_specs=pl.BlockSpec(memory_space=pltpu.VMEM),
        out_shape=pltpu.VMEM((rows, points, feat), half),
        scratch_shapes=[pltpu.VMEM(o.shape, o.dtype) for o in held_operands]
        + [
            pltpu.VMEM((2, points, feat), half),
            pltpu.VMEM((rows, points, feat), half),
            pltpu.VMEM((rows, groups, width, feat), half),
            pltpu.VMEM((rows, groups, width, feat), half),
            pltpu.VMEM((width, nb * groups, feat), half),
            pltpu.VMEM((held, 2 * KLAT, feat), jnp.float32),
            pltpu.VMEM((held, 2 * KLAT, feat), half),
            pltpu.VMEM((2, held - PACK // 2, 2 * KLAT, feat), half),
            pltpu.VMEM((points, feat), half),
            pltpu.VMEM((points, 2 * KLON), half),
            pltpu.VMEM((4, feat, feat), half),
            dma((2,)),
            dma((rows,)),
            dma((rows * (points // sub),)),
            dma((rows,)),
            dma((rows,)),
            dma((width // PACK - 1,)),
            dma((2 * (width // PACK - 1),)),
            dma((3 * (width // PACK),)),
            dma((rows // 2,)),
            dma((len(held_operands),)),
        ],
        compiler_params=pltpu.CompilerParams(
            collective_id=0, has_side_effects=True, vmem_limit_bytes=67043328 - rows * points * feat * 2
        ),
        name="layer",
    )(*operands)
    return out[None]


def streams(members, groups, lat_dev, points, feat):
    width = 2 * KLON // groups
    return (
        members == 2
        and groups == PACK
        and (2 * KLON) % (groups * PACK) == 0
        and points == 2 * KLON
        and feat % 128 == 0
        and lat_dev % 2 == 0
        and width % PACK == 0
        and width > PACK
    )


def layer(mesh_sizes, *args):
    if streams(*mesh_sizes, *args[0].shape[1:]):
        return fused(mesh_sizes, *args)
    return shards(mesh_sizes, *args)


def solution(mesh):
    in_specs = (P("ens", "grid", None, None), P("grid"), P(), P(), P(), P(), P(), P(), P(), P())
    out_specs = P("ens", "grid", None, None)
    sizes = (mesh.shape["ens"], mesh.shape["grid"])
    return jax.shard_map(
        functools.partial(layer, sizes),
        mesh=mesh,
        in_specs=in_specs,
        out_specs=out_specs,
        check_vma=False,
    )
```

```python
import functools
import math

import jax
import jax.numpy as jnp
import numpy as np
from jax import lax
from jax.experimental import pallas as pl
from jax.experimental.pallas import tpu as pltpu
from jax.sharding import PartitionSpec as P

HEAD = 32
NLAT = 384
KLON = 384
KLAT = 128
CHUNKS = 6
BACK_CHUNKS = 2

MESH = pl.DeviceIdType.MESH
SWAP_AHEAD = 6
ARRIVE_LAG = 3
PACK = 16

norm_eps = 1e-05


def layer_norm(widened, gain_vec):
    center = widened - jnp.mean(widened, axis=-1, keepdims=True)
    spread = jnp.mean(center * center, axis=-1, keepdims=True)
    return (center * lax.rsqrt(spread + norm_eps) * gain_vec).astype(jnp.bfloat16)


def wave_order(groups):
    held = KLON // groups
    place = jnp.arange(2 * KLON, dtype=jnp.int32)
    part = place // held % 2
    wave = place // (2 * held) * held + place % held
    return part, wave


def lon_forward(points, groups):
    part, wave = wave_order(groups)
    positions = jnp.arange(points, dtype=jnp.int32)
    turn_count = wave[:, None] * positions[None, :] % points
    angles = 2.0 * math.pi / points * turn_count.astype(jnp.float32)
    factor = 1.0 / math.sqrt(points)
    return jnp.where(
        part[:, None] == 0, jnp.cos(angles) * factor, -jnp.sin(angles) * factor
    ).astype(jnp.bfloat16)


def lon_inverse(points, groups):
    part, wave = wave_order(groups)
    positions = jnp.arange(points, dtype=jnp.int32)
    turn_count = positions[:, None] * wave[None, :] % points
    angles = 2.0 * math.pi / points * turn_count.astype(jnp.float32)
    weight = jnp.where(wave == 0, 1.0, 2.0).astype(jnp.float32)[None, :] / math.sqrt(points)
    return jnp.where(
        part[None, :] == 0, jnp.cos(angles) * weight, -jnp.sin(angles) * weight
    ).astype(jnp.bfloat16)


def lat_angles(row_count, mode_count):
    frequency = jnp.arange(mode_count, dtype=jnp.int32)
    frequency = jnp.where(frequency < mode_count // 2, frequency, frequency - mode_count)
    positions = jnp.arange(row_count, dtype=jnp.int32)
    turn_count = frequency[:, None] * positions[None, :] % row_count
    return 2.0 * math.pi / row_count * turn_count.astype(jnp.float32)


def lat_forward(row_count, mode_count):
    angles = lat_angles(row_count, mode_count)
    factor = 1.0 / math.sqrt(row_count)
    cosine = jnp.cos(angles) * factor
    sine_part = jnp.sin(angles) * factor
    return jnp.stack(
        [jnp.stack([cosine, sine_part], axis=1), jnp.stack([-sine_part, cosine], axis=1)]
    ).astype(jnp.bfloat16)


def lat_inverse(row_count, mode_count):
    angles = jnp.transpose(lat_angles(row_count, mode_count))
    factor = 1.0 / math.sqrt(row_count)
    cosine = jnp.cos(angles) * factor
    sine_part = jnp.sin(angles) * factor
    return jnp.stack([jnp.stack([cosine, -sine_part]), jnp.stack([sine_part, cosine])]).astype(
        jnp.bfloat16
    )


def complex_blocks(weight):
    real_part = weight[0]
    imag_part = weight[1]
    return jnp.stack([jnp.stack([real_part, imag_part]), jnp.stack([-imag_part, real_part])])


def mix_blocks(spec, big):
    blocks = spec.reshape(spec.shape[:3] + (big.shape[2], big.shape[3]))
    out_blocks = jnp.einsum("pqkbi,psbio->sqkbo", blocks, big, preferred_element_type=jnp.float32)
    return out_blocks.reshape(spec.shape)


def dot(left, right):
    return jnp.dot(left, right, preferred_element_type=jnp.float32)


def attend_kernel(others, first_row, sub, counts, own, *refs):
    other_refs = refs[:others]
    (gain_one, w_qkv, w_out, gain_two, table, sums, waves, attended, spectrum, normed) = refs[others:]
    points, feat = own.shape[1:]
    scale = 1.0 / math.sqrt(HEAD)
    for start in range(0, points, sub):
        rows = pl.ds(start, sub)
        fields = own[0, rows, :].astype(jnp.float32)
        joined = dot(layer_norm(fields, gain_one[...]), w_qkv[...]).astype(jnp.bfloat16)
        queries = joined[:, :feat].astype(jnp.float32)
        own_keys = joined[:, feat : 2 * feat].astype(jnp.float32)
        values = [joined[:, 2 * feat :].astype(jnp.float32)]
        shifted = [jnp.zeros((sub, feat), jnp.float32)]
        for ref in other_refs:
            side = layer_norm(ref[0, rows, :].astype(jnp.float32), gain_one[...])
            pair = dot(side, w_qkv[:, feat:]).astype(jnp.bfloat16)
            terms = queries * (pair[:, :feat].astype(jnp.float32) - own_keys)
            upper = terms.astype(jnp.bfloat16)
            lower = (terms - upper.astype(jnp.float32)).astype(jnp.bfloat16)
            total = dot(upper, sums[...]) + dot(lower, sums[...])
            shifted.append(total * scale)
            values.append(pair[:, feat:].astype(jnp.float32))
        largest = functools.reduce(jnp.maximum, shifted)
        exps = [jnp.exp(item - largest) for item in shifted]
        totals = functools.reduce(jnp.add, exps)
        mixed = functools.reduce(
            jnp.add,
            [e.astype(jnp.bfloat16).astype(jnp.float32) * v for e, v in zip(exps, values)],
        )
        mixed = (mixed / totals).astype(jnp.bfloat16)
        result = (fields + dot(mixed, w_out[...])).astype(jnp.bfloat16)
        attended[0, rows, :] = result
        normed[rows, :] = layer_norm(result.astype(jnp.float32), gain_two[...])
    kept = waves[...] < counts[first_row + pl.program_id(0)]
    spec = dot(table[...], normed[...])
    spec = jnp.where(kept, spec, 0.0).astype(jnp.bfloat16)
    if len(spectrum.shape) == 4:
        spectrum[:, 0] = spec.reshape(spectrum.shape[0], spectrum.shape[2], feat)
    else:
        spectrum[0] = spec


def attend(chunk, rows, aligned, groups, fields, others, counts, gains, weights, tables):
    points, feat = fields.shape[1:]
    first_row = chunk * rows
    sub = points // 3 if points % 48 == 0 else points
    whole = lambda a: pl.BlockSpec(a.shape, lambda i, c: (0,) * a.ndim)
    w_qkv, w_out = weights
    table, sums, waves = tables
    held = 2 * KLON // groups
    if aligned:
        spec_shape = (groups, rows, held, feat)
        spec_block = pl.BlockSpec((groups, 1, held, feat), lambda i, c: (0, i, 0, 0))
    else:
        spec_shape = (rows, 2 * KLON, feat)
        spec_block = pl.BlockSpec((1, 2 * KLON, feat), lambda i, c: (i, 0, 0))
    row_block = pl.BlockSpec((1, points, feat), lambda i, c: (i, 0, 0))
    own_block = pl.BlockSpec((1, points, feat), lambda i, c: (first_row + i, 0, 0))
    params = (gains[0], w_qkv, w_out, gains[1], table, sums, waves)
    flops = 2 * rows * points * feat * (feat * 8 + 2 * KLON)
    attended, spectrum = pl.pallas_call(
        functools.partial(attend_kernel, len(others), first_row, sub),
        grid_spec=pltpu.PrefetchScalarGridSpec(
            num_scalar_prefetch=1,
            grid=(rows,),
            in_specs=[own_block] + [row_block] * len(others) + [whole(p) for p in params],
            out_specs=[row_block, spec_block],
            scratch_shapes=[pltpu.VMEM((points, feat), jnp.bfloat16)],
        ),
        out_shape=[
            jax.ShapeDtypeStruct((rows, points, feat), jnp.bfloat16),
            jax.ShapeDtypeStruct(spec_shape, jnp.bfloat16),
        ],
        cost_estimate=pl.CostEstimate(
            flops=flops, bytes_accessed=rows * points * feat * 8, transcendentals=rows * points * feat * 2
        ),
        compiler_params=pltpu.CompilerParams(vmem_limit_bytes=40 * 1024 * 1024),
    )(counts, fields, *others, *params)
    if not aligned:
        spectrum = jnp.transpose(spectrum.reshape(rows, groups, held, feat), (1, 0, 2, 3))
    return attended, spectrum


def finish_kernel(first_row, counts, spectrum, attended, table, waves, *refs):
    out = refs[-1]
    feat = out.shape[-1]
    kept = waves[...] < counts[first_row + pl.program_id(0)]
    if len(spectrum.shape) == 4:
        spec = spectrum[:, 0].reshape(2 * KLON, feat)
    else:
        spec = spectrum[0]
    spec = jnp.where(kept, spec.astype(jnp.float32), 0.0).astype(jnp.bfloat16)
    out[0] = (attended[0].astype(jnp.float32) + dot(table[...], spec)).astype(jnp.bfloat16)


def finish(first_row, offset, lat_dev, aligned, groups, spectrum, attended, counts, table, waves, so_far):
    rows, points, feat = attended.shape
    held = 2 * KLON // groups
    whole = lambda a: pl.BlockSpec(a.shape, lambda i, c: (0,) * a.ndim)
    if aligned:
        spec_block = pl.BlockSpec((groups, 1, held, feat), lambda i, c: (0, offset + i, 0, 0))
    else:
        spectrum = jnp.transpose(spectrum, (1, 0, 2, 3)).reshape(-1, 2 * KLON, feat)
        spec_block = pl.BlockSpec((1, 2 * KLON, feat), lambda i, c: (offset + i, 0, 0))
    row_block = pl.BlockSpec((1, points, feat), lambda i, c: (i, 0, 0))
    out_block = pl.BlockSpec((1, points, feat), lambda i, c: (first_row + i, 0, 0))
    operands = [counts, spectrum, attended, table, waves]
    specs = [spec_block, row_block, whole(table), whole(waves)]
    aliases = {}
    if so_far is not None:
        aliases = {len(operands): 0}
        operands.append(so_far)
        specs.append(pl.BlockSpec(memory_space=pl.ANY))
    return pl.pallas_call(
        functools.partial(finish_kernel, first_row),
        grid_spec=pltpu.PrefetchScalarGridSpec(
            num_scalar_prefetch=1, grid=(rows,), in_specs=specs, out_specs=out_block
        ),
        out_shape=jax.ShapeDtypeStruct((lat_dev, points, feat), jnp.bfloat16),
        input_output_aliases=aliases,
        cost_estimate=pl.CostEstimate(
            flops=4 * rows * points * feat * KLON,
            bytes_accessed=rows * points * feat * 6,
            transcendentals=0,
        ),
        compiler_params=pltpu.CompilerParams(vmem_limit_bytes=40 * 1024 * 1024),
    )(*operands)


def shards(
    mesh_sizes, fields, mode_counts, gain_attn, w_query, w_key, w_value, w_out, gain_spec, w_first, w_second
):
    members, groups = mesh_sizes
    fields = fields[0]
    lat_dev, points, feat = fields.shape
    held = KLON // groups
    aligned = (2 * held) % 16 == 0
    chunks = max(c for c in range(1, CHUNKS + 1) if lat_dev % c == 0)
    rows = lat_dev // chunks
    shifts = [
        [(i, (i + s) % members) for i in range(members)] for s in range(1, members)
    ]
    others = []
    for c in range(chunks):
        others.append([lax.ppermute(fields[c * rows : (c + 1) * rows], "ens", s) for s in shifts])
    w_qkv = jnp.concatenate([w_query, w_key, w_value], axis=1)
    lanes = jnp.arange(feat, dtype=jnp.int32) // HEAD
    sums = (lanes[:, None] == lanes[None, :]).astype(jnp.bfloat16)
    waves = wave_order(groups)[1][:, None]
    gains = (gain_attn[None, :], gain_spec[None, :])
    tables = (lon_forward(points, groups), sums, waves)
    back_table = lon_inverse(points, groups)
    forward = lat_forward(NLAT, KLAT).reshape(2, KLAT, 2, groups, chunks, rows)
    backs = max(c for c in range(1, BACK_CHUNKS + 1) if chunks % c == 0)
    per_back = chunks // backs
    inverse = lat_inverse(NLAT, KLAT).reshape(2, 2, groups, backs, per_back * rows, KLAT)
    big_one = complex_blocks(w_first)
    big_two = complex_blocks(w_second)
    kept_fields = []
    rows_spec = None
    for c in range(chunks):
        attended, spectrum = attend(
            c, rows, aligned, groups, fields, others[c], mode_counts, gains, (w_qkv, w_out), tables
        )
        kept_fields.append(attended)
        arrived = lax.all_to_all(spectrum, "grid", split_axis=0, concat_axis=0)
        arrived = arrived.reshape(groups, rows, 2, held, feat)
        term = jnp.einsum(
            "pqrgj,gjrkd->pqkd",
            forward[:, :, :, :, c],
            arrived,
            preferred_element_type=jnp.float32,
        )
        rows_spec = term if rows_spec is None else rows_spec + term
        if c < chunks - 1:
            rows_spec = lax.optimization_barrier(rows_spec)
    rows_spec = rows_spec.astype(jnp.bfloat16)
    hidden = jnp.maximum(mix_blocks(rows_spec, big_one), 0.0).astype(jnp.bfloat16)
    second = mix_blocks(hidden, big_two).astype(jnp.bfloat16)
    out = None
    for b in range(backs):
        back_rows = jnp.einsum(
            "rpgjq,pqkd->gjrkd", inverse[:, :, :, b], second, preferred_element_type=jnp.float32
        ).astype(jnp.bfloat16)
        returned = lax.all_to_all(
            back_rows.reshape(groups, per_back * rows, 2 * held, feat), "grid", split_axis=0, concat_axis=0
        )
        for i in range(per_back):
            c = b * per_back + i
            out = finish(
                c * rows, i * rows, lat_dev, aligned, groups, returned, kept_fields[c], mode_counts,
                back_table, tables[2], out,
            )
    return out[None]


def np_wave_order(groups):
    held = KLON // groups
    each = PACK // 2
    place = np.arange(2 * KLON)
    group, pack, within = place // (2 * held), place % (2 * held) // PACK, place % each
    return place // each % 2, group * held + pack * each + within


def np_lon_forward(points, groups):
    part, wave = np_wave_order(groups)
    turns = wave[:, None] * np.arange(points)[None, :] % points
    angles = 2.0 * math.pi / points * turns
    rows = np.where(part[:, None] == 0, np.cos(angles), -np.sin(angles)) / math.sqrt(points)
    return jnp.asarray(rows.astype(np.float32), dtype=jnp.bfloat16)


def np_lat_tables(groups, batches, nb):
    frequency = np.arange(KLAT)
    frequency = np.where(frequency < KLAT // 2, frequency, frequency - KLAT)
    angles = 2.0 * math.pi / NLAT * (frequency[:, None] * np.arange(NLAT)[None, :] % NLAT)
    cosine = np.cos(angles) / math.sqrt(NLAT)
    sine = np.sin(angles) / math.sqrt(NLAT)
    both = np.stack([np.stack([cosine, sine], axis=1), np.stack([-sine, cosine], axis=1)])
    forward = both.reshape(2, KLAT, 2, groups, batches, nb).transpose(4, 0, 1, 2, 5, 3)
    forward = forward.reshape(batches, 2 * KLAT, 2 * nb * groups).astype(np.float32)
    inverse = both.reshape(2, KLAT, 2, 2, groups // 2, batches * nb).transpose(3, 2, 5, 4, 0, 1)
    inverse = inverse.reshape(2, batches * nb * groups, 2 * KLAT).astype(np.float32)
    return jnp.asarray(forward, dtype=jnp.bfloat16), jnp.asarray(inverse, dtype=jnp.bfloat16)


def np_turn(groups):
    count = groups * PACK
    source = np.arange(count).reshape(groups, PACK).T.reshape(-1)
    turn = np.zeros((count, count), np.float32)
    turn[np.arange(count), source] = 1.0
    return jnp.asarray(turn, dtype=jnp.bfloat16)


def enter_kernel(points_sub, nb, held_count, counts, fields, *refs):
    sources, out, held_refs = refs[:held_count], refs[held_count], refs[held_count + 1 : 2 * held_count + 1]
    rest, sems = refs[2 * held_count + 1 : -1], refs[-1]
    copies = [
        pltpu.make_async_copy(source, target, sems.at[i])
        for i, (source, target) in enumerate(zip(sources, held_refs))
    ]
    for copy in copies:
        copy.start()
    layer_kernel(points_sub, nb, copies, counts, fields, *held_refs, out, *rest)


def layer_kernel(
    points_sub,
    nb,
    copies,
    counts,
    fields,
    gain_one,
    w_query,
    w_key,
    w_value,
    w_out,
    gain_two,
    table,
    sums,
    waves,
    forward,
    inverse,
    turn,
    spread,
    w_first,
    w_second,
    attended,
    own,
    other,
    sent,
    arrived,
    turned,
    rows_spec,
    second,
    far,
    normed,
    back_table,
    blocks,
    own_sem,
    swap_send,
    swap_recv,
    fwd_send,
    fwd_recv,
    far_send,
    far_recv,
    back_send,
    back_recv,
    go_sem,
):
    rows, groups, width, feat = sent.shape
    points = other.shape[1]
    held = width // 2
    packs = width // PACK
    batches = rows // nb
    sub = points_sub
    member = lax.axis_index("ens")
    me = lax.axis_index("grid")
    scale = 1.0 / math.sqrt(HEAD)
    partners = [me ^ o for o in range(groups - 1, 0, -1)]
    each = PACK // 2
    half = groups // 2
    quarter = groups // 4
    side_at = me // half
    far_side = 1 - side_at
    place_at = lax.rem(me, half)
    lane_at = lax.rem(me, quarter)
    inner = me // quarter == 1 + side_at
    relay = (1 + far_side) * quarter + lane_at
    outer = 3 * side_at * quarter + lane_at
    slot_at = jnp.where(inner, 0, 1)
    relayed = packs - 1

    barrier = pltpu.get_barrier_semaphore()
    for t in partners:
        pl.semaphore_signal(barrier, inc=1, device_id={"grid": t}, device_id_type=MESH)
    pl.semaphore_signal(barrier, inc=1, device_id={"ens": 1 - member}, device_id_type=MESH)
    pl.semaphore_wait(barrier, groups)

    thirds = points // sub

    def swap(r, s):
        span = pl.ds(s * sub, sub)
        return pltpu.make_async_remote_copy(
            src_ref=fields.at[r, span],
            dst_ref=other.at[r, span],
            send_sem=swap_send.at[r],
            recv_sem=swap_recv.at[r * thirds + s],
            device_id={"ens": 1 - member},
            device_id_type=MESH,
        )

    def fetch(r, slot):
        return pltpu.make_async_copy(fields.at[r], own.at[slot], own_sem.at[slot])

    ahead = min(SWAP_AHEAD, rows)
    for r in range(ahead):
        for s in range(thirds):
            swap(r, s).start()
    fetch(0, 0).start()
    for copy in copies:
        copy.wait()

    eye = lax.broadcasted_iota(jnp.int32, (feat, feat), 0) // HEAD
    same = eye == lax.broadcasted_iota(jnp.int32, (feat, feat), 1) // HEAD
    for layer, weight in enumerate((w_first, w_second)):
        for part in range(2):
            wide = dot(weight[part], spread[...])
            blocks[2 * layer + part] = jnp.where(same, wide, 0.0).astype(jnp.bfloat16)
    back_table[...] = jnp.transpose(table[...])
    rows_spec[...] = jnp.zeros_like(rows_spec)

    def attend(r):
        slot = lax.rem(r, 2)
        fetch(r, slot).wait()

        @pl.when(r + 1 < rows)
        def _():
            fetch(r + 1, 1 - slot).start()

        @pl.when(r + ahead < rows)
        def _():
            for s in range(thirds):
                swap(r + ahead, s).start()

        for s in range(thirds):
            swap(r, s).wait_recv()
            span = pl.ds(s * sub, sub)
            field = own[slot, span, :].astype(jnp.float32)
            norm = layer_norm(field, gain_one[...])
            queries = dot(norm, w_query[...]).astype(jnp.bfloat16).astype(jnp.float32)
            own_keys = dot(norm, w_key[...]).astype(jnp.bfloat16).astype(jnp.float32)
            own_values = dot(norm, w_value[...]).astype(jnp.bfloat16).astype(jnp.float32)
            side = layer_norm(other[r, span, :].astype(jnp.float32), gain_one[...])
            keys = dot(side, w_key[...]).astype(jnp.bfloat16).astype(jnp.float32)
            values = dot(side, w_value[...]).astype(jnp.bfloat16).astype(jnp.float32)
            terms = queries * (keys - own_keys)
            upper = terms.astype(jnp.bfloat16)
            lower = (terms - upper.astype(jnp.float32)).astype(jnp.bfloat16)
            shifted = (dot(upper, sums[...]) + dot(lower, sums[...])) * scale
            largest = jnp.maximum(shifted, 0.0)
            own_exp = jnp.exp(-largest)
            side_exp = jnp.exp(shifted - largest)
            mixed = own_exp.astype(jnp.bfloat16).astype(jnp.float32) * own_values
            mixed += side_exp.astype(jnp.bfloat16).astype(jnp.float32) * values
            mixed = (mixed / (own_exp + side_exp)).astype(jnp.bfloat16)
            done = (field + dot(mixed, w_out[...])).astype(jnp.bfloat16)
            attended[r, span, :] = done
            normed[span, :] = layer_norm(done.astype(jnp.float32), gain_two[...])
        spec = dot(table[...], normed[...])
        spec = jnp.where(waves[...] < counts[r], spec, 0.0).astype(jnp.bfloat16)
        sent[r] = spec.reshape(groups, width, feat)
        arrived[r, me] = sent[r, me]
        for t in partners:
            pltpu.make_async_remote_copy(
                src_ref=sent.at[r, t],
                dst_ref=arrived.at[r, me],
                send_sem=fwd_send.at[r],
                recv_sem=fwd_recv.at[r],
                device_id={"grid": t},
                device_id_type=MESH,
            ).start()

    def turn_in(r):
        whole = arrived.at[r, pl.ds(0, groups - 1)]
        pltpu.make_async_copy(whole, whole, fwd_recv.at[r]).wait()
        place = pl.ds(pl.multiple_of(lax.rem(r, nb) * groups, PACK), groups)
        for b in range(packs):
            block = arrived[r, :, b * PACK : (b + 1) * PACK, :].reshape(groups * PACK, feat)
            moved = dot(turn[...], block).astype(jnp.bfloat16)
            turned[b * PACK : (b + 1) * PACK, place, :] = moved.reshape(PACK, groups, feat)

    def lat_in(b, first, count):
        def step(i, _):
            k = first + i
            at = k // each * PACK + lax.rem(k, each)
            pair = jnp.concatenate([turned[at], turned[at + each]], axis=0)
            rows_spec[k] += dot(forward[b], pair)
            return 0

        lax.fori_loop(0, count, step, 0, unroll=4)

    def phase_in(i, _):
        @pl.when(i < rows)
        def _():
            attend(i)

        @pl.when(i >= ARRIVE_LAG)
        def _():
            turn_in(i - ARRIVE_LAG)

        b = (i - ARRIVE_LAG) // nb

        @pl.when((i >= ARRIVE_LAG) & (lax.rem(i - ARRIVE_LAG, nb) == nb - 1) & (b < batches - 1))
        def _():
            lat_in(b, 0, held)

        return 0

    lax.fori_loop(0, rows + ARRIVE_LAG, phase_in, 0)

    mode = second.shape[1] // 2

    def complex_mix(real, imag, layer):
        w_real, w_imag = blocks[2 * layer], blocks[2 * layer + 1]
        return dot(real, w_real) - dot(imag, w_imag), dot(real, w_imag) + dot(imag, w_real)

    def ship(p):
        span = pl.ds(p * each, each)
        return pltpu.make_async_remote_copy(
            src_ref=second.at[span],
            dst_ref=far.at[pl.ds(slot_at * held + p * each, each)],
            send_sem=far_send.at[p],
            recv_sem=far_recv.at[slot_at * packs + p],
            device_id={"grid": relay},
            device_id_type=MESH,
        )

    def mix(p, _):
        lat_in(batches - 1, p * each, each)
        span = pl.ds(p * each, each)
        real = rows_spec[span, :mode].reshape(each * mode, feat).astype(jnp.bfloat16)
        imag = rows_spec[span, mode:].reshape(each * mode, feat).astype(jnp.bfloat16)
        real, imag = complex_mix(real, imag, 0)
        real = jnp.maximum(real, 0.0).astype(jnp.bfloat16)
        imag = jnp.maximum(imag, 0.0).astype(jnp.bfloat16)
        real, imag = complex_mix(real, imag, 1)
        second[span, :mode] = real.astype(jnp.bfloat16).reshape(each, mode, feat)
        second[span, mode:] = imag.astype(jnp.bfloat16).reshape(each, mode, feat)

        @pl.when(inner)
        def _():
            ship(p).start()

        return 0

    lax.fori_loop(0, packs, mix, 0)

    def wait_sent(r, _):
        whole = sent.at[r, pl.ds(0, groups - 1)]
        pltpu.make_async_copy(whole, whole, fwd_send.at[r]).wait()
        return 0

    lax.fori_loop(0, rows, wait_sent, 0)

    pair = PACK // half
    span_in = nb * groups
    span_out = rows * half

    def spread_rows(read, group, p, to_own, buffer, a, b, sem):
        to = side_at if to_own else far_side

        def lat(k, _):
            both = dot(inverse[to], read(k)).astype(jnp.bfloat16)
            for r in range(2):
                for c, start in enumerate(range(0, span_out, span_in)):
                    size = min(span_in, span_out - start)
                    at = r * span_out + start
                    turned[c * PACK + r * each + k, :size] = both[at : at + size]
            return 0

        lax.fori_loop(0, each, lat, 0, unroll=4)
        spot = pl.ds(pl.multiple_of(group * width + p * PACK, PACK), PACK)
        cut = pl.ds(pl.multiple_of(b * PACK, PACK), PACK)

        def send(i, _):
            per = span_in // PACK
            lead = pl.ds(i // per * PACK, PACK)
            block = turned[lead, pl.ds(pl.multiple_of(lax.rem(i, per) * PACK, PACK), PACK), :]
            moved = dot(turn[...], block.reshape(PACK * PACK, feat)).astype(jnp.bfloat16)
            span = pl.ds(i * pair, pair)
            buffer[span, pl.ds(a * half, half), cut, :] = moved.reshape(pair, half, PACK, feat)
            if to_own:
                other[span, spot, :] = buffer[span, a * half + place_at, cut, :]
            for o in range(half - 1, 0 if to_own else -1, -1):
                t = place_at ^ o
                pltpu.make_async_remote_copy(
                    src_ref=buffer.at[span, a * half + t, cut],
                    dst_ref=other.at[span, spot],
                    send_sem=sem,
                    recv_sem=back_recv.at[i],
                    device_id={"grid": to * half + t},
                    device_id_type=MESH,
                ).start()
            return 0

        lax.fori_loop(0, rows // pair, send, 0)

    def own_rows(p, _):
        spread_rows(lambda k: second[p * each + k], me, p, True, sent, 0, p, back_send.at[p])
        return 0

    lax.fori_loop(0, packs, own_rows, 0)

    @pl.when(jnp.logical_not(inner))
    def _():
        pl.semaphore_wait(go_sem, 1)
        for p in range(relayed):
            ship(p).start()
        last = packs - 1
        spread_rows(lambda k: second[last * each + k], me, last, False, sent, 1, last, back_send.at[packs])

    @pl.when(inner)
    def _():
        def relay_rows(q, _):
            u, p = q // packs, lax.rem(q, packs)
            group = (1 + far_side + u * (2 * far_side - 1)) * quarter + lane_at
            base = u * held + p * each
            got = far.at[pl.ds(base, each)]
            pltpu.make_async_copy(got, got, far_recv.at[q]).wait()

            @pl.when(q == packs - 1)
            def _():
                for each_pack in range(packs):
                    ship(each_pack).wait_send()
                pl.semaphore_signal(go_sem, inc=1, device_id={"grid": outer}, device_id_type=MESH)

            sem = back_send.at[packs + 1 + q]
            spread_rows(lambda k: far[base + k], group, p, True, arrived, u, p, sem)
            return 0

        lax.fori_loop(0, packs + relayed, relay_rows, 0)

    def finish(j):
        weight = jnp.where(waves[...] == 0, 1.0, 2.0)
        weight = jnp.where(waves[...] < counts[j], weight, 0.0)
        spec = (other[j].astype(jnp.float32) * weight).astype(jnp.bfloat16)
        total = attended[j].astype(jnp.float32) + dot(back_table[...], spec)
        attended[j] = total.astype(jnp.bfloat16)

    def phase_out(i, _):
        span = pl.ds(i * pair, pair)

        @pl.when(inner)
        def _():
            whole = other.at[span, pl.ds(0, (groups - 1) * width - (packs + relayed) * PACK)]
            pltpu.make_async_copy(whole, whole, back_recv.at[i]).wait()

        @pl.when(jnp.logical_not(inner))
        def _():
            whole = other.at[span, pl.ds(0, (groups - 1) * width)]
            pltpu.make_async_copy(whole, whole, back_recv.at[i]).wait()

        for r in range(pair):
            finish(i * pair + r)
        return 0

    lax.fori_loop(0, rows // pair, phase_out, 0)

    def drain(r, _):
        pltpu.make_async_copy(fields.at[r], fields.at[r], swap_send.at[r]).wait()
        return 0

    lax.fori_loop(0, rows, drain, 0)
    most = sent.at[:, pl.ds(0, half), pl.ds(0, PACK)]
    fewer = sent.at[:, pl.ds(0, half - 1), pl.ds(0, PACK)]
    for p in range(packs):
        pltpu.make_async_copy(fewer, fewer, back_send.at[p]).wait()

    @pl.when(inner)
    def _():
        for q in range(packs + relayed):
            pltpu.make_async_copy(fewer, fewer, back_send.at[packs + 1 + q]).wait()

    @pl.when(jnp.logical_not(inner))
    def _():
        for p in range(relayed):
            ship(p).wait_send()
        pltpu.make_async_copy(most, most, back_send.at[packs]).wait()


def fused(mesh_sizes, fields, mode_counts, gain_attn, w_query, w_key, w_value, w_out, gain_spec, w_first, w_second):
    _, groups = mesh_sizes
    fields = fields[0]
    rows, points, feat = fields.shape
    width = 2 * KLON // groups
    held = width // 2
    nb = max(n for n in range(1, rows + 1) if rows % n == 0 and 2 * n * groups <= max(feat, 2 * groups))
    forward, inverse = np_lat_tables(groups, rows // nb, nb)
    turn = np_turn(groups)
    block = w_first.shape[-1]
    lanes = np.arange(feat)
    heads = jnp.asarray((lanes[:, None] // HEAD == lanes[None, :] // HEAD).astype(np.float32), dtype=jnp.bfloat16)
    spread = jnp.asarray((np.arange(block)[:, None] == lanes[None, :] % block).astype(np.float32), dtype=jnp.bfloat16)
    waves = jnp.asarray(np_wave_order(groups)[1][:, None], dtype=jnp.int32)
    operands = [
        mode_counts, fields, gain_attn[None, :], w_query, w_key, w_value, w_out, gain_spec[None, :],
        np_lon_forward(points, groups), heads, waves, forward, inverse, turn, spread,
        w_first.reshape(2, feat, block), w_second.reshape(2, feat, block),
    ]
    hbm = pl.BlockSpec(memory_space=pl.ANY)
    specs = [pl.BlockSpec(memory_space=pltpu.SMEM)] + [hbm] * (len(operands) - 1)
    held_operands = operands[2:]
    sub = points // 3 if points % 48 == 0 else points
    half = jnp.bfloat16
    dma = pltpu.SemaphoreType.DMA
    out = pl.pallas_call(
        functools.partial(enter_kernel, sub, nb, len(held_operands)),
        in_specs=specs,
        out_specs=pl.BlockSpec(memory_space=pltpu.VMEM),
        out_shape=pltpu.VMEM((rows, points, feat), half),
        scratch_shapes=[pltpu.VMEM(o.shape, o.dtype) for o in held_operands]
        + [
            pltpu.VMEM((2, points, feat), half),
            pltpu.VMEM((rows, points, feat), half),
            pltpu.VMEM((rows, groups, width, feat), half),
            pltpu.VMEM((rows, groups, width, feat), half),
            pltpu.VMEM((width, nb * groups, feat), half),
            pltpu.VMEM((held, 2 * KLAT, feat), jnp.float32),
            pltpu.VMEM((held, 2 * KLAT, feat), half),
            pltpu.VMEM((2 * held - PACK // 2, 2 * KLAT, feat), half),
            pltpu.VMEM((points, feat), half),
            pltpu.VMEM((points, 2 * KLON), half),
            pltpu.VMEM((4, feat, feat), half),
            dma((2,)),
            dma((rows,)),
            dma((rows * (points // sub),)),
            dma((rows,)),
            dma((rows,)),
            dma((width // PACK,)),
            dma((2 * (width // PACK) - 1,)),
            dma((3 * (width // PACK),)),
            dma((rows // 2,)),
            pltpu.SemaphoreType.REGULAR,
            dma((len(held_operands),)),
        ],
        compiler_params=pltpu.CompilerParams(
            collective_id=0, has_side_effects=True, vmem_limit_bytes=67043328 - rows * points * feat * 2
        ),
        name="layer",
    )(*operands)
    return out[None]


def streams(members, groups, lat_dev, points, feat):
    width = 2 * KLON // groups
    return (
        members == 2
        and groups == PACK
        and (2 * KLON) % (groups * PACK) == 0
        and points == 2 * KLON
        and feat % 128 == 0
        and lat_dev % 2 == 0
        and width % PACK == 0
        and width > PACK
    )


def layer(mesh_sizes, *args):
    if streams(*mesh_sizes, *args[0].shape[1:]):
        return fused(mesh_sizes, *args)
    return shards(mesh_sizes, *args)


def solution(mesh):
    in_specs = (P("ens", "grid", None, None), P("grid"), P(), P(), P(), P(), P(), P(), P(), P())
    out_specs = P("ens", "grid", None, None)
    sizes = (mesh.shape["ens"], mesh.shape["grid"])
    return jax.shard_map(
        functools.partial(layer, sizes),
        mesh=mesh,
        in_specs=in_specs,
        out_specs=out_specs,
        check_vma=False,
    )
```

```python
import functools
import math

import jax
import jax.numpy as jnp
import numpy as np
from jax import lax
from jax.experimental import pallas as pl
from jax.experimental.pallas import tpu as pltpu
from jax.sharding import PartitionSpec as P

HEAD = 32
NLAT = 384
KLON = 384
KLAT = 128
CHUNKS = 6
BACK_CHUNKS = 2

MESH = pl.DeviceIdType.MESH
SWAP_AHEAD = 6
ARRIVE_LAG = 3
PACK = 16

norm_eps = 1e-05


def layer_norm(widened, gain_vec):
    center = widened - jnp.mean(widened, axis=-1, keepdims=True)
    spread = jnp.mean(center * center, axis=-1, keepdims=True)
    return (center * lax.rsqrt(spread + norm_eps) * gain_vec).astype(jnp.bfloat16)


def wave_order(groups):
    held = KLON // groups
    place = jnp.arange(2 * KLON, dtype=jnp.int32)
    part = place // held % 2
    wave = place // (2 * held) * held + place % held
    return part, wave


def lon_forward(points, groups):
    part, wave = wave_order(groups)
    positions = jnp.arange(points, dtype=jnp.int32)
    turn_count = wave[:, None] * positions[None, :] % points
    angles = 2.0 * math.pi / points * turn_count.astype(jnp.float32)
    factor = 1.0 / math.sqrt(points)
    return jnp.where(
        part[:, None] == 0, jnp.cos(angles) * factor, -jnp.sin(angles) * factor
    ).astype(jnp.bfloat16)


def lon_inverse(points, groups):
    part, wave = wave_order(groups)
    positions = jnp.arange(points, dtype=jnp.int32)
    turn_count = positions[:, None] * wave[None, :] % points
    angles = 2.0 * math.pi / points * turn_count.astype(jnp.float32)
    weight = jnp.where(wave == 0, 1.0, 2.0).astype(jnp.float32)[None, :] / math.sqrt(points)
    return jnp.where(
        part[None, :] == 0, jnp.cos(angles) * weight, -jnp.sin(angles) * weight
    ).astype(jnp.bfloat16)


def lat_angles(row_count, mode_count):
    frequency = jnp.arange(mode_count, dtype=jnp.int32)
    frequency = jnp.where(frequency < mode_count // 2, frequency, frequency - mode_count)
    positions = jnp.arange(row_count, dtype=jnp.int32)
    turn_count = frequency[:, None] * positions[None, :] % row_count
    return 2.0 * math.pi / row_count * turn_count.astype(jnp.float32)


def lat_forward(row_count, mode_count):
    angles = lat_angles(row_count, mode_count)
    factor = 1.0 / math.sqrt(row_count)
    cosine = jnp.cos(angles) * factor
    sine_part = jnp.sin(angles) * factor
    return jnp.stack(
        [jnp.stack([cosine, sine_part], axis=1), jnp.stack([-sine_part, cosine], axis=1)]
    ).astype(jnp.bfloat16)


def lat_inverse(row_count, mode_count):
    angles = jnp.transpose(lat_angles(row_count, mode_count))
    factor = 1.0 / math.sqrt(row_count)
    cosine = jnp.cos(angles) * factor
    sine_part = jnp.sin(angles) * factor
    return jnp.stack([jnp.stack([cosine, -sine_part]), jnp.stack([sine_part, cosine])]).astype(
        jnp.bfloat16
    )


def complex_blocks(weight):
    real_part = weight[0]
    imag_part = weight[1]
    return jnp.stack([jnp.stack([real_part, imag_part]), jnp.stack([-imag_part, real_part])])


def mix_blocks(spec, big):
    blocks = spec.reshape(spec.shape[:3] + (big.shape[2], big.shape[3]))
    out_blocks = jnp.einsum("pqkbi,psbio->sqkbo", blocks, big, preferred_element_type=jnp.float32)
    return out_blocks.reshape(spec.shape)


def dot(left, right):
    return jnp.dot(left, right, preferred_element_type=jnp.float32)


def attend_kernel(others, first_row, sub, counts, own, *refs):
    other_refs = refs[:others]
    (gain_one, w_qkv, w_out, gain_two, table, sums, waves, attended, spectrum, normed) = refs[others:]
    points, feat = own.shape[1:]
    scale = 1.0 / math.sqrt(HEAD)
    for start in range(0, points, sub):
        rows = pl.ds(start, sub)
        fields = own[0, rows, :].astype(jnp.float32)
        joined = dot(layer_norm(fields, gain_one[...]), w_qkv[...]).astype(jnp.bfloat16)
        queries = joined[:, :feat].astype(jnp.float32)
        own_keys = joined[:, feat : 2 * feat].astype(jnp.float32)
        values = [joined[:, 2 * feat :].astype(jnp.float32)]
        shifted = [jnp.zeros((sub, feat), jnp.float32)]
        for ref in other_refs:
            side = layer_norm(ref[0, rows, :].astype(jnp.float32), gain_one[...])
            pair = dot(side, w_qkv[:, feat:]).astype(jnp.bfloat16)
            terms = queries * (pair[:, :feat].astype(jnp.float32) - own_keys)
            upper = terms.astype(jnp.bfloat16)
            lower = (terms - upper.astype(jnp.float32)).astype(jnp.bfloat16)
            total = dot(upper, sums[...]) + dot(lower, sums[...])
            shifted.append(total * scale)
            values.append(pair[:, feat:].astype(jnp.float32))
        largest = functools.reduce(jnp.maximum, shifted)
        exps = [jnp.exp(item - largest) for item in shifted]
        totals = functools.reduce(jnp.add, exps)
        mixed = functools.reduce(
            jnp.add,
            [e.astype(jnp.bfloat16).astype(jnp.float32) * v for e, v in zip(exps, values)],
        )
        mixed = (mixed / totals).astype(jnp.bfloat16)
        result = (fields + dot(mixed, w_out[...])).astype(jnp.bfloat16)
        attended[0, rows, :] = result
        normed[rows, :] = layer_norm(result.astype(jnp.float32), gain_two[...])
    kept = waves[...] < counts[first_row + pl.program_id(0)]
    spec = dot(table[...], normed[...])
    spec = jnp.where(kept, spec, 0.0).astype(jnp.bfloat16)
    if len(spectrum.shape) == 4:
        spectrum[:, 0] = spec.reshape(spectrum.shape[0], spectrum.shape[2], feat)
    else:
        spectrum[0] = spec


def attend(chunk, rows, aligned, groups, fields, others, counts, gains, weights, tables):
    points, feat = fields.shape[1:]
    first_row = chunk * rows
    sub = points // 3 if points % 48 == 0 else points
    whole = lambda a: pl.BlockSpec(a.shape, lambda i, c: (0,) * a.ndim)
    w_qkv, w_out = weights
    table, sums, waves = tables
    held = 2 * KLON // groups
    if aligned:
        spec_shape = (groups, rows, held, feat)
        spec_block = pl.BlockSpec((groups, 1, held, feat), lambda i, c: (0, i, 0, 0))
    else:
        spec_shape = (rows, 2 * KLON, feat)
        spec_block = pl.BlockSpec((1, 2 * KLON, feat), lambda i, c: (i, 0, 0))
    row_block = pl.BlockSpec((1, points, feat), lambda i, c: (i, 0, 0))
    own_block = pl.BlockSpec((1, points, feat), lambda i, c: (first_row + i, 0, 0))
    params = (gains[0], w_qkv, w_out, gains[1], table, sums, waves)
    flops = 2 * rows * points * feat * (feat * 8 + 2 * KLON)
    attended, spectrum = pl.pallas_call(
        functools.partial(attend_kernel, len(others), first_row, sub),
        grid_spec=pltpu.PrefetchScalarGridSpec(
            num_scalar_prefetch=1,
            grid=(rows,),
            in_specs=[own_block] + [row_block] * len(others) + [whole(p) for p in params],
            out_specs=[row_block, spec_block],
            scratch_shapes=[pltpu.VMEM((points, feat), jnp.bfloat16)],
        ),
        out_shape=[
            jax.ShapeDtypeStruct((rows, points, feat), jnp.bfloat16),
            jax.ShapeDtypeStruct(spec_shape, jnp.bfloat16),
        ],
        cost_estimate=pl.CostEstimate(
            flops=flops, bytes_accessed=rows * points * feat * 8, transcendentals=rows * points * feat * 2
        ),
        compiler_params=pltpu.CompilerParams(vmem_limit_bytes=40 * 1024 * 1024),
    )(counts, fields, *others, *params)
    if not aligned:
        spectrum = jnp.transpose(spectrum.reshape(rows, groups, held, feat), (1, 0, 2, 3))
    return attended, spectrum


def finish_kernel(first_row, counts, spectrum, attended, table, waves, *refs):
    out = refs[-1]
    feat = out.shape[-1]
    kept = waves[...] < counts[first_row + pl.program_id(0)]
    if len(spectrum.shape) == 4:
        spec = spectrum[:, 0].reshape(2 * KLON, feat)
    else:
        spec = spectrum[0]
    spec = jnp.where(kept, spec.astype(jnp.float32), 0.0).astype(jnp.bfloat16)
    out[0] = (attended[0].astype(jnp.float32) + dot(table[...], spec)).astype(jnp.bfloat16)


def finish(first_row, offset, lat_dev, aligned, groups, spectrum, attended, counts, table, waves, so_far):
    rows, points, feat = attended.shape
    held = 2 * KLON // groups
    whole = lambda a: pl.BlockSpec(a.shape, lambda i, c: (0,) * a.ndim)
    if aligned:
        spec_block = pl.BlockSpec((groups, 1, held, feat), lambda i, c: (0, offset + i, 0, 0))
    else:
        spectrum = jnp.transpose(spectrum, (1, 0, 2, 3)).reshape(-1, 2 * KLON, feat)
        spec_block = pl.BlockSpec((1, 2 * KLON, feat), lambda i, c: (offset + i, 0, 0))
    row_block = pl.BlockSpec((1, points, feat), lambda i, c: (i, 0, 0))
    out_block = pl.BlockSpec((1, points, feat), lambda i, c: (first_row + i, 0, 0))
    operands = [counts, spectrum, attended, table, waves]
    specs = [spec_block, row_block, whole(table), whole(waves)]
    aliases = {}
    if so_far is not None:
        aliases = {len(operands): 0}
        operands.append(so_far)
        specs.append(pl.BlockSpec(memory_space=pl.ANY))
    return pl.pallas_call(
        functools.partial(finish_kernel, first_row),
        grid_spec=pltpu.PrefetchScalarGridSpec(
            num_scalar_prefetch=1, grid=(rows,), in_specs=specs, out_specs=out_block
        ),
        out_shape=jax.ShapeDtypeStruct((lat_dev, points, feat), jnp.bfloat16),
        input_output_aliases=aliases,
        cost_estimate=pl.CostEstimate(
            flops=4 * rows * points * feat * KLON,
            bytes_accessed=rows * points * feat * 6,
            transcendentals=0,
        ),
        compiler_params=pltpu.CompilerParams(vmem_limit_bytes=40 * 1024 * 1024),
    )(*operands)


def shards(
    mesh_sizes, fields, mode_counts, gain_attn, w_query, w_key, w_value, w_out, gain_spec, w_first, w_second
):
    members, groups = mesh_sizes
    fields = fields[0]
    lat_dev, points, feat = fields.shape
    held = KLON // groups
    aligned = (2 * held) % 16 == 0
    chunks = max(c for c in range(1, CHUNKS + 1) if lat_dev % c == 0)
    rows = lat_dev // chunks
    shifts = [
        [(i, (i + s) % members) for i in range(members)] for s in range(1, members)
    ]
    others = []
    for c in range(chunks):
        others.append([lax.ppermute(fields[c * rows : (c + 1) * rows], "ens", s) for s in shifts])
    w_qkv = jnp.concatenate([w_query, w_key, w_value], axis=1)
    lanes = jnp.arange(feat, dtype=jnp.int32) // HEAD
    sums = (lanes[:, None] == lanes[None, :]).astype(jnp.bfloat16)
    waves = wave_order(groups)[1][:, None]
    gains = (gain_attn[None, :], gain_spec[None, :])
    tables = (lon_forward(points, groups), sums, waves)
    back_table = lon_inverse(points, groups)
    forward = lat_forward(NLAT, KLAT).reshape(2, KLAT, 2, groups, chunks, rows)
    backs = max(c for c in range(1, BACK_CHUNKS + 1) if chunks % c == 0)
    per_back = chunks // backs
    inverse = lat_inverse(NLAT, KLAT).reshape(2, 2, groups, backs, per_back * rows, KLAT)
    big_one = complex_blocks(w_first)
    big_two = complex_blocks(w_second)
    kept_fields = []
    rows_spec = None
    for c in range(chunks):
        attended, spectrum = attend(
            c, rows, aligned, groups, fields, others[c], mode_counts, gains, (w_qkv, w_out), tables
        )
        kept_fields.append(attended)
        arrived = lax.all_to_all(spectrum, "grid", split_axis=0, concat_axis=0)
        arrived = arrived.reshape(groups, rows, 2, held, feat)
        term = jnp.einsum(
            "pqrgj,gjrkd->pqkd",
            forward[:, :, :, :, c],
            arrived,
            preferred_element_type=jnp.float32,
        )
        rows_spec = term if rows_spec is None else rows_spec + term
        if c < chunks - 1:
            rows_spec = lax.optimization_barrier(rows_spec)
    rows_spec = rows_spec.astype(jnp.bfloat16)
    hidden = jnp.maximum(mix_blocks(rows_spec, big_one), 0.0).astype(jnp.bfloat16)
    second = mix_blocks(hidden, big_two).astype(jnp.bfloat16)
    out = None
    for b in range(backs):
        back_rows = jnp.einsum(
            "rpgjq,pqkd->gjrkd", inverse[:, :, :, b], second, preferred_element_type=jnp.float32
        ).astype(jnp.bfloat16)
        returned = lax.all_to_all(
            back_rows.reshape(groups, per_back * rows, 2 * held, feat), "grid", split_axis=0, concat_axis=0
        )
        for i in range(per_back):
            c = b * per_back + i
            out = finish(
                c * rows, i * rows, lat_dev, aligned, groups, returned, kept_fields[c], mode_counts,
                back_table, tables[2], out,
            )
    return out[None]


def np_wave_order(groups):
    held = KLON // groups
    each = PACK // 2
    place = np.arange(2 * KLON)
    group, pack, within = place // (2 * held), place % (2 * held) // PACK, place % each
    return place // each % 2, group * held + pack * each + within


def np_lon_forward(points, groups):
    part, wave = np_wave_order(groups)
    turns = wave[:, None] * np.arange(points)[None, :] % points
    angles = 2.0 * math.pi / points * turns
    rows = np.where(part[:, None] == 0, np.cos(angles), -np.sin(angles)) / math.sqrt(points)
    return jnp.asarray(rows.astype(np.float32), dtype=jnp.bfloat16)


def np_lat_tables(groups, batches, nb):
    frequency = np.arange(KLAT)
    frequency = np.where(frequency < KLAT // 2, frequency, frequency - KLAT)
    angles = 2.0 * math.pi / NLAT * (frequency[:, None] * np.arange(NLAT)[None, :] % NLAT)
    cosine = np.cos(angles) / math.sqrt(NLAT)
    sine = np.sin(angles) / math.sqrt(NLAT)
    both = np.stack([np.stack([cosine, sine], axis=1), np.stack([-sine, cosine], axis=1)])
    forward = both.reshape(2, KLAT, 2, groups, batches, nb).transpose(4, 0, 1, 2, 5, 3)
    forward = forward.reshape(batches, 2 * KLAT, 2 * nb * groups).astype(np.float32)
    inverse = both.reshape(2, KLAT, 2, 2, groups // 2, batches * nb).transpose(3, 2, 5, 4, 0, 1)
    inverse = inverse.reshape(2, batches * nb * groups, 2 * KLAT).astype(np.float32)
    return jnp.asarray(forward, dtype=jnp.bfloat16), jnp.asarray(inverse, dtype=jnp.bfloat16)


def np_turn(groups):
    count = groups * PACK
    source = np.arange(count).reshape(groups, PACK).T.reshape(-1)
    turn = np.zeros((count, count), np.float32)
    turn[np.arange(count), source] = 1.0
    return jnp.asarray(turn, dtype=jnp.bfloat16)


def enter_kernel(points_sub, nb, held_count, counts, fields, *refs):
    sources, out, held_refs = refs[:held_count], refs[held_count], refs[held_count + 1 : 2 * held_count + 1]
    rest, sems = refs[2 * held_count + 1 : -1], refs[-1]
    copies = [
        pltpu.make_async_copy(source, target, sems.at[i])
        for i, (source, target) in enumerate(zip(sources, held_refs))
    ]
    for copy in copies:
        copy.start()
    layer_kernel(points_sub, nb, copies, counts, fields, *held_refs, out, *rest)


def layer_kernel(
    points_sub,
    nb,
    copies,
    counts,
    fields,
    gain_one,
    w_query,
    w_key,
    w_value,
    w_out,
    gain_two,
    table,
    sums,
    waves,
    forward,
    inverse,
    turn,
    spread,
    w_first,
    w_second,
    attended,
    own,
    other,
    sent,
    arrived,
    turned,
    rows_spec,
    second,
    far,
    normed,
    back_table,
    blocks,
    own_sem,
    swap_send,
    swap_recv,
    fwd_send,
    fwd_recv,
    far_send,
    far_recv,
    back_send,
    back_recv,
    go_sem,
):
    rows, groups, width, feat = sent.shape
    points = other.shape[1]
    held = width // 2
    packs = width // PACK
    batches = rows // nb
    sub = points_sub
    member = lax.axis_index("ens")
    me = lax.axis_index("grid")
    scale = 1.0 / math.sqrt(HEAD)
    partners = [me ^ o for o in range(groups - 1, 0, -1)]
    each = PACK // 2
    half = groups // 2
    quarter = groups // 4
    side_at = me // half
    far_side = 1 - side_at
    place_at = lax.rem(me, half)
    lane_at = lax.rem(me, quarter)
    inner = me // quarter == 1 + side_at
    relay = (1 + far_side) * quarter + lane_at
    outer = 3 * side_at * quarter + lane_at
    slot_at = jnp.where(inner, 0, 1)
    relayed = packs - 1

    barrier = pltpu.get_barrier_semaphore()
    for t in partners:
        pl.semaphore_signal(barrier, inc=1, device_id={"grid": t}, device_id_type=MESH)
    pl.semaphore_signal(barrier, inc=1, device_id={"ens": 1 - member}, device_id_type=MESH)
    pl.semaphore_wait(barrier, groups)

    thirds = points // sub

    def swap(r, s):
        span = pl.ds(s * sub, sub)
        return pltpu.make_async_remote_copy(
            src_ref=fields.at[r, span],
            dst_ref=other.at[r, span],
            send_sem=swap_send.at[r],
            recv_sem=swap_recv.at[r * thirds + s],
            device_id={"ens": 1 - member},
            device_id_type=MESH,
        )

    def fetch(r, slot):
        return pltpu.make_async_copy(fields.at[r], own.at[slot], own_sem.at[slot])

    ahead = min(SWAP_AHEAD, rows)
    for r in range(ahead):
        for s in range(thirds):
            swap(r, s).start()
    fetch(0, 0).start()
    for copy in copies:
        copy.wait()

    eye = lax.broadcasted_iota(jnp.int32, (feat, feat), 0) // HEAD
    same = eye == lax.broadcasted_iota(jnp.int32, (feat, feat), 1) // HEAD
    for layer, weight in enumerate((w_first, w_second)):
        for part in range(2):
            wide = dot(weight[part], spread[...])
            blocks[2 * layer + part] = jnp.where(same, wide, 0.0).astype(jnp.bfloat16)
    back_table[...] = jnp.transpose(table[...])
    rows_spec[...] = jnp.zeros_like(rows_spec)

    def attend(r):
        slot = lax.rem(r, 2)
        fetch(r, slot).wait()

        @pl.when(r + 1 < rows)
        def _():
            fetch(r + 1, 1 - slot).start()

        @pl.when(r + ahead < rows)
        def _():
            for s in range(thirds):
                swap(r + ahead, s).start()

        for s in range(thirds):
            swap(r, s).wait_recv()
            span = pl.ds(s * sub, sub)
            field = own[slot, span, :].astype(jnp.float32)
            norm = layer_norm(field, gain_one[...])
            queries = dot(norm, w_query[...]).astype(jnp.bfloat16).astype(jnp.float32)
            own_keys = dot(norm, w_key[...]).astype(jnp.bfloat16).astype(jnp.float32)
            own_values = dot(norm, w_value[...]).astype(jnp.bfloat16).astype(jnp.float32)
            side = layer_norm(other[r, span, :].astype(jnp.float32), gain_one[...])
            keys = dot(side, w_key[...]).astype(jnp.bfloat16).astype(jnp.float32)
            values = dot(side, w_value[...]).astype(jnp.bfloat16).astype(jnp.float32)
            terms = queries * (keys - own_keys)
            upper = terms.astype(jnp.bfloat16)
            lower = (terms - upper.astype(jnp.float32)).astype(jnp.bfloat16)
            shifted = (dot(upper, sums[...]) + dot(lower, sums[...])) * scale
            largest = jnp.maximum(shifted, 0.0)
            own_exp = jnp.exp(-largest)
            side_exp = jnp.exp(shifted - largest)
            mixed = own_exp.astype(jnp.bfloat16).astype(jnp.float32) * own_values
            mixed += side_exp.astype(jnp.bfloat16).astype(jnp.float32) * values
            mixed = (mixed / (own_exp + side_exp)).astype(jnp.bfloat16)
            done = (field + dot(mixed, w_out[...])).astype(jnp.bfloat16)
            attended[r, span, :] = done
            normed[span, :] = layer_norm(done.astype(jnp.float32), gain_two[...])
        spec = dot(table[...], normed[...])
        spec = jnp.where(waves[...] < counts[r], spec, 0.0).astype(jnp.bfloat16)
        sent[r] = spec.reshape(groups, width, feat)
        arrived[r, me] = sent[r, me]
        for t in partners:
            pltpu.make_async_remote_copy(
                src_ref=sent.at[r, t],
                dst_ref=arrived.at[r, me],
                send_sem=fwd_send.at[r],
                recv_sem=fwd_recv.at[r],
                device_id={"grid": t},
                device_id_type=MESH,
            ).start()

    def turn_in(r):
        whole = arrived.at[r, pl.ds(0, groups - 1)]
        pltpu.make_async_copy(whole, whole, fwd_recv.at[r]).wait()
        place = pl.ds(pl.multiple_of(lax.rem(r, nb) * groups, PACK), groups)
        for b in range(packs):
            block = arrived[r, :, b * PACK : (b + 1) * PACK, :].reshape(groups * PACK, feat)
            moved = dot(turn[...], block).astype(jnp.bfloat16)
            turned[b * PACK : (b + 1) * PACK, place, :] = moved.reshape(PACK, groups, feat)

    def lat_in(b, first, count):
        def step(i, _):
            k = first + i
            at = k // each * PACK + lax.rem(k, each)
            pair = jnp.concatenate([turned[at], turned[at + each]], axis=0)
            rows_spec[k] += dot(forward[b], pair)
            return 0

        lax.fori_loop(0, count, step, 0, unroll=8)

    def phase_in(i, _):
        @pl.when(i < rows)
        def _():
            attend(i)

        @pl.when(i >= ARRIVE_LAG)
        def _():
            turn_in(i - ARRIVE_LAG)

        b = (i - ARRIVE_LAG) // nb

        @pl.when((i >= ARRIVE_LAG) & (lax.rem(i - ARRIVE_LAG, nb) == nb - 1) & (b < batches - 1))
        def _():
            lat_in(b, 0, held)

        return 0

    lax.fori_loop(0, rows + ARRIVE_LAG, phase_in, 0)

    mode = second.shape[1] // 2

    def complex_mix(real, imag, layer):
        w_real, w_imag = blocks[2 * layer], blocks[2 * layer + 1]
        return dot(real, w_real) - dot(imag, w_imag), dot(real, w_imag) + dot(imag, w_real)

    def ship(p):
        span = pl.ds(p * each, each)
        return pltpu.make_async_remote_copy(
            src_ref=second.at[span],
            dst_ref=far.at[pl.ds(slot_at * held + p * each, each)],
            send_sem=far_send.at[p],
            recv_sem=far_recv.at[slot_at * packs + p],
            device_id={"grid": relay},
            device_id_type=MESH,
        )

    def mix(p, _):
        lat_in(batches - 1, p * each, each)
        span = pl.ds(p * each, each)
        real = rows_spec[span, :mode].reshape(each * mode, feat).astype(jnp.bfloat16)
        imag = rows_spec[span, mode:].reshape(each * mode, feat).astype(jnp.bfloat16)
        real, imag = complex_mix(real, imag, 0)
        real = jnp.maximum(real, 0.0).astype(jnp.bfloat16)
        imag = jnp.maximum(imag, 0.0).astype(jnp.bfloat16)
        real, imag = complex_mix(real, imag, 1)
        second[span, :mode] = real.astype(jnp.bfloat16).reshape(each, mode, feat)
        second[span, mode:] = imag.astype(jnp.bfloat16).reshape(each, mode, feat)

        @pl.when(inner)
        def _():
            ship(p).start()

        return 0

    lax.fori_loop(0, packs, mix, 0)

    def wait_sent(r, _):
        whole = sent.at[r, pl.ds(0, groups - 1)]
        pltpu.make_async_copy(whole, whole, fwd_send.at[r]).wait()
        return 0

    lax.fori_loop(0, rows, wait_sent, 0)

    pair = PACK // half
    span_in = nb * groups
    span_out = rows * half

    def spread_rows(read, group, p, to_own, buffer, a, b, sem):
        to = side_at if to_own else far_side

        def lat(k, _):
            both = dot(inverse[to], read(k)).astype(jnp.bfloat16)
            for r in range(2):
                for c, start in enumerate(range(0, span_out, span_in)):
                    size = min(span_in, span_out - start)
                    at = r * span_out + start
                    turned[c * PACK + r * each + k, :size] = both[at : at + size]
            return 0

        lax.fori_loop(0, each, lat, 0, unroll=8)
        spot = pl.ds(pl.multiple_of(group * width + p * PACK, PACK), PACK)
        cut = pl.ds(pl.multiple_of(b * PACK, PACK), PACK)

        def send(i, _):
            per = span_in // PACK
            lead = pl.ds(i // per * PACK, PACK)
            block = turned[lead, pl.ds(pl.multiple_of(lax.rem(i, per) * PACK, PACK), PACK), :]
            moved = dot(turn[...], block.reshape(PACK * PACK, feat)).astype(jnp.bfloat16)
            span = pl.ds(i * pair, pair)
            buffer[span, pl.ds(a * half, half), cut, :] = moved.reshape(pair, half, PACK, feat)
            if to_own:
                other[span, spot, :] = buffer[span, a * half + place_at, cut, :]
            for o in range(half - 1, 0 if to_own else -1, -1):
                t = place_at ^ o
                pltpu.make_async_remote_copy(
                    src_ref=buffer.at[span, a * half + t, cut],
                    dst_ref=other.at[span, spot],
                    send_sem=sem,
                    recv_sem=back_recv.at[i],
                    device_id={"grid": to * half + t},
                    device_id_type=MESH,
                ).start()
            return 0

        lax.fori_loop(0, rows // pair, send, 0, unroll=2)

    def own_rows(p, _):
        spread_rows(lambda k: second[p * each + k], me, p, True, sent, 0, p, back_send.at[p])
        return 0

    lax.fori_loop(0, packs, own_rows, 0)

    @pl.when(jnp.logical_not(inner))
    def _():
        pl.semaphore_wait(go_sem, 1)
        for p in range(relayed):
            ship(p).start()
        last = packs - 1
        spread_rows(lambda k: second[last * each + k], me, last, False, sent, 1, last, back_send.at[packs])

    @pl.when(inner)
    def _():
        def relay_rows(q, _):
            u, p = q // packs, lax.rem(q, packs)
            group = (1 + far_side + u * (2 * far_side - 1)) * quarter + lane_at
            base = u * held + p * each
            got = far.at[pl.ds(base, each)]
            pltpu.make_async_copy(got, got, far_recv.at[q]).wait()

            @pl.when(q == packs - 1)
            def _():
                for each_pack in range(packs):
                    ship(each_pack).wait_send()
                pl.semaphore_signal(go_sem, inc=1, device_id={"grid": outer}, device_id_type=MESH)

            sem = back_send.at[packs + 1 + q]
            spread_rows(lambda k: far[base + k], group, p, True, arrived, u, p, sem)
            return 0

        lax.fori_loop(0, packs + relayed, relay_rows, 0)

    def finish(j):
        weight = jnp.where(waves[...] == 0, 1.0, 2.0)
        weight = jnp.where(waves[...] < counts[j], weight, 0.0)
        spec = (other[j].astype(jnp.float32) * weight).astype(jnp.bfloat16)
        total = attended[j].astype(jnp.float32) + dot(back_table[...], spec)
        attended[j] = total.astype(jnp.bfloat16)

    def phase_out(i, _):
        span = pl.ds(i * pair, pair)

        @pl.when(inner)
        def _():
            whole = other.at[span, pl.ds(0, (groups - 1) * width - (packs + relayed) * PACK)]
            pltpu.make_async_copy(whole, whole, back_recv.at[i]).wait()

        @pl.when(jnp.logical_not(inner))
        def _():
            whole = other.at[span, pl.ds(0, (groups - 1) * width)]
            pltpu.make_async_copy(whole, whole, back_recv.at[i]).wait()

        for r in range(pair):
            finish(i * pair + r)
        return 0

    lax.fori_loop(0, rows // pair, phase_out, 0)

    def drain(r, _):
        pltpu.make_async_copy(fields.at[r], fields.at[r], swap_send.at[r]).wait()
        return 0

    lax.fori_loop(0, rows, drain, 0)
    most = sent.at[:, pl.ds(0, half), pl.ds(0, PACK)]
    fewer = sent.at[:, pl.ds(0, half - 1), pl.ds(0, PACK)]
    for p in range(packs):
        pltpu.make_async_copy(fewer, fewer, back_send.at[p]).wait()

    @pl.when(inner)
    def _():
        for q in range(packs + relayed):
            pltpu.make_async_copy(fewer, fewer, back_send.at[packs + 1 + q]).wait()

    @pl.when(jnp.logical_not(inner))
    def _():
        for p in range(relayed):
            ship(p).wait_send()
        pltpu.make_async_copy(most, most, back_send.at[packs]).wait()


def fused(mesh_sizes, fields, mode_counts, gain_attn, w_query, w_key, w_value, w_out, gain_spec, w_first, w_second):
    _, groups = mesh_sizes
    fields = fields[0]
    rows, points, feat = fields.shape
    width = 2 * KLON // groups
    held = width // 2
    nb = max(n for n in range(1, rows + 1) if rows % n == 0 and 2 * n * groups <= max(feat, 2 * groups))
    forward, inverse = np_lat_tables(groups, rows // nb, nb)
    turn = np_turn(groups)
    block = w_first.shape[-1]
    lanes = np.arange(feat)
    heads = jnp.asarray((lanes[:, None] // HEAD == lanes[None, :] // HEAD).astype(np.float32), dtype=jnp.bfloat16)
    spread = jnp.asarray((np.arange(block)[:, None] == lanes[None, :] % block).astype(np.float32), dtype=jnp.bfloat16)
    waves = jnp.asarray(np_wave_order(groups)[1][:, None], dtype=jnp.int32)
    operands = [
        mode_counts, fields, gain_attn[None, :], w_query, w_key, w_value, w_out, gain_spec[None, :],
        np_lon_forward(points, groups), heads, waves, forward, inverse, turn, spread,
        w_first.reshape(2, feat, block), w_second.reshape(2, feat, block),
    ]
    hbm = pl.BlockSpec(memory_space=pl.ANY)
    specs = [pl.BlockSpec(memory_space=pltpu.SMEM)] + [hbm] * (len(operands) - 1)
    held_operands = operands[2:]
    sub = points // 3 if points % 48 == 0 else points
    half = jnp.bfloat16
    dma = pltpu.SemaphoreType.DMA
    out = pl.pallas_call(
        functools.partial(enter_kernel, sub, nb, len(held_operands)),
        in_specs=specs,
        out_specs=pl.BlockSpec(memory_space=pltpu.VMEM),
        out_shape=pltpu.VMEM((rows, points, feat), half),
        scratch_shapes=[pltpu.VMEM(o.shape, o.dtype) for o in held_operands]
        + [
            pltpu.VMEM((2, points, feat), half),
            pltpu.VMEM((rows, points, feat), half),
            pltpu.VMEM((rows, groups, width, feat), half),
            pltpu.VMEM((rows, groups, width, feat), half),
            pltpu.VMEM((width, nb * groups, feat), half),
            pltpu.VMEM((held, 2 * KLAT, feat), jnp.float32),
            pltpu.VMEM((held, 2 * KLAT, feat), half),
            pltpu.VMEM((2 * held - PACK // 2, 2 * KLAT, feat), half),
            pltpu.VMEM((points, feat), half),
            pltpu.VMEM((points, 2 * KLON), half),
            pltpu.VMEM((4, feat, feat), half),
            dma((2,)),
            dma((rows,)),
            dma((rows * (points // sub),)),
            dma((rows,)),
            dma((rows,)),
            dma((width // PACK,)),
            dma((2 * (width // PACK) - 1,)),
            dma((3 * (width // PACK),)),
            dma((rows // 2,)),
            pltpu.SemaphoreType.REGULAR,
            dma((len(held_operands),)),
        ],
        compiler_params=pltpu.CompilerParams(
            collective_id=0, has_side_effects=True, vmem_limit_bytes=67043328 - rows * points * feat * 2
        ),
        name="layer",
    )(*operands)
    return out[None]


def streams(members, groups, lat_dev, points, feat):
    width = 2 * KLON // groups
    return (
        members == 2
        and groups == PACK
        and (2 * KLON) % (groups * PACK) == 0
        and points == 2 * KLON
        and feat % 128 == 0
        and lat_dev % 2 == 0
        and width % PACK == 0
        and width > PACK
    )


def layer(mesh_sizes, *args):
    if streams(*mesh_sizes, *args[0].shape[1:]):
        return fused(mesh_sizes, *args)
    return shards(mesh_sizes, *args)


def solution(mesh):
    in_specs = (P("ens", "grid", None, None), P("grid"), P(), P(), P(), P(), P(), P(), P(), P())
    out_specs = P("ens", "grid", None, None)
    sizes = (mesh.shape["ens"], mesh.shape["grid"])
    return jax.shard_map(
        functools.partial(layer, sizes),
        mesh=mesh,
        in_specs=in_specs,
        out_specs=out_specs,
        check_vma=False,
    )
```
